128 devices in a mesh: row: 16 (over z, x), col: 8 (over y, core).
Axes of the slice: x: 4, y: 4, z: 4, core: 2. Of those that a mesh axis runs over, the one named last changes fastest.
Arguments:
- residual: bfloat16 [512, 1024, 256], P(('row', 'col')), may hold values from -6 to 6
- interface_inverse: bfloat16 [512, 1024, 1024], P(('row', 'col'))
- modes: bfloat16 [512, 1024, 32], P(('row', 'col')), may hold values from -0.375 to 0.375
- coarse_map: int32 [16384], P(('row', 'col')), may hold values from 0 to 16383, each once
- coarse_inverse: bfloat16 [16384, 16384], P('row', 'col')
- neighbours: int32 [512, 2], P(('row', 'col')), may hold values from 0 to 511, as said below
- block_sizes: int32 [512, 2], P(('row', 'col')), may hold values from 128 to 256, as said below
- block_offsets: int32 [512, 2], P(('row', 'col')), may hold values from 0 to 384, as said below
Outputs:
- preconditioned: bfloat16 [512, 1024, 256], P(('row', 'col'))
The draws below stay inside these ranges and needn't reach their ends.
Inputs may be any that keep to these rules, and one draw needn't show every extreme that they name: In round k the neighbour of subdomain s is (g XOR a_k) * 4 + (s mod 4) XOR b_k with g = s div 4, where a_k, b_k are the same for all subdomains, a_k is nonzero and a_0 differs from a_1; neighbours are mutual. `block_sizes`: each is 128 or 256, and equal for both sides of a shared block. `block_offsets`: the block of round k lies inside rows [k * 256, (k + 1) * 256) and starts at k * 256 or k * 256 + 256 // 2.
All inputs are finite; a program needn't handle non-finite values.
Results may differ from the reference program's by a relative error of at most 0.0052.
Values may be sent and summed in bfloat16 or wider, within the bound.
No kernel may reach another device: no remote copies, remote signals or barrier semaphores. Data moves between devices by JAX's collectives and lax.ppermute only.
A program may use at most 128 MiB of HBM per device.

```python
import math
import jax
import jax.numpy as jnp
from jax import lax

TRACE = 1024
MODES = 32
SHARE = 256
SUB_DEV = 4
CASES = 256
SUBDOMAINS = 512
COARSE = 16384


def dominant(key, leading, order):
    first_key, second_key = jax.random.split(key, 2)
    shape = leading + (order, order)
    identity = (lax.broadcasted_iota(jnp.int32, (order, order), 0) == lax.broadcasted_iota(jnp.int32, (order, order), 1)).astype(jnp.float32)
    diagonal = jnp.exp(jax.random.uniform(first_key, leading + (order, 1), jnp.float32, math.log(0.5), math.log(2.0)))
    spread = jax.random.normal(second_key, shape, jnp.float32) * (0.6 / math.sqrt(order))
    return (diagonal * identity + spread).astype(jnp.bfloat16)


def draw_interface_inverse(key, part):
    return dominant(jax.random.fold_in(key, 3), (SUBDOMAINS,), TRACE)


def draw_coarse_inverse(key, part):
    return dominant(jax.random.fold_in(key, 5), (), COARSE)


def layout(key):
    base = jax.random.fold_in(key, 11)
    keys = jax.random.split(base, 5)
    groups = SUBDOMAINS // SUB_DEV
    first = jax.random.randint(keys[0], (), 1, groups)
    second = 1 + (first - 1 + jax.random.randint(keys[1], (), 1, groups - 1)) % (groups - 1)
    masks = jnp.stack([first, second]).astype(jnp.int32)
    inner = jax.random.randint(keys[2], (2,), 0, SUB_DEV).astype(jnp.int32)
    index = jnp.arange(SUBDOMAINS).astype(jnp.int32)
    group = index // SUB_DEV
    within = index % SUB_DEV
    partner = jnp.bitwise_xor(group[:, None], masks[None, :]) * SUB_DEV + jnp.bitwise_xor(within[:, None], inner[None, :])
    levels = jax.random.randint(keys[3], (2, SUBDOMAINS), 1, 3).astype(jnp.int32)
    levels = levels.at[0, 0].set(2)
    levels = levels.at[1, partner[SUBDOMAINS - 1, 1]].set(1)
    lower = jnp.minimum(index[:, None], partner)
    sizes = jnp.stack([levels[0][lower[:, 0]], levels[1][lower[:, 1]]], 1) * (SHARE // 2)
    movable = jax.random.randint(keys[4], (SUBDOMAINS, 2), 0, 2).astype(jnp.int32)
    movable = movable.at[SUBDOMAINS - 1, 1].set(1)
    offsets = jnp.arange(2).astype(jnp.int32)[None, :] * SHARE + SHARE // 2 * movable * (sizes == SHARE // 2).astype(jnp.int32)
    return (partner.astype(jnp.int32), sizes.astype(jnp.int32), offsets.astype(jnp.int32))


def draw_neighbours(key, part):
    return layout(key)[0]


def draw_block_sizes(key, part):
    return layout(key)[1]


def draw_block_offsets(key, part):
    return layout(key)[2]


def level_of(own_key, shape, pieces, smallest, high):
    def one(axis_at, parts):
        draws = jax.random.uniform(jax.random.fold_in(jax.random.fold_in(own_key, 6), axis_at), (parts,), jnp.float32, smallest / len(pieces), high / len(pieces))
        return jnp.repeat(jnp.exp(draws), shape[axis_at] // parts).reshape((-1,) + (1,) * (len(shape) - axis_at - 1))

    level = one(*pieces[0])
    for cut in pieces[1:]:
        level = level * one(*cut)
    return level


def centred(key, dims, scale, most, cuts=(), dtype=jnp.bfloat16):
    result = scale * jax.random.normal(key, dims, jnp.float32)
    if cuts:
        result = result * level_of(key, dims, cuts, -0.22, 0.18)
    return jnp.clip(result, -most, most).astype(dtype)


def setup_inputs(seed: int = 0) -> dict:
    arg_keys = jax.random.split(jax.random.key(seed), 9)
    return {
        "residual": centred(arg_keys[0], (SUBDOMAINS, TRACE, CASES), 1.0, 6.0, ((0, 128),)),
        "interface_inverse": draw_interface_inverse(jax.random.fold_in(arg_keys[8], 71), 0),
        "modes": centred(arg_keys[2], (SUBDOMAINS, TRACE, MODES), SHARE ** -0.5, 0.375, ((0, 128),)),
        "coarse_map": jax.random.permutation(arg_keys[3], COARSE).astype(jnp.int32),
        "coarse_inverse": draw_coarse_inverse(jax.random.fold_in(arg_keys[8], 71), 0),
        "neighbours": draw_neighbours(jax.random.fold_in(arg_keys[8], 71), 0),
        "block_sizes": draw_block_sizes(jax.random.fold_in(arg_keys[8], 71), 0),
        "block_offsets": draw_block_offsets(jax.random.fold_in(arg_keys[8], 71), 0),
    }


def neighbour_sum(field, neighbours, block_sizes, block_offsets):
    count = field.shape[0]
    cases = field.shape[2]
    half_share = SHARE // 2
    row_index = jnp.arange(SHARE).astype(jnp.int32)
    summed = field.astype(jnp.float32)
    for which in range(2):
        start = which * SHARE
        region = field[:, start:start + SHARE].astype(jnp.float32)
        relative = block_offsets[:, which] - start
        shifted = jnp.concatenate([region[:, half_share:], jnp.zeros((count, half_share, cases), jnp.float32)], 1)
        aligned = jnp.where((relative == 0)[:, None, None], region, shifted)
        inside = (row_index[None, :] < block_sizes[:, which][:, None])[:, :, None]
        aligned = jnp.where(inside, aligned, jnp.zeros_like(aligned))
        arrived = aligned[neighbours[:, which]]
        moved = jnp.concatenate([jnp.zeros((count, half_share, cases), jnp.float32), arrived[:, :SHARE - half_share]], 1)
        placed = jnp.where((relative == 0)[:, None, None], arrived, moved)
        summed = summed + jnp.pad(placed, ((0, 0), (start, TRACE - start - SHARE), (0, 0)))
    return summed


def weights_of(block_sizes, block_offsets):
    trace_rows = jnp.arange(TRACE).astype(jnp.int32)
    covered = jnp.zeros((block_sizes.shape[0], TRACE), jnp.float32)
    for which in range(2):
        lower = block_offsets[:, which][:, None]
        upper = lower + block_sizes[:, which][:, None]
        covered = covered + jnp.where((trace_rows[None, :] >= lower) & (trace_rows[None, :] < upper), 1.0, 0.0).astype(jnp.float32)
    return 1.0 / (1.0 + covered)


def solve_one(pair):
    return jnp.dot(pair[0], pair[1], preferred_element_type=jnp.float32)


def reference(residual, interface_inverse, modes, coarse_map, coarse_inverse, neighbours, block_sizes, block_offsets):
    omega = weights_of(block_sizes, block_offsets)
    weighted = (omega[:, :, None] * neighbour_sum(residual, neighbours, block_sizes, block_offsets)).astype(jnp.bfloat16)
    local_part = lax.map(solve_one, (interface_inverse, weighted))
    restricted = jnp.einsum("swm,swr->smr", modes.astype(jnp.float32), weighted.astype(jnp.float32)).astype(jnp.bfloat16)
    cases = residual.shape[2]
    coarse_rhs = jnp.zeros((COARSE, cases), jnp.bfloat16).at[coarse_map].set(restricted.reshape(COARSE, cases))
    coarse_solution = jnp.dot(coarse_inverse, coarse_rhs, preferred_element_type=jnp.float32).astype(jnp.bfloat16)
    picked = coarse_solution[coarse_map].reshape(SUBDOMAINS, MODES, cases)
    prolonged = local_part + jnp.einsum("swm,smr->swr", modes.astype(jnp.float32), picked.astype(jnp.float32))
    corrected = (omega[:, :, None] * prolonged).astype(jnp.bfloat16)
    return neighbour_sum(corrected, neighbours, block_sizes, block_offsets).astype(jnp.bfloat16)
```

```python
import jax
import jax.numpy as jnp
from jax import lax
from jax.experimental import pallas as pl
from jax.experimental.pallas import tpu as pltpu
from jax.sharding import PartitionSpec as P

AXES = ("row", "col")
MODES = 32
HALF = 128
LANE = 128
GROUP = 8
VMEM_LIMIT = 40 * 1024 * 1024


def spread(value):
    return lax.all_to_all(value, AXES, 0, 0, tiled=True)


def call(kernel, out_shape, **kw):
    return pl.pallas_call(
        kernel,
        out_shape=out_shape,
        compiler_params=pltpu.CompilerParams(vmem_limit_bytes=VMEM_LIMIT),
        **kw,
    )


def smem():
    return pl.BlockSpec(memory_space=pltpu.SMEM)


def table_of(neighbours, block_sizes, block_offsets):
    count = neighbours.shape[0]
    own = lax.axis_index(AXES).astype(jnp.int32)
    device_mask = jnp.bitwise_xor(neighbours[0] // count, own)
    inner_mask = neighbours[0] % count
    second = (block_offsets // HALF) % 2
    both = block_sizes // HALF - 1
    return jnp.concatenate([device_mask, inner_mask, second.reshape(-1), both.reshape(-1)]).astype(
        jnp.int32
    )


def flags(table, sub, which):
    return table[4 + sub * 2 + which], table[12 + sub * 2 + which]


def pack_blocks(field, table):
    count, _, cases = field.shape
    second = table[4:12].reshape(count, 2)
    region = field[:, : 4 * HALF].reshape(count, 2, 2, HALF, cases)
    first = jnp.where((second == 1)[:, :, None, None], region[:, :, 1], region[:, :, 0])
    aligned = jnp.stack([first, region[:, :, 1]], 1)
    pieces = aligned.reshape(count, 2, 2, HALF // 8, 8, cases).transpose(0, 1, 3, 2, 4, 5)
    return pieces.reshape(-1, 2, 8, cases)


def reroute_kernel(table, chunks, out):
    def step(device, carry):
        for which in range(2):
            out[device, which] = chunks[jnp.bitwise_xor(device, table[which]), which]
        return carry

    lax.fori_loop(0, chunks.shape[0], step, 0, unroll=8)


def exchange(field, table):
    chunks = spread(pack_blocks(field, table))
    chunks = call(
        reroute_kernel,
        jax.ShapeDtypeStruct(chunks.shape, chunks.dtype),
        in_specs=[smem(), pl.BlockSpec(memory_space=pltpu.VMEM)],
        out_specs=pl.BlockSpec(memory_space=pltpu.VMEM),
    )(table, chunks)
    count, cases = field.shape[0], field.shape[2]
    return spread(chunks).reshape(count, 2, HALF // 8, 2, 8, cases)


def arrived_rows(table, sub, which, half, arrived):
    second, both = flags(table, sub, which)
    inside = jnp.maximum(both, (second == half).astype(jnp.int32)).astype(jnp.float32)
    other = jnp.bitwise_xor(sub, table[2 + which])
    rows = arrived[other, half * both, :, which].astype(jnp.float32)
    return rows.reshape(HALF, rows.shape[-1]), inside


def weigh_kernel(table, residual, modes, arrived, weighted, restricted):
    sub = pl.program_id(0)
    for which in range(2):
        for half in range(2):
            start = (which * 2 + half) * HALF
            rows, inside = arrived_rows(table, sub, which, half, arrived)
            own = residual[0, start : start + HALF].astype(jnp.float32)
            value = (own + rows * inside) * (1.0 - 0.5 * inside)
            weighted[0, start : start + HALF] = value.astype(jnp.bfloat16)
    weighted[0, 4 * HALF :] = residual[0, 4 * HALF :]
    restricted[0] = lax.dot_general(
        modes[0], weighted[0], (((0,), (0,)), ((), ())), preferred_element_type=jnp.float32
    ).astype(jnp.bfloat16)


def finish_kernel(table, corrected, arrived, out):
    sub = pl.program_id(0)
    for which in range(2):
        for half in range(2):
            start = (which * 2 + half) * HALF
            rows, inside = arrived_rows(table, sub, which, half, arrived)
            own = corrected[0, start : start + HALF].astype(jnp.float32)
            out[0, start : start + HALF] = (own + rows * inside).astype(jnp.bfloat16)
    out[0, 4 * HALF :] = corrected[0, 4 * HALF :]


def correct_kernel(table, local, modes, picked, corrected):
    sub = pl.program_id(0)
    added = lax.dot_general(
        modes[0], picked[0], (((1,), (0,)), ((), ())), preferred_element_type=jnp.float32
    )
    for which in range(2):
        for half in range(2):
            start = (which * 2 + half) * HALF
            second, both = flags(table, sub, which)
            inside = jnp.maximum(both, (second == half).astype(jnp.int32)).astype(jnp.float32)
            value = local[0, start : start + HALF] + added[start : start + HALF]
            corrected[0, start : start + HALF] = (value * (1.0 - 0.5 * inside)).astype(jnp.bfloat16)
    corrected[0, 4 * HALF :] = (local[0, 4 * HALF :] + added[4 * HALF :]).astype(jnp.bfloat16)


def scatter_kernel(received, out, total, staged):
    devices = received.shape[0]
    place = lax.broadcasted_iota(jnp.int32, (LANE, LANE), 0).astype(jnp.float32)
    total[...] = jnp.zeros_like(total)

    def step(block, carry):
        left, right = [], []
        for inner in range(GROUP):
            piece = received[block * GROUP + inner].astype(jnp.float32)
            high = place == piece[2:3]
            low = place == piece[3:4]
            left.append(
                jnp.concatenate(
                    [jnp.where(high, piece[0:1], 0.0), jnp.where(high, piece[1:2], 0.0)], 0
                ).astype(jnp.bfloat16)
            )
            right.append(jnp.where(low, 1.0, 0.0).astype(jnp.bfloat16))
        total[...] += lax.dot_general(
            jnp.concatenate(left, 1),
            jnp.concatenate(right, 1),
            (((1,), (1,)), ((), ())),
            preferred_element_type=jnp.float32,
        )
        return carry

    lax.fori_loop(0, devices // GROUP, step, 0)
    blocks, _, columns = staged.shape
    pieces = columns // LANE
    for block in range(blocks):
        for case in range(2):
            for piece in range(pieces):
                at = case * LANE + block * pieces + piece
                staged[block, case : case + 1, piece * LANE : (piece + 1) * LANE] = total[at : at + 1]

    def copies(row, carry):
        for block in range(blocks):
            out[row * blocks + block] = staged[block].astype(jnp.bfloat16)
        return carry

    lax.fori_loop(0, devices // blocks, copies, 0)


def gather_kernel(received, partial, out, solved):
    devices, _, rows = partial.shape
    pieces = rows // LANE
    row_blocks = LANE // pieces
    col_blocks = devices // row_blocks
    for block in range(row_blocks):
        value = partial[block * col_blocks].astype(jnp.float32)
        for col in range(1, col_blocks):
            value = value + partial[block * col_blocks + col].astype(jnp.float32)
        for piece in range(pieces):
            for case in range(2):
                at = case * LANE + block * pieces + piece
                solved[at : at + 1] = value[case : case + 1, piece * LANE : (piece + 1) * LANE]
    turned = jnp.concatenate([solved[:LANE].T, solved[LANE:].T], 0).astype(jnp.bfloat16)
    place = lax.broadcasted_iota(jnp.int32, (LANE, LANE), 0).astype(jnp.float32)

    def step(block, carry):
        highs, lows = [], []
        for inner in range(GROUP):
            piece = received[block * GROUP + inner].astype(jnp.float32)
            highs.append(jnp.where(place == piece[2:3], 1.0, 0.0).astype(jnp.bfloat16))
            lows.append(place == piece[3:4])
        chosen = lax.dot_general(
            turned,
            jnp.concatenate(highs, 1),
            (((1,), (0,)), ((), ())),
            preferred_element_type=jnp.float32,
        )
        for inner in range(GROUP):
            lanes = slice(inner * LANE, (inner + 1) * LANE)
            both = [
                jnp.sum(
                    jnp.where(lows[inner], chosen[case * LANE : (case + 1) * LANE, lanes], 0.0),
                    axis=0,
                    keepdims=True,
                )
                for case in range(2)
            ]
            out[block * GROUP + inner] = jnp.concatenate(both, 0).astype(jnp.bfloat16)
        return carry

    lax.fori_loop(0, devices // GROUP, step, 0)


def whole():
    return pl.BlockSpec(memory_space=pltpu.VMEM)


def per_sub(*shape):
    zeros = (0,) * len(shape)
    return pl.BlockSpec((1,) + shape, lambda sub: (sub,) + zeros)


def same(*shape):
    zeros = (0,) * len(shape)
    return pl.BlockSpec(shape, lambda sub: zeros)


def shards(
    residual,
    interface_inverse,
    modes,
    coarse_map,
    coarse_inverse,
    neighbours,
    block_sizes,
    block_offsets,
):
    count, trace_len, cases = residual.shape
    devices = cases // 2
    table = table_of(neighbours, block_sizes, block_offsets)
    field = jax.ShapeDtypeStruct(residual.shape, jnp.bfloat16)

    arrived = exchange(residual, table)
    weighted, restricted = call(
        weigh_kernel,
        (field, jax.ShapeDtypeStruct((count, MODES, cases), jnp.bfloat16)),
        grid=(count,),
        in_specs=[
            smem(),
            per_sub(trace_len, cases),
            per_sub(trace_len, MODES),
            same(*arrived.shape),
        ],
        out_specs=(per_sub(trace_len, cases), per_sub(MODES, cases)),
    )(table, residual, modes, arrived)
    local_part = jnp.einsum(
        "sij,sjr->sir", interface_inverse, weighted, preferred_element_type=jnp.float32
    )

    by_case = restricted.reshape(count * MODES, cases).T.reshape(devices, 2, count * MODES)
    digits = jnp.stack([coarse_map // LANE, coarse_map % LANE]).astype(jnp.bfloat16)
    received = spread(
        jnp.concatenate([by_case, jnp.broadcast_to(digits[None], (devices,) + digits.shape)], 1)
    )
    rows, columns = coarse_inverse.shape
    placed = call(
        scatter_kernel,
        jax.ShapeDtypeStruct((devices, 2, columns), jnp.bfloat16),
        in_specs=[whole()],
        out_specs=whole(),
        scratch_shapes=[
            pltpu.VMEM((2 * LANE, LANE), jnp.float32),
            pltpu.VMEM((LANE * LANE // columns, 2, columns), jnp.float32),
        ],
    )(received)
    coarse_rhs = spread(placed).reshape(cases, columns)
    partial_sum = lax.dot_general(
        coarse_rhs, coarse_inverse, (((1,), (1,)), ((), ())), preferred_element_type=jnp.float32
    ).astype(jnp.bfloat16)
    partial_sum = spread(partial_sum.reshape(devices, 2, rows))
    picked = call(
        gather_kernel,
        jax.ShapeDtypeStruct((devices, 2, LANE), jnp.bfloat16),
        in_specs=[whole(), whole()],
        out_specs=whole(),
        scratch_shapes=[pltpu.VMEM((2 * LANE, LANE), jnp.float32)],
    )(received, partial_sum)
    picked = spread(picked).reshape(cases, count * MODES).T.reshape(count, MODES, cases)

    corrected = call(
        correct_kernel,
        field,
        grid=(count,),
        in_specs=[
            smem(),
            per_sub(trace_len, cases),
            per_sub(trace_len, MODES),
            per_sub(MODES, cases),
        ],
        out_specs=per_sub(trace_len, cases),
    )(table, local_part, modes, picked)
    arrived = exchange(corrected, table)
    return call(
        finish_kernel,
        field,
        grid=(count,),
        in_specs=[smem(), per_sub(trace_len, cases), same(*arrived.shape)],
        out_specs=per_sub(trace_len, cases),
    )(table, corrected, arrived)


def solution(mesh):
    return jax.shard_map(
        shards,
        mesh=mesh,
        in_specs=(
            P(AXES, None, None),
            P(AXES, None, None),
            P(AXES, None, None),
            P(AXES),
            P("row", "col"),
            P(AXES, None),
            P(AXES, None),
            P(AXES, None),
        ),
        out_specs=P(AXES, None, None),
        check_vma=False,
    )
```

```python
import jax
import jax.numpy as jnp
from jax import lax
from jax.experimental import pallas as pl
from jax.experimental.pallas import tpu as pltpu
from jax.sharding import PartitionSpec as P

AXES = ("row", "col")
MODES = 32
HALF = 128
LANE = 128
GROUP = 8
VMEM_LIMIT = 40 * 1024 * 1024


def spread(value):
    return lax.all_to_all(value, AXES, 0, 0, tiled=True)


def call(kernel, out_shape, **kw):
    return pl.pallas_call(
        kernel,
        out_shape=out_shape,
        compiler_params=pltpu.CompilerParams(vmem_limit_bytes=VMEM_LIMIT),
        **kw,
    )


def smem():
    return pl.BlockSpec(memory_space=pltpu.SMEM)


def table_of(neighbours, block_sizes, block_offsets):
    count = neighbours.shape[0]
    own = lax.axis_index(AXES).astype(jnp.int32)
    device_mask = jnp.bitwise_xor(neighbours[0] // count, own)
    inner_mask = neighbours[0] % count
    second = (block_offsets // HALF) % 2
    both = block_sizes // HALF - 1
    return jnp.concatenate([device_mask, inner_mask, second.reshape(-1), both.reshape(-1)]).astype(
        jnp.int32
    )


def flags(table, sub, which):
    return table[4 + sub * 2 + which], table[12 + sub * 2 + which]


def store_blocks(table, sub, load, packed):
    for which in range(2):
        second, _ = flags(table, sub, which)
        for half in range(2):
            start = which * 2 * HALF + (second * HALF if half == 0 else HALF)
            rows = load(pl.multiple_of(start, HALF)).astype(jnp.float32)
            packed[0, half, :, which] = rows.reshape(HALF // 8, 8, rows.shape[-1]).astype(jnp.bfloat16)


def pack_kernel(table, field, packed):
    store_blocks(table, pl.program_id(0), lambda start: field[0, pl.ds(start, HALF)], packed)


def local_kernel(table, inverse, weighted, local, packed):
    local[0] = jnp.dot(inverse[0], weighted[0], preferred_element_type=jnp.float32)
    store_blocks(table, pl.program_id(0), lambda start: local[0, pl.ds(start, HALF)], packed)


def reroute_kernel(table, chunks, out):
    def step(device, carry):
        for which in range(2):
            out[device, which] = chunks[jnp.bitwise_xor(device, table[which]), which]
        return carry

    lax.fori_loop(0, chunks.shape[0], step, 0, unroll=8)


def exchange(packed, table):
    count, cases = packed.shape[0], packed.shape[-1]
    chunks = spread(packed.reshape(-1, 2, 8, cases))
    chunks = call(
        reroute_kernel,
        jax.ShapeDtypeStruct(chunks.shape, chunks.dtype),
        in_specs=[smem(), whole()],
        out_specs=whole(),
    )(table, chunks)
    return spread(chunks).reshape(packed.shape)


def arrived_rows(table, sub, which, half, arrived):
    second, both = flags(table, sub, which)
    inside = jnp.maximum(both, (second == half).astype(jnp.int32)).astype(jnp.float32)
    other = jnp.bitwise_xor(sub, table[2 + which])
    rows = arrived[other, half * both, :, which].astype(jnp.float32)
    return rows.reshape(HALF, rows.shape[-1]), inside


def weigh_kernel(table, residual, modes, arrived, weighted, restricted):
    sub = pl.program_id(0)
    for which in range(2):
        for half in range(2):
            start = (which * 2 + half) * HALF
            rows, inside = arrived_rows(table, sub, which, half, arrived)
            own = residual[0, start : start + HALF].astype(jnp.float32)
            value = (own + rows * inside) * (1.0 - 0.5 * inside)
            weighted[0, start : start + HALF] = value.astype(jnp.bfloat16)
    weighted[0, 4 * HALF :] = residual[0, 4 * HALF :]
    restricted[0] = lax.dot_general(
        modes[0], weighted[0], (((1,), (0,)), ((), ())), preferred_element_type=jnp.float32
    ).astype(jnp.bfloat16)


def prolong(modes, picked):
    return lax.dot_general(
        modes, picked, (((0,), (0,)), ((), ())), preferred_element_type=jnp.float32
    )


def finish_kernel(table, local, modes, picked, arrived, arrived_modes, out):
    sub = pl.program_id(0)
    added = prolong(modes[0], picked[0, sub])
    for which in range(2):
        other = jnp.bitwise_xor(sub, table[2 + which])
        for half in range(2):
            start = (which * 2 + half) * HALF
            rows, inside = arrived_rows(table, sub, which, half, arrived)
            _, both = flags(table, sub, which)
            theirs = prolong(arrived_modes[which, other, half * both], picked[1 + which, other])
            theirs = (0.5 * (rows + theirs)).astype(jnp.bfloat16).astype(jnp.float32)
            own = local[0, start : start + HALF] + added[start : start + HALF]
            own = (own * (1.0 - 0.5 * inside)).astype(jnp.bfloat16).astype(jnp.float32)
            out[0, start : start + HALF] = (own + theirs * inside).astype(jnp.bfloat16)
    out[0, 4 * HALF :] = (local[0, 4 * HALF :] + added[4 * HALF :]).astype(jnp.bfloat16)


def scatter_kernel(table, received, out, total, staged):
    devices = received.shape[0]
    place = lax.broadcasted_iota(jnp.int32, (LANE, LANE), 0).astype(jnp.float32)
    total[...] = jnp.zeros_like(total)

    def step(block, carry):
        left, right = [], []
        for inner in range(GROUP):
            piece = received[block * GROUP + inner].astype(jnp.float32)
            high = place == piece[2:3]
            low = place == piece[3:4]
            left.append(
                jnp.concatenate(
                    [jnp.where(high, piece[0:1], 0.0), jnp.where(high, piece[1:2], 0.0)], 0
                ).astype(jnp.bfloat16)
            )
            right.append(jnp.where(low, 1.0, 0.0).astype(jnp.bfloat16))
        total[...] += lax.dot_general(
            jnp.concatenate(left, 1),
            jnp.concatenate(right, 1),
            (((1,), (1,)), ((), ())),
            preferred_element_type=jnp.float32,
        )
        return carry

    lax.fori_loop(0, devices // GROUP, step, 0)
    blocks, _, columns = staged.shape
    pieces = columns // LANE
    for block in range(blocks):
        for case in range(2):
            for piece in range(pieces):
                at = case * LANE + block * pieces + piece
                staged[block, case : case + 1, piece * LANE : (piece + 1) * LANE] = total[at : at + 1]

    def copies(row, carry):
        for block in range(blocks):
            device = row * blocks + block
            out[device, :, :columns] = staged[block].astype(jnp.bfloat16)
            shared = []
            for which in range(2):
                piece = received[jnp.bitwise_xor(device, table[which])].astype(jnp.float32)
                at = 4 + 2 * which
                shared.append(jnp.concatenate([piece[at : at + 1], piece[at + 1 : at + 2]], 1))
            out[device, :, columns:] = jnp.concatenate(shared, 0).astype(jnp.bfloat16)
        return carry

    lax.fori_loop(0, devices // blocks, copies, 0)


def gather_kernel(table, received, partial, out, solved, chosen_rows):
    devices, _, rows = partial.shape
    pieces = rows // LANE
    row_blocks = LANE // pieces
    col_blocks = devices // row_blocks
    for block in range(row_blocks):
        value = partial[block * col_blocks].astype(jnp.float32)
        for col in range(1, col_blocks):
            value = value + partial[block * col_blocks + col].astype(jnp.float32)
        for piece in range(pieces):
            for case in range(2):
                at = case * LANE + block * pieces + piece
                solved[at : at + 1] = value[case : case + 1, piece * LANE : (piece + 1) * LANE]
    turned = jnp.concatenate([solved[:LANE].T, solved[LANE:].T], 0).astype(jnp.bfloat16)
    place = lax.broadcasted_iota(jnp.int32, (LANE, LANE), 0).astype(jnp.float32)

    def step(block, carry):
        highs, lows = [], []
        for inner in range(GROUP):
            piece = received[block * GROUP + inner].astype(jnp.float32)
            highs.append(jnp.where(place == piece[2:3], 1.0, 0.0).astype(jnp.bfloat16))
            lows.append(place == piece[3:4])
        chosen = lax.dot_general(
            turned,
            jnp.concatenate(highs, 1),
            (((1,), (0,)), ((), ())),
            preferred_element_type=jnp.float32,
        )
        for inner in range(GROUP):
            lanes = slice(inner * LANE, (inner + 1) * LANE)
            both = [
                jnp.sum(
                    jnp.where(lows[inner], chosen[case * LANE : (case + 1) * LANE, lanes], 0.0),
                    axis=0,
                    keepdims=True,
                )
                for case in range(2)
            ]
            chosen_rows[block * GROUP + inner] = jnp.concatenate(both, 0)
        return carry

    lax.fori_loop(0, devices // GROUP, step, 0)

    def share(device, carry):
        rows = [
            chosen_rows[device],
            chosen_rows[jnp.bitwise_xor(device, table[0])],
            chosen_rows[jnp.bitwise_xor(device, table[1])],
        ]
        rows.append(jnp.zeros_like(rows[0]))
        out[device] = jnp.concatenate(rows, 0).astype(jnp.bfloat16)
        return carry

    lax.fori_loop(0, devices, share, 0, unroll=4)


def whole():
    return pl.BlockSpec(memory_space=pltpu.VMEM)


def per_sub(*shape):
    zeros = (0,) * len(shape)
    return pl.BlockSpec((1,) + shape, lambda sub: (sub,) + zeros)


def same(*shape):
    zeros = (0,) * len(shape)
    return pl.BlockSpec(shape, lambda sub: zeros)


def shards(
    residual,
    interface_inverse,
    modes,
    coarse_map,
    coarse_inverse,
    neighbours,
    block_sizes,
    block_offsets,
):
    count, trace_len, cases = residual.shape
    devices = cases // 2
    table = table_of(neighbours, block_sizes, block_offsets)
    field = jax.ShapeDtypeStruct(residual.shape, jnp.bfloat16)

    turned_modes = modes.transpose(0, 2, 1)
    packed_spec = per_sub(2, HALF // 8, 2, 8, cases)
    packed_shape = jax.ShapeDtypeStruct((count, 2, HALF // 8, 2, 8, cases), jnp.bfloat16)

    packed = call(
        pack_kernel,
        packed_shape,
        grid=(count,),
        in_specs=[smem(), per_sub(trace_len, cases)],
        out_specs=packed_spec,
    )(table, residual)
    arrived = exchange(packed, table)
    weighted, restricted = call(
        weigh_kernel,
        (field, jax.ShapeDtypeStruct((count, MODES, cases), jnp.bfloat16)),
        grid=(count,),
        in_specs=[
            smem(),
            per_sub(trace_len, cases),
            per_sub(MODES, trace_len),
            same(*arrived.shape),
        ],
        out_specs=(per_sub(trace_len, cases), per_sub(MODES, cases)),
    )(table, residual, turned_modes, arrived)

    by_case = restricted.reshape(count * MODES, cases).T.reshape(devices, 2, count * MODES)
    digits = jnp.stack([coarse_map // LANE, coarse_map % LANE]).astype(jnp.bfloat16)
    shared = turned_modes[:, :, : 4 * HALF].reshape(count, MODES, 2, 2, HALF)
    second = table[4:12].reshape(count, 1, 2, 1) == 1
    shared = jnp.stack(
        [jnp.where(second, shared[:, :, :, 1], shared[:, :, :, 0]), shared[:, :, :, 1]], 3
    ).reshape(devices, 4, HALF)
    received = spread(
        jnp.concatenate(
            [by_case, jnp.broadcast_to(digits[None], (devices,) + digits.shape), shared], 1
        )
    )
    local_part, packed = call(
        local_kernel,
        (jax.ShapeDtypeStruct(residual.shape, jnp.float32), packed_shape),
        grid=(count,),
        in_specs=[smem(), per_sub(trace_len, trace_len), per_sub(trace_len, cases)],
        out_specs=(per_sub(trace_len, cases), packed_spec),
    )(table, interface_inverse, weighted)
    arrived_local = exchange(packed, table)

    rows, columns = coarse_inverse.shape
    placed = call(
        scatter_kernel,
        jax.ShapeDtypeStruct((devices, 2, columns + 2 * HALF), jnp.bfloat16),
        in_specs=[smem(), whole()],
        out_specs=whole(),
        scratch_shapes=[
            pltpu.VMEM((2 * LANE, LANE), jnp.float32),
            pltpu.VMEM((LANE * LANE // columns, 2, columns), jnp.float32),
        ],
    )(table, received)
    placed = spread(placed)
    coarse_rhs = placed[:, :, :columns].reshape(cases, columns)
    arrived_modes = placed[:, :, columns:].reshape(count, MODES, 2, 2, HALF).transpose(2, 0, 3, 1, 4)
    partial_sum = lax.dot_general(
        coarse_rhs, coarse_inverse, (((1,), (1,)), ((), ())), preferred_element_type=jnp.float32
    ).astype(jnp.bfloat16)
    partial_sum = spread(partial_sum.reshape(devices, 2, rows))
    picked = call(
        gather_kernel,
        jax.ShapeDtypeStruct((devices, 8, LANE), jnp.bfloat16),
        in_specs=[smem(), whole(), whole()],
        out_specs=whole(),
        scratch_shapes=[
            pltpu.VMEM((2 * LANE, LANE), jnp.float32),
            pltpu.VMEM((devices, 2, LANE), jnp.float32),
        ],
    )(table, received, partial_sum)
    picked = spread(picked)[:, :6].reshape(devices, 3, 2, count * MODES).transpose(1, 3, 0, 2)
    picked = picked.reshape(3, count, MODES, cases)
    return call(
        finish_kernel,
        field,
        grid=(count,),
        in_specs=[
            smem(),
            per_sub(trace_len, cases),
            per_sub(MODES, trace_len),
            same(*picked.shape),
            same(*arrived_local.shape),
            same(*arrived_modes.shape),
        ],
        out_specs=per_sub(trace_len, cases),
    )(table, local_part, turned_modes, picked, arrived_local, arrived_modes)


def solution(mesh):
    return jax.shard_map(
        shards,
        mesh=mesh,
        in_specs=(
            P(AXES, None, None),
            P(AXES, None, None),
            P(AXES, None, None),
            P(AXES),
            P("row", "col"),
            P(AXES, None),
            P(AXES, None),
            P(AXES, None),
        ),
        out_specs=P(AXES, None, None),
        check_vma=False,
    )
```

```python
import functools

import jax
import jax.numpy as jnp
from jax import lax
from jax.experimental import pallas as pl
from jax.experimental.pallas import tpu as pltpu
from jax.sharding import PartitionSpec as P

AXES = ("row", "col")
MODES = 32
HALF = 128
LANE = 128
GROUP = 8
VMEM_LIMIT = 40 * 1024 * 1024


def spread(value):
    return lax.all_to_all(value, AXES, 0, 0, tiled=True)


def call(kernel, out_shape, **kw):
    return pl.pallas_call(
        kernel,
        out_shape=out_shape,
        compiler_params=pltpu.CompilerParams(vmem_limit_bytes=VMEM_LIMIT),
        **kw,
    )


def smem():
    return pl.BlockSpec(memory_space=pltpu.SMEM)


def table_of(neighbours, block_sizes, block_offsets):
    count = neighbours.shape[0]
    own = lax.axis_index(AXES).astype(jnp.int32)
    device_mask = jnp.bitwise_xor(neighbours[0] // count, own)
    inner_mask = neighbours[0] % count
    second = (block_offsets // HALF) % 2
    both = block_sizes // HALF - 1
    return jnp.concatenate([device_mask, inner_mask, second.reshape(-1), both.reshape(-1)]).astype(
        jnp.int32
    )


def flags(table, sub, which):
    return table[4 + sub * 2 + which], table[12 + sub * 2 + which]


def store_blocks(offsets, sub, load, packed):
    for which in range(2):
        second = jnp.bitwise_and(jnp.right_shift(offsets[which, sub], 7), 1)
        for half in range(2):
            start = which * 2 * HALF + (second * HALF if half == 0 else HALF)
            rows = load(pl.multiple_of(start, HALF)).astype(jnp.float32)
            packed[0, half, :, which] = rows.reshape(HALF // 8, 8, rows.shape[-1]).astype(jnp.bfloat16)


def pack_kernel(offsets, field, packed):
    store_blocks(offsets, pl.program_id(0), lambda start: field[0, pl.ds(start, HALF)], packed)


def local_kernel(offsets, inverse, weighted, local, packed):
    local[0] = jnp.dot(inverse[0], weighted[0], preferred_element_type=jnp.float32)
    store_blocks(offsets, pl.program_id(0), lambda start: local[0, pl.ds(start, HALF)], packed)


def reroute_kernel(table, chunks, out):
    def step(device, carry):
        for which in range(2):
            out[device, which] = chunks[jnp.bitwise_xor(device, table[which]), which]
        return carry

    lax.fori_loop(0, chunks.shape[0], step, 0, unroll=8)


def exchange(packed, table):
    count, cases = packed.shape[0], packed.shape[-1]
    chunks = spread(packed.reshape(-1, 2, 8, cases))
    chunks = call(
        reroute_kernel,
        jax.ShapeDtypeStruct(chunks.shape, chunks.dtype),
        in_specs=[smem(), whole()],
        out_specs=whole(),
    )(table, chunks)
    return spread(chunks).reshape(packed.shape)


def arrived_rows(table, sub, which, half, arrived):
    second, both = flags(table, sub, which)
    inside = jnp.maximum(both, (second == half).astype(jnp.int32)).astype(jnp.float32)
    other = jnp.bitwise_xor(sub, table[2 + which])
    rows = arrived[other, half * both, :, which].astype(jnp.float32)
    return rows.reshape(HALF, rows.shape[-1]), inside


def weigh_kernel(table, residual, modes, arrived, weighted, restricted):
    sub = pl.program_id(0)
    for which in range(2):
        for half in range(2):
            start = (which * 2 + half) * HALF
            rows, inside = arrived_rows(table, sub, which, half, arrived)
            own = residual[0, start : start + HALF].astype(jnp.float32)
            value = (own + rows * inside) * (1.0 - 0.5 * inside)
            weighted[0, start : start + HALF] = value.astype(jnp.bfloat16)
    weighted[0, 4 * HALF :] = residual[0, 4 * HALF :]
    restricted[0] = lax.dot_general(
        modes[0], weighted[0], (((1,), (0,)), ((), ())), preferred_element_type=jnp.float32
    ).astype(jnp.bfloat16)


def prolong(modes, picked):
    return lax.dot_general(
        modes, picked, (((0,), (0,)), ((), ())), preferred_element_type=jnp.float32
    )


def finish_kernel(table, local, modes, picked, arrived, arrived_modes, out):
    sub = pl.program_id(0)
    added = prolong(modes[0], picked[0, sub])
    for which in range(2):
        other = jnp.bitwise_xor(sub, table[2 + which])
        for half in range(2):
            start = (which * 2 + half) * HALF
            rows, inside = arrived_rows(table, sub, which, half, arrived)
            _, both = flags(table, sub, which)
            theirs = prolong(arrived_modes[which, other, half * both], picked[1 + which, other])
            theirs = (0.5 * (rows + theirs)).astype(jnp.bfloat16).astype(jnp.float32)
            own = local[0, start : start + HALF] + added[start : start + HALF]
            own = (own * (1.0 - 0.5 * inside)).astype(jnp.bfloat16).astype(jnp.float32)
            out[0, start : start + HALF] = (own + theirs * inside).astype(jnp.bfloat16)
    out[0, 4 * HALF :] = (local[0, 4 * HALF :] + added[4 * HALF :]).astype(jnp.bfloat16)


def scatter_kernel(table, received, packed, out, total, staged):
    devices = received.shape[0]
    place = lax.broadcasted_iota(jnp.int32, (LANE, LANE), 0).astype(jnp.float32)
    total[...] = jnp.zeros_like(total)

    def step(block, carry):
        left, right = [], []
        for inner in range(GROUP):
            piece = received[block * GROUP + inner].astype(jnp.float32)
            high = place == piece[2:3]
            low = place == piece[3:4]
            left.append(
                jnp.concatenate(
                    [jnp.where(high, piece[0:1], 0.0), jnp.where(high, piece[1:2], 0.0)], 0
                ).astype(jnp.bfloat16)
            )
            right.append(jnp.where(low, 1.0, 0.0).astype(jnp.bfloat16))
        total[...] += lax.dot_general(
            jnp.concatenate(left, 1),
            jnp.concatenate(right, 1),
            (((1,), (1,)), ((), ())),
            preferred_element_type=jnp.float32,
        )
        return carry

    lax.fori_loop(0, devices // GROUP, step, 0)
    blocks, _, columns = staged.shape
    pieces = columns // LANE
    for block in range(blocks):
        for case in range(2):
            for piece in range(pieces):
                at = case * LANE + block * pieces + piece
                staged[block, case : case + 1, piece * LANE : (piece + 1) * LANE] = total[at : at + 1]

    for block in range(blocks):
        value = staged[block].astype(jnp.bfloat16)

        def copies(row, carry, block=block, value=value):
            out[row * blocks + block, :, :columns] = value
            return carry

        lax.fori_loop(0, devices // blocks, copies, 0, unroll=4)

    local_at = columns + 2 * HALF

    def forward(device, carry):
        shared = []
        for which in range(2):
            piece = received[jnp.bitwise_xor(device, table[which])].astype(jnp.float32)
            at = 4 + 2 * which
            shared.append(jnp.concatenate([piece[at : at + 1], piece[at + 1 : at + 2]], 1))
        out[device, :, columns:local_at] = jnp.concatenate(shared, 0).astype(jnp.bfloat16)
        out[device, :, local_at:] = packed[device]
        return carry

    lax.fori_loop(0, devices, forward, 0, unroll=4)


def join_kernel(table, partial, merged, out):
    rows = partial.shape[-1]
    size = (out.shape[-1] - rows) // 2
    base = merged.shape[-1] - 2 * size

    def step(device, carry):
        out[device, :, :rows] = partial[device]
        for which in range(2):
            out[device, :, rows + which * size : rows + (which + 1) * size] = merged[
                jnp.bitwise_xor(device, table[which]), :, base + which * size : base + (which + 1) * size
            ]
        return carry

    lax.fori_loop(0, partial.shape[0], step, 0, unroll=4)


def gather_kernel(table, received, partial, out, solved, chosen_rows, *, row_blocks):
    devices, _, _ = partial.shape
    pieces = LANE // row_blocks
    rows = pieces * LANE
    col_blocks = devices // row_blocks
    for block in range(row_blocks):
        value = partial[block * col_blocks, :, :rows].astype(jnp.float32)
        for col in range(1, col_blocks):
            value = value + partial[block * col_blocks + col, :, :rows].astype(jnp.float32)
        for piece in range(pieces):
            for case in range(2):
                at = case * LANE + block * pieces + piece
                solved[at : at + 1] = value[case : case + 1, piece * LANE : (piece + 1) * LANE]
    turned = jnp.concatenate([solved[:LANE].T, solved[LANE:].T], 0).astype(jnp.bfloat16)
    place = lax.broadcasted_iota(jnp.int32, (LANE, LANE), 0).astype(jnp.float32)

    def step(block, carry):
        highs, lows = [], []
        for inner in range(GROUP):
            piece = received[block * GROUP + inner].astype(jnp.float32)
            highs.append(jnp.where(place == piece[2:3], 1.0, 0.0).astype(jnp.bfloat16))
            lows.append(place == piece[3:4])
        chosen = lax.dot_general(
            turned,
            jnp.concatenate(highs, 1),
            (((1,), (0,)), ((), ())),
            preferred_element_type=jnp.float32,
        )
        for inner in range(GROUP):
            lanes = slice(inner * LANE, (inner + 1) * LANE)
            both = [
                jnp.sum(
                    jnp.where(lows[inner], chosen[case * LANE : (case + 1) * LANE, lanes], 0.0),
                    axis=0,
                    keepdims=True,
                )
                for case in range(2)
            ]
            chosen_rows[block * GROUP + inner] = jnp.concatenate(both, 0)
        return carry

    lax.fori_loop(0, devices // GROUP, step, 0)

    def share(device, carry):
        rows = [
            chosen_rows[device],
            chosen_rows[jnp.bitwise_xor(device, table[0])],
            chosen_rows[jnp.bitwise_xor(device, table[1])],
        ]
        rows.append(jnp.zeros_like(rows[0]))
        out[device] = jnp.concatenate(rows, 0).astype(jnp.bfloat16)
        return carry

    lax.fori_loop(0, devices, share, 0, unroll=4)


def whole():
    return pl.BlockSpec(memory_space=pltpu.VMEM)


def per_sub(*shape):
    zeros = (0,) * len(shape)
    return pl.BlockSpec((1,) + shape, lambda sub: (sub,) + zeros)


def same(*shape):
    zeros = (0,) * len(shape)
    return pl.BlockSpec(shape, lambda sub: zeros)


def shards(
    residual,
    interface_inverse,
    modes,
    coarse_map,
    coarse_inverse,
    neighbours,
    block_sizes,
    block_offsets,
):
    count, trace_len, cases = residual.shape
    devices = cases // 2
    table = table_of(neighbours, block_sizes, block_offsets)
    field = jax.ShapeDtypeStruct(residual.shape, jnp.bfloat16)

    turned_modes = modes.transpose(0, 2, 1)
    offsets = block_offsets.T
    packed_spec = per_sub(2, HALF // 8, 2, 8, cases)
    packed_shape = jax.ShapeDtypeStruct((count, 2, HALF // 8, 2, 8, cases), jnp.bfloat16)

    packed = call(
        pack_kernel,
        packed_shape,
        grid=(count,),
        in_specs=[smem(), per_sub(trace_len, cases)],
        out_specs=packed_spec,
    )(offsets, residual)
    arrived = exchange(packed, table)
    weighted, restricted = call(
        weigh_kernel,
        (field, jax.ShapeDtypeStruct((count, MODES, cases), jnp.bfloat16)),
        grid=(count,),
        in_specs=[
            smem(),
            per_sub(trace_len, cases),
            per_sub(MODES, trace_len),
            same(*arrived.shape),
        ],
        out_specs=(per_sub(trace_len, cases), per_sub(MODES, cases)),
    )(table, residual, turned_modes, arrived)

    by_case = restricted.reshape(count * MODES, cases).T.reshape(devices, 2, count * MODES)
    digits = jnp.stack([coarse_map // LANE, coarse_map % LANE]).astype(jnp.bfloat16)
    shared = turned_modes[:, :, : 4 * HALF].reshape(count, MODES, 2, 2, HALF)
    second = table[4:12].reshape(count, 1, 2, 1) == 1
    shared = jnp.stack(
        [jnp.where(second, shared[:, :, :, 1], shared[:, :, :, 0]), shared[:, :, :, 1]], 3
    ).reshape(devices, 4, HALF)
    received = spread(
        jnp.concatenate(
            [by_case, jnp.broadcast_to(digits[None], (devices,) + digits.shape), shared], 1
        )
    )
    local_part, packed = call(
        local_kernel,
        (jax.ShapeDtypeStruct(residual.shape, jnp.float32), packed_shape),
        grid=(count,),
        in_specs=[smem(), per_sub(trace_len, trace_len), per_sub(trace_len, cases)],
        out_specs=(per_sub(trace_len, cases), packed_spec),
    )(offsets, interface_inverse, weighted)
    lanes = 2 * 4 * cases
    packed = packed.reshape(devices, 2, 4, 2, cases).transpose(0, 3, 1, 2, 4).reshape(devices, 2, lanes)

    rows, columns = coarse_inverse.shape
    placed = call(
        scatter_kernel,
        jax.ShapeDtypeStruct((devices, 2, columns + 2 * HALF + lanes), jnp.bfloat16),
        in_specs=[smem(), whole(), whole()],
        out_specs=whole(),
        scratch_shapes=[
            pltpu.VMEM((2 * LANE, LANE), jnp.float32),
            pltpu.VMEM((LANE * LANE // columns, 2, columns), jnp.float32),
        ],
    )(table, received, packed)
    placed = spread(placed)
    coarse_rhs = placed[:, :, :columns].reshape(cases, columns)
    arrived_modes = placed[:, :, columns : columns + 2 * HALF].reshape(count, MODES, 2, 2, HALF).transpose(2, 0, 3, 1, 4)
    partial_sum = lax.dot_general(
        coarse_rhs, coarse_inverse, (((1,), (1,)), ((), ())), preferred_element_type=jnp.float32
    ).astype(jnp.bfloat16)
    joined = call(
        join_kernel,
        jax.ShapeDtypeStruct((devices, 2, rows + lanes), jnp.bfloat16),
        in_specs=[smem(), whole(), whole()],
        out_specs=whole(),
    )(table, partial_sum.reshape(devices, 2, rows), placed)
    joined = spread(joined)
    arrived_local = joined[:, :, rows:].reshape(devices, 2, 2, 4, cases).transpose(0, 2, 3, 1, 4)
    arrived_local = arrived_local.reshape(packed_shape.shape)
    picked = call(
        functools.partial(gather_kernel, row_blocks=lax.axis_size("row")),
        jax.ShapeDtypeStruct((devices, 8, LANE), jnp.bfloat16),
        in_specs=[smem(), whole(), whole()],
        out_specs=whole(),
        scratch_shapes=[
            pltpu.VMEM((2 * LANE, LANE), jnp.float32),
            pltpu.VMEM((devices, 2, LANE), jnp.float32),
        ],
    )(table, received, joined)
    picked = spread(picked)[:, :6].reshape(devices, 3, 2, count * MODES).transpose(1, 3, 0, 2)
    picked = picked.reshape(3, count, MODES, cases)
    return call(
        finish_kernel,
        field,
        grid=(count,),
        in_specs=[
            smem(),
            per_sub(trace_len, cases),
            per_sub(MODES, trace_len),
            same(*picked.shape),
            same(*arrived_local.shape),
            same(*arrived_modes.shape),
        ],
        out_specs=per_sub(trace_len, cases),
    )(table, local_part, turned_modes, picked, arrived_local, arrived_modes)


def solution(mesh):
    return jax.shard_map(
        shards,
        mesh=mesh,
        in_specs=(
            P(AXES, None, None),
            P(AXES, None, None),
            P(AXES, None, None),
            P(AXES),
            P("row", "col"),
            P(AXES, None),
            P(AXES, None),
            P(AXES, None),
        ),
        out_specs=P(AXES, None, None),
        check_vma=False,
    )
```

```python
import functools

import jax
import jax.numpy as jnp
from jax import lax
from jax.experimental import pallas as pl
from jax.experimental.pallas import tpu as pltpu
from jax.sharding import PartitionSpec as P

AXES = ("row", "col")
MODES = 32
HALF = 128
LANE = 128
GROUP = 8
VMEM_LIMIT = 12 * 1024 * 1024


def spread(value):
    return lax.all_to_all(value, AXES, 0, 0, tiled=True)


def call(kernel, out_shape, **kw):
    return pl.pallas_call(
        kernel,
        out_shape=out_shape,
        compiler_params=pltpu.CompilerParams(vmem_limit_bytes=VMEM_LIMIT),
        **kw,
    )


def smem():
    return pl.BlockSpec(memory_space=pltpu.SMEM)


def table_of(neighbours, block_sizes, block_offsets):
    count = neighbours.shape[0]
    own = lax.axis_index(AXES).astype(jnp.int32)
    device_mask = jnp.bitwise_xor(neighbours[0] // count, own)
    inner_mask = neighbours[0] % count
    second = (block_offsets // HALF) % 2
    both = block_sizes // HALF - 1
    return jnp.concatenate([device_mask, inner_mask, second.reshape(-1), both.reshape(-1)]).astype(
        jnp.int32
    )


def flags(table, sub, which):
    return table[4 + sub * 2 + which], table[12 + sub * 2 + which]


def store_blocks(offsets, sub, load, packed):
    for which in range(2):
        second = jnp.bitwise_and(jnp.right_shift(offsets[which, sub], 7), 1)
        for half in range(2):
            start = which * 2 * HALF + (second * HALF if half == 0 else HALF)
            rows = load(pl.multiple_of(start, HALF)).astype(jnp.float32)
            packed[0, half, :, which] = rows.reshape(HALF // 8, 8, rows.shape[-1]).astype(jnp.bfloat16)


def pack_kernel(offsets, field, packed):
    store_blocks(offsets, pl.program_id(0), lambda start: field[0, pl.ds(start, HALF)], packed)


def local_kernel(offsets, inverse, weighted, local, packed):
    local[0] = jnp.dot(inverse[0], weighted[0], preferred_element_type=jnp.float32)
    store_blocks(offsets, pl.program_id(0), lambda start: local[0, pl.ds(start, HALF)], packed)


def reroute_kernel(table, chunks, out):
    def step(device, carry):
        for which in range(2):
            out[device, which] = chunks[jnp.bitwise_xor(device, table[which]), which]
        return carry

    lax.fori_loop(0, chunks.shape[0], step, 0, unroll=8)


def exchange(packed, table):
    count, cases = packed.shape[0], packed.shape[-1]
    chunks = spread(packed.reshape(-1, 2, 8, cases))
    chunks = call(
        reroute_kernel,
        jax.ShapeDtypeStruct(chunks.shape, chunks.dtype),
        in_specs=[smem(), whole()],
        out_specs=whole(),
    )(table, chunks)
    return spread(chunks).reshape(packed.shape)


def arrived_rows(table, sub, which, half, arrived):
    second, both = flags(table, sub, which)
    inside = jnp.maximum(both, (second == half).astype(jnp.int32)).astype(jnp.float32)
    other = jnp.bitwise_xor(sub, table[2 + which])
    rows = arrived(other, half * both).astype(jnp.float32)
    return rows.reshape(HALF, rows.shape[-1]), inside


def weigh_kernel(table, residual, modes, arrived, base, weighted, payload, restricted, turned):
    sub = pl.program_id(0)
    for which in range(2):
        for half in range(2):
            start = (which * 2 + half) * HALF
            rows, inside = arrived_rows(
                table, sub, which, half, lambda i, h, which=which: arrived[i, h, :, which]
            )
            own = residual[0, start : start + HALF].astype(jnp.float32)
            value = (own + rows * inside) * (1.0 - 0.5 * inside)
            weighted[0, start : start + HALF] = value.astype(jnp.bfloat16)
    weighted[0, 4 * HALF :] = residual[0, 4 * HALF :]
    restricted[pl.ds(pl.multiple_of(sub * MODES, MODES), MODES)] = lax.dot_general(
        modes[0], weighted[0], (((1,), (0,)), ((), ())), preferred_element_type=jnp.float32
    )

    @pl.when(sub == pl.num_programs(0) - 1)
    def _():
        devices, rows, _ = payload.shape
        turned[: 2 * devices] = restricted[...].T
        turned[2 * devices :] = jnp.zeros((turned.shape[0] - 2 * devices, LANE), jnp.float32)
        own = lax.broadcasted_iota(jnp.int32, (rows, LANE), 0) < 2

        def step(device, carry):
            piece = turned[pl.ds(2 * device, rows)]
            rest = base[device].astype(jnp.float32)
            payload[device] = jnp.where(own, piece, rest).astype(jnp.bfloat16)
            return carry

        lax.fori_loop(0, devices, step, 0, unroll=8)


def prolong(modes, picked):
    return lax.dot_general(
        modes, picked, (((0,), (0,)), ((), ())), preferred_element_type=jnp.float32
    )


def finish_kernel(table, local, modes, picked, first, second, arrived_modes, out):
    sub = pl.program_id(0)
    added = prolong(modes[0], picked[0, sub])
    for which in range(2):
        other = jnp.bitwise_xor(sub, table[2 + which])
        for half in range(2):
            start = (which * 2 + half) * HALF
            rows, inside = arrived_rows(
                table, sub, which, half, lambda *at, which=which: (first, second)[which][at]
            )
            _, both = flags(table, sub, which)
            theirs = prolong(arrived_modes[which, other, half * both], picked[1 + which, other])
            theirs = (0.5 * (rows + theirs)).astype(jnp.bfloat16).astype(jnp.float32)
            own = local[0, start : start + HALF] + added[start : start + HALF]
            own = (own * (1.0 - 0.5 * inside)).astype(jnp.bfloat16).astype(jnp.float32)
            out[0, start : start + HALF] = (own + theirs * inside).astype(jnp.bfloat16)
    out[0, 4 * HALF :] = (local[0, 4 * HALF :] + added[4 * HALF :]).astype(jnp.bfloat16)


def scatter_kernel(table, received, packed, out, total, staged):
    devices = received.shape[0]
    place = lax.broadcasted_iota(jnp.int32, (LANE, LANE), 0).astype(jnp.float32)
    total[...] = jnp.zeros_like(total)

    def step(block, carry):
        left, right = [], []
        for inner in range(GROUP):
            piece = received[block * GROUP + inner].astype(jnp.float32)
            high = place == piece[2:3]
            low = place == piece[3:4]
            left.append(
                jnp.concatenate(
                    [jnp.where(high, piece[0:1], 0.0), jnp.where(high, piece[1:2], 0.0)], 0
                ).astype(jnp.bfloat16)
            )
            right.append(jnp.where(low, 1.0, 0.0).astype(jnp.bfloat16))
        total[...] += lax.dot_general(
            jnp.concatenate(left, 1),
            jnp.concatenate(right, 1),
            (((1,), (1,)), ((), ())),
            preferred_element_type=jnp.float32,
        )
        return carry

    lax.fori_loop(0, devices // GROUP, step, 0)
    blocks, _, columns = staged.shape
    pieces = columns // LANE
    for block in range(blocks):
        for case in range(2):
            for piece in range(pieces):
                at = case * LANE + block * pieces + piece
                staged[block, case : case + 1, piece * LANE : (piece + 1) * LANE] = total[at : at + 1]

    for block in range(blocks):
        value = staged[block].astype(jnp.bfloat16)

        def copies(row, carry, block=block, value=value):
            out[row * blocks + block, :, :columns] = value
            return carry

        lax.fori_loop(0, devices // blocks, copies, 0, unroll=4)

    local_at = columns + 2 * HALF

    def forward(device, carry):
        shared = []
        for which in range(2):
            piece = received[jnp.bitwise_xor(device, table[which])].astype(jnp.float32)
            at = 4 + 2 * which
            shared.append(jnp.concatenate([piece[at : at + 1], piece[at + 1 : at + 2]], 1))
        out[device, :, columns:local_at] = jnp.concatenate(shared, 0).astype(jnp.bfloat16)
        out[device, :, local_at:] = packed[device, :, : out.shape[-1] - local_at]
        return carry

    lax.fori_loop(0, devices, forward, 0, unroll=4)


def join_kernel(table, partial, merged, packed, out):
    rows, size = partial.shape[-1], packed.shape[-1] // 2
    base = merged.shape[-1] - size

    def step(device, carry):
        out[device, :, :rows] = partial[device]
        out[device, :, rows : rows + size] = merged[jnp.bitwise_xor(device, table[0]), :, base:]
        out[device, :, rows + size :] = packed[device, :, size:]
        return carry

    lax.fori_loop(0, partial.shape[0], step, 0, unroll=4)


def gather_kernel(table, received, partial, out, solved, chosen_rows, *, row_blocks):
    devices, _, _ = partial.shape
    pieces = LANE // row_blocks
    rows = pieces * LANE
    col_blocks = devices // row_blocks
    for block in range(row_blocks):
        value = partial[block * col_blocks, :, :rows].astype(jnp.float32)
        for col in range(1, col_blocks):
            value = value + partial[block * col_blocks + col, :, :rows].astype(jnp.float32)
        for piece in range(pieces):
            for case in range(2):
                at = case * LANE + block * pieces + piece
                solved[at : at + 1] = value[case : case + 1, piece * LANE : (piece + 1) * LANE]
    turned = jnp.concatenate([solved[:LANE].T, solved[LANE:].T], 0).astype(jnp.bfloat16)
    place = lax.broadcasted_iota(jnp.int32, (LANE, LANE), 0).astype(jnp.float32)

    def step(block, carry):
        highs, lows = [], []
        for inner in range(GROUP):
            piece = received[block * GROUP + inner].astype(jnp.float32)
            highs.append(jnp.where(place == piece[2:3], 1.0, 0.0).astype(jnp.bfloat16))
            lows.append(place == piece[3:4])
        chosen = lax.dot_general(
            turned,
            jnp.concatenate(highs, 1),
            (((1,), (0,)), ((), ())),
            preferred_element_type=jnp.float32,
        )
        for inner in range(GROUP):
            lanes = slice(inner * LANE, (inner + 1) * LANE)
            both = [
                jnp.sum(
                    jnp.where(lows[inner], chosen[case * LANE : (case + 1) * LANE, lanes], 0.0),
                    axis=0,
                    keepdims=True,
                )
                for case in range(2)
            ]
            chosen_rows[block * GROUP + inner] = jnp.concatenate(both, 0)
        return carry

    lax.fori_loop(0, devices // GROUP, step, 0)

    size = out.shape[-1] - 3 * LANE

    def share(device, carry):
        first, second = (jnp.bitwise_xor(device, table[which]) for which in range(2))
        for at, source in enumerate((device, first, second)):
            out[device, :, at * LANE : (at + 1) * LANE] = chosen_rows[source].astype(jnp.bfloat16)
        out[device, :, 3 * LANE :] = partial[second, :, partial.shape[-1] - size :]
        return carry

    lax.fori_loop(0, devices, share, 0, unroll=4)


def whole():
    return pl.BlockSpec(memory_space=pltpu.VMEM)


def per_sub(*shape):
    zeros = (0,) * len(shape)
    return pl.BlockSpec((1,) + shape, lambda sub: (sub,) + zeros)


def same(*shape):
    zeros = (0,) * len(shape)
    return pl.BlockSpec(shape, lambda sub: zeros)


def shards(
    residual,
    interface_inverse,
    modes,
    coarse_map,
    coarse_inverse,
    neighbours,
    block_sizes,
    block_offsets,
):
    count, trace_len, cases = residual.shape
    devices = cases // 2
    table = table_of(neighbours, block_sizes, block_offsets)
    field = jax.ShapeDtypeStruct(residual.shape, jnp.bfloat16)

    turned_modes = modes.transpose(0, 2, 1)
    offsets = block_offsets.T
    packed_spec = per_sub(2, HALF // 8, 2, 8, cases)
    packed_shape = jax.ShapeDtypeStruct((count, 2, HALF // 8, 2, 8, cases), jnp.bfloat16)

    packed = call(
        pack_kernel,
        packed_shape,
        grid=(count,),
        in_specs=[smem(), per_sub(trace_len, cases)],
        out_specs=packed_spec,
    )(offsets, residual)
    arrived = exchange(packed, table)
    digits = jnp.stack([coarse_map // LANE, coarse_map % LANE]).astype(jnp.bfloat16)
    digits = jnp.concatenate([jnp.zeros_like(digits), digits], 0)
    shared = turned_modes[:, :, : 4 * HALF].reshape(count, MODES, 2, 2, HALF)
    second = table[4:12].reshape(count, 1, 2, 1) == 1
    shared = jnp.stack(
        [jnp.where(second, shared[:, :, :, 1], shared[:, :, :, 0]), shared[:, :, :, 1]], 3
    ).reshape(devices, 4, HALF)
    base = jnp.concatenate([jnp.broadcast_to(digits[None], (devices,) + digits.shape), shared], 1)
    weighted, payload = call(
        weigh_kernel,
        (field, jax.ShapeDtypeStruct(base.shape, jnp.bfloat16)),
        grid=(count,),
        in_specs=[
            smem(),
            per_sub(trace_len, cases),
            per_sub(MODES, trace_len),
            same(*arrived.shape),
            same(*base.shape),
        ],
        out_specs=(per_sub(trace_len, cases), same(*base.shape)),
        scratch_shapes=[
            pltpu.VMEM((count * MODES, cases), jnp.float32),
            pltpu.VMEM((cases + 8, LANE), jnp.float32),
        ],
    )(table, residual, turned_modes, arrived, base)
    received = spread(payload)

    local_part, packed = call(
        local_kernel,
        (jax.ShapeDtypeStruct(residual.shape, jnp.float32), packed_shape),
        grid=(count,),
        in_specs=[smem(), per_sub(trace_len, trace_len), per_sub(trace_len, cases)],
        out_specs=(per_sub(trace_len, cases), packed_spec),
    )(offsets, interface_inverse, weighted)
    lanes = 2 * 4 * cases
    packed = packed.reshape(devices, 2, 4, 2, cases).transpose(0, 3, 1, 2, 4).reshape(devices, 2, lanes)

    rows, columns = coarse_inverse.shape
    placed = call(
        scatter_kernel,
        jax.ShapeDtypeStruct((devices, 2, columns + 2 * HALF + lanes // 2), jnp.bfloat16),
        in_specs=[smem(), whole(), whole()],
        out_specs=whole(),
        scratch_shapes=[
            pltpu.VMEM((2 * LANE, LANE), jnp.float32),
            pltpu.VMEM((LANE * LANE // columns, 2, columns), jnp.float32),
        ],
    )(table, received, packed)
    placed = spread(placed)
    coarse_rhs = placed[:, :, :columns].reshape(cases, columns)
    arrived_modes = placed[:, :, columns : columns + 2 * HALF].reshape(count, MODES, 2, 2, HALF).transpose(2, 0, 3, 1, 4)
    partial_sum = lax.dot_general(
        coarse_rhs, coarse_inverse, (((1,), (1,)), ((), ())), preferred_element_type=jnp.float32
    ).astype(jnp.bfloat16)
    joined = call(
        join_kernel,
        jax.ShapeDtypeStruct((devices, 2, rows + lanes), jnp.bfloat16),
        in_specs=[smem(), whole(), whole(), whole()],
        out_specs=whole(),
    )(table, partial_sum.reshape(devices, 2, rows), placed, packed)
    joined = spread(joined)

    def unpack(value):
        value = value.reshape(devices, 2, 4, cases).transpose(0, 2, 1, 3)
        return value.reshape(count, 2, HALF // 8, 8, cases)

    picked = call(
        functools.partial(gather_kernel, row_blocks=lax.axis_size("row")),
        jax.ShapeDtypeStruct((devices, 2, 3 * LANE + lanes // 2), jnp.bfloat16),
        in_specs=[smem(), whole(), whole()],
        out_specs=whole(),
        scratch_shapes=[
            pltpu.VMEM((2 * LANE, LANE), jnp.float32),
            pltpu.VMEM((devices, 2, LANE), jnp.float32),
        ],
    )(table, received, joined)
    picked = spread(picked)
    arrived_first = unpack(joined[:, :, rows : rows + lanes // 2])
    arrived_second = unpack(picked[:, :, 3 * LANE :])
    picked = picked[:, :, : 3 * LANE].reshape(devices, 2, 3, count * MODES).transpose(2, 3, 0, 1)
    picked = picked.reshape(3, count, MODES, cases)
    return call(
        finish_kernel,
        field,
        grid=(count,),
        in_specs=[
            smem(),
            per_sub(trace_len, cases),
            per_sub(MODES, trace_len),
            same(*picked.shape),
            same(*arrived_first.shape),
            same(*arrived_second.shape),
            same(*arrived_modes.shape),
        ],
        out_specs=per_sub(trace_len, cases),
    )(table, local_part, turned_modes, picked, arrived_first, arrived_second, arrived_modes)


def solution(mesh):
    return jax.shard_map(
        shards,
        mesh=mesh,
        in_specs=(
            P(AXES, None, None),
            P(AXES, None, None),
            P(AXES, None, None),
            P(AXES),
            P("row", "col"),
            P(AXES, None),
            P(AXES, None),
            P(AXES, None),
        ),
        out_specs=P(AXES, None, None),
        check_vma=False,
    )
```

```python
import functools

import jax
import jax.numpy as jnp
from jax import lax
from jax.experimental import pallas as pl
from jax.experimental.pallas import tpu as pltpu
from jax.sharding import PartitionSpec as P

AXES = ("row", "col")
MODES = 32
HALF = 128
LANE = 128
GROUP = 8
VMEM_LIMIT = 16 * 1024 * 1024


def spread(value):
    return lax.all_to_all(value, AXES, 0, 0, tiled=True)


def call(kernel, out_shape, **kw):
    return pl.pallas_call(
        kernel,
        out_shape=out_shape,
        compiler_params=pltpu.CompilerParams(vmem_limit_bytes=VMEM_LIMIT),
        **kw,
    )


def smem():
    return pl.BlockSpec(memory_space=pltpu.SMEM)


def table_of(neighbours, block_sizes, block_offsets):
    count = neighbours.shape[0]
    own = lax.axis_index(AXES).astype(jnp.int32)
    device_mask = jnp.bitwise_xor(neighbours[0] // count, own)
    inner_mask = neighbours[0] % count
    second = (block_offsets // HALF) % 2
    both = block_sizes // HALF - 1
    return jnp.concatenate([device_mask, inner_mask, second.reshape(-1), both.reshape(-1)]).astype(
        jnp.int32
    )


def flags(table, sub, which):
    return table[4 + sub * 2 + which], table[12 + sub * 2 + which]


def store_blocks(offsets, sub, load, packed):
    for which in range(2):
        second = jnp.bitwise_and(jnp.right_shift(offsets[which, sub], 7), 1)
        for half in range(2):
            start = which * 2 * HALF + (second * HALF if half == 0 else HALF)
            rows = load(pl.multiple_of(start, HALF)).astype(jnp.float32)
            for lane in range(2):
                tile = rows[:, lane * LANE : (lane + 1) * LANE].reshape(HALF // 8, 8, LANE)
                packed[0, half, :, which * 2 + lane] = tile.astype(jnp.bfloat16)


def pack_kernel(offsets, field, packed):
    store_blocks(offsets, pl.program_id(0), lambda start: field[0, pl.ds(start, HALF)], packed)


def local_kernel(offsets, inverse, weighted, local, packed):
    local[0] = jnp.dot(inverse[0], weighted[0], preferred_element_type=jnp.float32)
    store_blocks(offsets, pl.program_id(0), lambda start: local[0, pl.ds(start, HALF)], packed)


def reroute_kernel(table, chunks, out):
    size = chunks.shape[1] // 2

    def step(device, carry):
        for which in range(2):
            rows = slice(which * size, (which + 1) * size)
            out[device, rows] = chunks[jnp.bitwise_xor(device, table[which]), rows]
        return carry

    lax.fori_loop(0, chunks.shape[0], step, 0, unroll=8)


def exchange(packed, table):
    chunks = spread(packed.reshape(-1, 32, LANE))
    chunks = call(
        reroute_kernel,
        jax.ShapeDtypeStruct(chunks.shape, chunks.dtype),
        in_specs=[smem(), whole()],
        out_specs=whole(),
    )(table, chunks)
    return spread(chunks).reshape(packed.shape)


def arrived_rows(table, sub, which, half, arrived):
    second, both = flags(table, sub, which)
    inside = jnp.maximum(both, (second == half).astype(jnp.int32)).astype(jnp.float32)
    other = jnp.bitwise_xor(sub, table[2 + which])
    tiles = [
        arrived[other, half * both, :, which * 2 + lane].astype(jnp.float32).reshape(HALF, LANE)
        for lane in range(2)
    ]
    return jnp.concatenate(tiles, 1), inside


def weigh_kernel(table, residual, modes, arrived, base, weighted, payload, restricted, turned):
    sub = pl.program_id(0)
    for which in range(2):
        for half in range(2):
            start = (which * 2 + half) * HALF
            rows, inside = arrived_rows(table, sub, which, half, arrived)
            own = residual[0, start : start + HALF].astype(jnp.float32)
            value = (own + rows * inside) * (1.0 - 0.5 * inside)
            weighted[0, start : start + HALF] = value.astype(jnp.bfloat16)
    weighted[0, 4 * HALF :] = residual[0, 4 * HALF :]
    restricted[pl.ds(pl.multiple_of(sub * MODES, MODES), MODES)] = lax.dot_general(
        modes[0], weighted[0], (((1,), (0,)), ((), ())), preferred_element_type=jnp.float32
    )

    @pl.when(sub == pl.num_programs(0) - 1)
    def _():
        devices, rows, _ = payload.shape
        turned[: 2 * devices] = restricted[...].T
        turned[2 * devices :] = jnp.zeros((turned.shape[0] - 2 * devices, LANE), jnp.float32)
        own = lax.broadcasted_iota(jnp.int32, (rows, LANE), 0) < 2

        def step(device, carry):
            piece = turned[pl.ds(2 * device, rows)]
            rest = base[device].astype(jnp.float32)
            payload[device] = jnp.where(own, piece, rest).astype(jnp.bfloat16)
            return carry

        lax.fori_loop(0, devices, step, 0, unroll=8)


def prolong(modes, picked):
    return lax.dot_general(
        modes, picked, (((0,), (0,)), ((), ())), preferred_element_type=jnp.float32
    )


def finish_kernel(table, local, modes, arrived, arrived_modes, out, pairs, picked):
    sub = pl.program_id(0)

    @pl.when(sub == 0)
    def _():
        for first in range(4):
            for half in range(2):

                def step(piece, carry, first=first, half=half):
                    for inner in range(4):
                        tile = arrived[first, half, piece * 4 + inner, 4].astype(jnp.float32)
                        at = (first * 2 + half) * 32 + pl.multiple_of(piece * 8, 8) + inner * 2
                        for kind in range(3):
                            pairs[kind, pl.ds(at, 2)] = tile[kind * 2 : kind * 2 + 2]
                    return carry

                lax.fori_loop(0, 4, step, 0)
        for kind in range(3):
            picked[kind] = pairs[kind].T.reshape(picked.shape[1:]).astype(jnp.bfloat16)

    added = prolong(modes[0], picked[0, sub])
    for which in range(2):
        other = jnp.bitwise_xor(sub, table[2 + which])
        for half in range(2):
            start = (which * 2 + half) * HALF
            rows, inside = arrived_rows(table, sub, which, half, arrived)
            _, both = flags(table, sub, which)
            theirs = prolong(arrived_modes[which, other, half * both], picked[1 + which, other])
            theirs = (0.5 * (rows + theirs)).astype(jnp.bfloat16).astype(jnp.float32)
            own = local[0, start : start + HALF] + added[start : start + HALF]
            own = (own * (1.0 - 0.5 * inside)).astype(jnp.bfloat16).astype(jnp.float32)
            out[0, start : start + HALF] = (own + theirs * inside).astype(jnp.bfloat16)
    out[0, 4 * HALF :] = (local[0, 4 * HALF :] + added[4 * HALF :]).astype(jnp.bfloat16)


def scatter_kernel(table, received, out, total, staged):
    devices = received.shape[0]
    place = lax.broadcasted_iota(jnp.int32, (LANE, LANE), 0).astype(jnp.float32)
    total[...] = jnp.zeros_like(total)

    def step(block, carry):
        left, right = [], []
        for inner in range(GROUP):
            piece = received[block * GROUP + inner].astype(jnp.float32)
            high = place == piece[2:3]
            low = place == piece[3:4]
            left.append(
                jnp.concatenate(
                    [jnp.where(high, piece[0:1], 0.0), jnp.where(high, piece[1:2], 0.0)], 0
                ).astype(jnp.bfloat16)
            )
            right.append(jnp.where(low, 1.0, 0.0).astype(jnp.bfloat16))
        total[...] += lax.dot_general(
            jnp.concatenate(left, 1),
            jnp.concatenate(right, 1),
            (((1,), (1,)), ((), ())),
            preferred_element_type=jnp.float32,
        )
        return carry

    lax.fori_loop(0, devices // GROUP, step, 0)
    blocks, size, _ = staged.shape
    pieces = size // 2
    for block in range(blocks):
        for case in range(2):
            for piece in range(pieces):
                at = case * LANE + block * pieces + piece
                staged[block, piece * 2 + case : piece * 2 + case + 1] = total[at : at + 1]
    for block in range(blocks):
        value = staged[block].astype(jnp.bfloat16)

        def copies(row, carry, block=block, value=value):
            out[row * blocks + block, :size] = value
            return carry

        lax.fori_loop(0, devices // blocks, copies, 0, unroll=4)
    first = lax.broadcasted_iota(jnp.int32, (8, LANE), 0) < 6

    def forward(device, carry):
        pieces = [
            received[jnp.bitwise_xor(device, table[which])].astype(jnp.float32) for which in range(2)
        ]
        out[device, size:] = jnp.where(first, pieces[0], pieces[1]).astype(jnp.bfloat16)
        return carry

    lax.fori_loop(0, devices, forward, 0, unroll=4)


def product_kernel(placed, inverse, packed, out, pairs, left, parts):
    at_step = pl.program_id(0)
    groups = placed.shape[0] // 4
    tiles, steps = pairs.shape[0], parts.shape[0]

    @pl.when(at_step == 0)
    def _():
        def step(group, carry):
            for inner in range(4):
                rows = placed[group * 4 + inner, : 2 * tiles].astype(jnp.float32)
                at = pl.multiple_of(group * 8, 8) + 2 * inner
                for tile in range(tiles):
                    pairs[tile, pl.ds(at, 2)] = rows[2 * tile : 2 * tile + 2]
            return carry

        lax.fori_loop(0, groups, step, 0)
        for tile in range(tiles):
            left[:, tile * LANE : (tile + 1) * LANE] = pairs[tile].astype(jnp.bfloat16)

    parts[at_step] = lax.dot_general(
        left[...], inverse[...], (((1,), (1,)), ((), ())), preferred_element_type=jnp.float32
    )

    @pl.when(at_step == steps - 1)
    def _():
        size = steps * parts.shape[2] // LANE * 2

        def step(group, carry):
            at = pl.multiple_of(group * 8, 8)
            tall = [
                parts[part, pl.ds(at, 8), lane * LANE : (lane + 1) * LANE]
                for part in range(steps)
                for lane in range(parts.shape[2] // LANE)
            ]
            for inner in range(4):
                rows = jnp.concatenate([tile[2 * inner : 2 * inner + 2] for tile in tall], 0)
                out[group * 4 + inner, :size] = rows.astype(jnp.bfloat16)
                out[group * 4 + inner, size:] = packed[group * 4 + inner]
            return carry

        lax.fori_loop(0, groups, step, 0)


def gather_kernel(table, received, partial, out, solved, chosen_rows, *, row_blocks):
    devices = received.shape[0]
    pieces = LANE // row_blocks
    col_blocks = devices // row_blocks
    for block in range(row_blocks):
        value = partial[block * col_blocks, : 2 * pieces].astype(jnp.float32)
        for col in range(1, col_blocks):
            value = value + partial[block * col_blocks + col, : 2 * pieces].astype(jnp.float32)
        for piece in range(pieces):
            for case in range(2):
                at = case * LANE + block * pieces + piece
                solved[at : at + 1] = value[2 * piece + case : 2 * piece + case + 1]
    turned = jnp.concatenate([solved[:LANE].T, solved[LANE:].T], 0).astype(jnp.bfloat16)
    place = lax.broadcasted_iota(jnp.int32, (LANE, LANE), 0).astype(jnp.float32)

    def step(block, carry):
        highs, lows = [], []
        for inner in range(GROUP):
            piece = received[block * GROUP + inner].astype(jnp.float32)
            highs.append(jnp.where(place == piece[2:3], 1.0, 0.0).astype(jnp.bfloat16))
            lows.append(place == piece[3:4])
        chosen = lax.dot_general(
            turned,
            jnp.concatenate(highs, 1),
            (((1,), (0,)), ((), ())),
            preferred_element_type=jnp.float32,
        )
        for inner in range(GROUP):
            lanes = slice(inner * LANE, (inner + 1) * LANE)
            both = [
                jnp.sum(
                    jnp.where(lows[inner], chosen[case * LANE : (case + 1) * LANE, lanes], 0.0),
                    axis=0,
                    keepdims=True,
                )
                for case in range(2)
            ]
            chosen_rows[block * GROUP + inner] = jnp.concatenate(both, 0)
        return carry

    lax.fori_loop(0, devices // GROUP, step, 0)

    size = (partial.shape[1] - 2 * pieces) // 2

    def share(device, carry):
        sources = [jnp.bitwise_xor(device, table[which]) for which in range(2)]
        for which in range(2):
            at = 2 * pieces + which * size
            out[device, which * size : (which + 1) * size] = partial[sources[which], at : at + size]
        rows = [chosen_rows[device], chosen_rows[sources[0]], chosen_rows[sources[1]]]
        rows.append(jnp.zeros_like(rows[0]))
        out[device, 2 * size :] = jnp.concatenate(rows, 0).astype(jnp.bfloat16)
        return carry

    lax.fori_loop(0, devices, share, 0, unroll=4)


def whole():
    return pl.BlockSpec(memory_space=pltpu.VMEM)


def per_sub(*shape):
    zeros = (0,) * len(shape)
    return pl.BlockSpec((1,) + shape, lambda sub: (sub,) + zeros)


def same(*shape):
    zeros = (0,) * len(shape)
    return pl.BlockSpec(shape, lambda sub: zeros)


def shards(
    residual,
    interface_inverse,
    modes,
    coarse_map,
    coarse_inverse,
    neighbours,
    block_sizes,
    block_offsets,
):
    count, trace_len, cases = residual.shape
    devices = cases // 2
    table = table_of(neighbours, block_sizes, block_offsets)
    field = jax.ShapeDtypeStruct(residual.shape, jnp.bfloat16)

    turned_modes = modes.transpose(0, 2, 1)
    offsets = block_offsets.T
    packed_spec = per_sub(2, HALF // 8, 4, 8, LANE)
    packed_shape = jax.ShapeDtypeStruct((count, 2, HALF // 8, 4, 8, LANE), jnp.bfloat16)

    packed = call(
        pack_kernel,
        packed_shape,
        grid=(count,),
        in_specs=[smem(), per_sub(trace_len, cases)],
        out_specs=packed_spec,
    )(offsets, residual)
    arrived = exchange(packed, table)
    digits = jnp.stack([coarse_map // LANE, coarse_map % LANE]).astype(jnp.bfloat16)
    digits = jnp.concatenate([jnp.zeros_like(digits), digits], 0)
    shared = turned_modes[:, :, : 4 * HALF].reshape(count, MODES, 2, 2, HALF)
    second = table[4:12].reshape(count, 1, 2, 1) == 1
    shared = jnp.stack(
        [jnp.where(second, shared[:, :, :, 1], shared[:, :, :, 0]), shared[:, :, :, 1]], 3
    ).reshape(devices, 4, HALF)
    base = jnp.concatenate([jnp.broadcast_to(digits[None], (devices,) + digits.shape), shared], 1)
    weighted, payload = call(
        weigh_kernel,
        (field, jax.ShapeDtypeStruct(base.shape, jnp.bfloat16)),
        grid=(count,),
        in_specs=[
            smem(),
            per_sub(trace_len, cases),
            per_sub(MODES, trace_len),
            same(*arrived.shape),
            same(*base.shape),
        ],
        out_specs=(per_sub(trace_len, cases), same(*base.shape)),
        scratch_shapes=[
            pltpu.VMEM((count * MODES, cases), jnp.float32),
            pltpu.VMEM((cases + 8, LANE), jnp.float32),
        ],
    )(table, residual, turned_modes, arrived, base)
    received = spread(payload)
    weighted, received = lax.optimization_barrier((weighted, received))

    local_part, packed = call(
        local_kernel,
        (jax.ShapeDtypeStruct(residual.shape, jnp.float32), packed_shape),
        grid=(count,),
        in_specs=[smem(), per_sub(trace_len, trace_len), per_sub(trace_len, cases)],
        out_specs=(per_sub(trace_len, cases), packed_spec),
    )(offsets, interface_inverse, weighted)
    packed = packed.reshape(devices, 32, LANE)

    rows, columns = coarse_inverse.shape
    placed = call(
        scatter_kernel,
        jax.ShapeDtypeStruct((devices, 2 * columns // LANE + 8, LANE), jnp.bfloat16),
        in_specs=[smem(), whole()],
        out_specs=whole(),
        scratch_shapes=[
            pltpu.VMEM((2 * LANE, LANE), jnp.float32),
            pltpu.VMEM((LANE * LANE // columns, 2 * columns // LANE, LANE), jnp.float32),
        ],
    )(table, received)
    placed = spread(placed)
    arrived_modes = placed[:, 2 * columns // LANE + 4 :].reshape(count, MODES, 2, 2, HALF)
    arrived_modes = arrived_modes.transpose(2, 0, 3, 1, 4)
    steps = 4
    joined_shape = (devices, 2 * rows // LANE + 32, LANE)
    joined = call(
        product_kernel,
        jax.ShapeDtypeStruct(joined_shape, jnp.bfloat16),
        grid=(steps,),
        in_specs=[
            same(*placed.shape),
            pl.BlockSpec((rows // steps, columns), lambda step: (step, 0)),
            same(*packed.shape),
        ],
        out_specs=same(*joined_shape),
        scratch_shapes=[
            pltpu.VMEM((columns // LANE, cases, LANE), jnp.float32),
            pltpu.VMEM((cases, columns), jnp.bfloat16),
            pltpu.VMEM((steps, cases, rows // steps), jnp.float32),
        ],
    )(placed, coarse_inverse, packed)
    joined = spread(joined)
    last = call(
        functools.partial(gather_kernel, row_blocks=lax.axis_size("row")),
        jax.ShapeDtypeStruct((devices, 40, LANE), jnp.bfloat16),
        in_specs=[smem(), whole(), whole()],
        out_specs=whole(),
        scratch_shapes=[
            pltpu.VMEM((2 * LANE, LANE), jnp.float32),
            pltpu.VMEM((devices, 2, LANE), jnp.float32),
        ],
    )(table, received, joined)
    last = spread(last).reshape(count, 2, HALF // 8, 5, 8, LANE)
    return call(
        finish_kernel,
        field,
        grid=(count,),
        in_specs=[
            smem(),
            per_sub(trace_len, cases),
            per_sub(MODES, trace_len),
            same(*last.shape),
            same(*arrived_modes.shape),
        ],
        out_specs=per_sub(trace_len, cases),
        scratch_shapes=[
            pltpu.VMEM((3, cases, LANE), jnp.float32),
            pltpu.VMEM((3, count, MODES, cases), jnp.bfloat16),
        ],
    )(table, local_part, turned_modes, last, arrived_modes)


def solution(mesh):
    return jax.shard_map(
        shards,
        mesh=mesh,
        in_specs=(
            P(AXES, None, None),
            P(AXES, None, None),
            P(AXES, None, None),
            P(AXES),
            P("row", "col"),
            P(AXES, None),
            P(AXES, None),
            P(AXES, None),
        ),
        out_specs=P(AXES, None, None),
        check_vma=False,
    )
```

```python
import functools

import jax
import jax.numpy as jnp
from jax import lax
from jax.experimental import pallas as pl
from jax.experimental.pallas import tpu as pltpu
from jax.sharding import PartitionSpec as P

AXES = ("row", "col")
MODES = 32
HALF = 128
LANE = 128
GROUP = 8
VMEM_LIMIT = 16 * 1024 * 1024


def spread(value):
    return lax.all_to_all(value, AXES, 0, 0, tiled=True)


def call(kernel, out_shape, **kw):
    return pl.pallas_call(
        kernel,
        out_shape=out_shape,
        compiler_params=pltpu.CompilerParams(vmem_limit_bytes=VMEM_LIMIT),
        **kw,
    )


def in_hbm(value):
    return pltpu.with_memory_space_constraint(value, pltpu.HBM)


def smem():
    return pl.BlockSpec(memory_space=pltpu.SMEM)


def table_of(neighbours, block_sizes, block_offsets):
    count = neighbours.shape[0]
    own = lax.axis_index(AXES).astype(jnp.int32)
    device_mask = jnp.bitwise_xor(neighbours[0] // count, own)
    inner_mask = neighbours[0] % count
    second = (block_offsets // HALF) % 2
    both = block_sizes // HALF - 1
    return jnp.concatenate([device_mask, inner_mask, second.reshape(-1), both.reshape(-1)]).astype(
        jnp.int32
    )


def flags(table, sub, which):
    return table[4 + sub * 2 + which], table[12 + sub * 2 + which]


def store_blocks(offsets, sub, load, packed):
    for which in range(2):
        second = jnp.bitwise_and(jnp.right_shift(offsets[which, sub], 7), 1)
        for half in range(2):
            start = which * 2 * HALF + (second * HALF if half == 0 else HALF)
            rows = load(pl.multiple_of(start, HALF)).astype(jnp.float32)
            for lane in range(2):
                tile = rows[:, lane * LANE : (lane + 1) * LANE].reshape(HALF // 8, 8, LANE)
                packed[0, half, :, which * 2 + lane] = tile.astype(jnp.bfloat16)


def pack_kernel(offsets, field, packed):
    store_blocks(offsets, pl.program_id(0), lambda start: field[0, pl.ds(start, HALF)], packed)


def local_kernel(offsets, inverse, weighted, local, packed):
    local[0] = jnp.dot(inverse[0], weighted[0], preferred_element_type=jnp.float32)
    store_blocks(offsets, pl.program_id(0), lambda start: local[0, pl.ds(start, HALF)], packed)


def reroute_kernel(table, chunks, out):
    size = chunks.shape[1] // 2

    def step(device, carry):
        for which in range(2):
            rows = slice(which * size, (which + 1) * size)
            out[device, rows] = chunks[jnp.bitwise_xor(device, table[which]), rows]
        return carry

    lax.fori_loop(0, chunks.shape[0], step, 0, unroll=8)


def exchange(packed, table):
    chunks = spread(packed.reshape(-1, 32, LANE))
    chunks = call(
        reroute_kernel,
        jax.ShapeDtypeStruct(chunks.shape, chunks.dtype),
        in_specs=[smem(), whole()],
        out_specs=whole(),
    )(table, chunks)
    return spread(chunks).reshape(packed.shape)


def arrived_rows(table, sub, which, half, arrived):
    second, both = flags(table, sub, which)
    inside = jnp.maximum(both, (second == half).astype(jnp.int32)).astype(jnp.float32)
    other = jnp.bitwise_xor(sub, table[2 + which])
    tiles = [
        arrived[other, half * both, :, which * 2 + lane].astype(jnp.float32).reshape(HALF, LANE)
        for lane in range(2)
    ]
    return jnp.concatenate(tiles, 1), inside


def weigh_kernel(table, residual, modes, arrived, base, weighted, payload, restricted, turned):
    sub = pl.program_id(0)
    for which in range(2):
        for half in range(2):
            start = (which * 2 + half) * HALF
            rows, inside = arrived_rows(table, sub, which, half, arrived)
            own = residual[0, start : start + HALF].astype(jnp.float32)
            value = (own + rows * inside) * (1.0 - 0.5 * inside)
            weighted[0, start : start + HALF] = value.astype(jnp.bfloat16)
    weighted[0, 4 * HALF :] = residual[0, 4 * HALF :]
    restricted[pl.ds(pl.multiple_of(sub * MODES, MODES), MODES)] = lax.dot_general(
        modes[0], weighted[0], (((1,), (0,)), ((), ())), preferred_element_type=jnp.float32
    )

    @pl.when(sub == pl.num_programs(0) - 1)
    def _():
        devices, rows, _ = payload.shape
        turned[: 2 * devices] = restricted[...].T
        turned[2 * devices :] = jnp.zeros((turned.shape[0] - 2 * devices, LANE), jnp.float32)
        own = lax.broadcasted_iota(jnp.int32, (rows, LANE), 0) < 2

        def step(device, carry):
            piece = turned[pl.ds(2 * device, rows)]
            rest = base[device].astype(jnp.float32)
            payload[device] = jnp.where(own, piece, rest).astype(jnp.bfloat16)
            return carry

        lax.fori_loop(0, devices, step, 0, unroll=8)


def prolong(modes, picked):
    return lax.dot_general(
        modes, picked, (((0,), (0,)), ((), ())), preferred_element_type=jnp.float32
    )


def finish_kernel(table, local, modes, arrived, arrived_modes, out, pairs, picked):
    sub = pl.program_id(0)

    @pl.when(sub == 0)
    def _():
        for first in range(4):
            for half in range(2):

                def step(piece, carry, first=first, half=half):
                    for inner in range(4):
                        tile = arrived[first, half, piece * 4 + inner, 4].astype(jnp.float32)
                        at = (first * 2 + half) * 32 + pl.multiple_of(piece * 8, 8) + inner * 2
                        for kind in range(3):
                            pairs[kind, pl.ds(at, 2)] = tile[kind * 2 : kind * 2 + 2]
                    return carry

                lax.fori_loop(0, 4, step, 0)
        for kind in range(3):
            picked[kind] = pairs[kind].T.reshape(picked.shape[1:]).astype(jnp.bfloat16)

    added = prolong(modes[0], picked[0, sub])
    for which in range(2):
        other = jnp.bitwise_xor(sub, table[2 + which])
        for half in range(2):
            start = (which * 2 + half) * HALF
            rows, inside = arrived_rows(table, sub, which, half, arrived)
            _, both = flags(table, sub, which)
            theirs = prolong(arrived_modes[which * 2 + half * both, other], picked[1 + which, other])
            theirs = (0.5 * (rows + theirs)).astype(jnp.bfloat16).astype(jnp.float32)
            own = local[0, start : start + HALF] + added[start : start + HALF]
            own = (own * (1.0 - 0.5 * inside)).astype(jnp.bfloat16).astype(jnp.float32)
            out[0, start : start + HALF] = (own + theirs * inside).astype(jnp.bfloat16)
    out[0, 4 * HALF :] = (local[0, 4 * HALF :] + added[4 * HALF :]).astype(jnp.bfloat16)


def scatter_kernel(table, received, out, total, staged):
    devices = received.shape[0]
    place = lax.broadcasted_iota(jnp.int32, (LANE, LANE), 0).astype(jnp.float32)
    total[...] = jnp.zeros_like(total)

    def step(block, carry):
        left, right = [], []
        for inner in range(GROUP):
            piece = received[block * GROUP + inner].astype(jnp.float32)
            high = place == piece[2:3]
            low = place == piece[3:4]
            left.append(
                jnp.concatenate(
                    [jnp.where(high, piece[0:1], 0.0), jnp.where(high, piece[1:2], 0.0)], 0
                ).astype(jnp.bfloat16)
            )
            right.append(jnp.where(low, 1.0, 0.0).astype(jnp.bfloat16))
        total[...] += lax.dot_general(
            jnp.concatenate(left, 1),
            jnp.concatenate(right, 1),
            (((1,), (1,)), ((), ())),
            preferred_element_type=jnp.float32,
        )
        return carry

    lax.fori_loop(0, devices // GROUP, step, 0)
    blocks, size, _ = staged.shape
    pieces = size // 2
    for block in range(blocks):
        for case in range(2):
            for piece in range(pieces):
                at = case * LANE + block * pieces + piece
                staged[block, piece * 2 + case : piece * 2 + case + 1] = total[at : at + 1]
    for block in range(blocks):
        value = staged[block].astype(jnp.bfloat16)

        def copies(row, carry, block=block, value=value):
            out[row * blocks + block, :size] = value
            return carry

        lax.fori_loop(0, devices // blocks, copies, 0, unroll=4)
    first = lax.broadcasted_iota(jnp.int32, (8, LANE), 0) < 6

    def forward(device, carry):
        pieces = [
            received[jnp.bitwise_xor(device, table[which])].astype(jnp.float32) for which in range(2)
        ]
        out[device, size:] = jnp.where(first, pieces[0], pieces[1]).astype(jnp.bfloat16)
        return carry

    lax.fori_loop(0, devices, forward, 0, unroll=4)


def product_kernel(placed, inverse, packed, out, their_modes, pairs, left, parts):
    at_step = pl.program_id(0)
    groups = placed.shape[0] // 4
    tiles, steps = pairs.shape[0], parts.shape[0]

    @pl.when(at_step == 0)
    def _():
        def step(group, carry):
            for inner in range(4):
                rows = placed[group * 4 + inner, : 2 * tiles].astype(jnp.float32)
                at = pl.multiple_of(group * 8, 8) + 2 * inner
                for tile in range(tiles):
                    pairs[tile, pl.ds(at, 2)] = rows[2 * tile : 2 * tile + 2]
            return carry

        lax.fori_loop(0, groups, step, 0)
        for tile in range(tiles):
            left[:, tile * LANE : (tile + 1) * LANE] = pairs[tile].astype(jnp.bfloat16)

    @pl.when(at_step == 1)
    def _():
        def step(group, carry):
            for inner in range(8):
                row = pl.multiple_of(group * 8, 8) + inner
                tile = placed[row, 2 * tiles :].astype(jnp.float32)
                for kind in range(4):
                    pairs[kind, pl.ds(row, 1)] = tile[4 + kind : 5 + kind]
            return carry

        lax.fori_loop(0, placed.shape[0] // 8, step, 0)
        for kind in range(4):
            value = pairs[kind, : placed.shape[0]].astype(jnp.bfloat16)
            their_modes[kind] = value.reshape(their_modes.shape[1:])

    parts[at_step] = lax.dot_general(
        left[...], inverse[...], (((1,), (1,)), ((), ())), preferred_element_type=jnp.float32
    )

    @pl.when(at_step == steps - 1)
    def _():
        size = steps * parts.shape[2] // LANE * 2

        def step(group, carry):
            at = pl.multiple_of(group * 8, 8)
            tall = [
                parts[part, pl.ds(at, 8), lane * LANE : (lane + 1) * LANE]
                for part in range(steps)
                for lane in range(parts.shape[2] // LANE)
            ]
            for inner in range(4):
                rows = jnp.concatenate([tile[2 * inner : 2 * inner + 2] for tile in tall], 0)
                out[group * 4 + inner, :size] = rows.astype(jnp.bfloat16)
                out[group * 4 + inner, size:] = packed[group * 4 + inner]
            return carry

        lax.fori_loop(0, groups, step, 0)


def gather_kernel(table, received, partial, out, solved, chosen_rows, *, row_blocks):
    devices = received.shape[0]
    pieces = LANE // row_blocks
    col_blocks = devices // row_blocks
    for block in range(row_blocks):
        value = partial[block * col_blocks, : 2 * pieces].astype(jnp.float32)
        for col in range(1, col_blocks):
            value = value + partial[block * col_blocks + col, : 2 * pieces].astype(jnp.float32)
        for piece in range(pieces):
            for case in range(2):
                at = case * LANE + block * pieces + piece
                solved[at : at + 1] = value[2 * piece + case : 2 * piece + case + 1]
    turned = jnp.concatenate([solved[:LANE].T, solved[LANE:].T], 0).astype(jnp.bfloat16)
    place = lax.broadcasted_iota(jnp.int32, (LANE, LANE), 0).astype(jnp.float32)

    def step(block, carry):
        highs, lows = [], []
        for inner in range(GROUP):
            piece = received[block * GROUP + inner].astype(jnp.float32)
            highs.append(jnp.where(place == piece[2:3], 1.0, 0.0).astype(jnp.bfloat16))
            lows.append(place == piece[3:4])
        chosen = lax.dot_general(
            turned,
            jnp.concatenate(highs, 1),
            (((1,), (0,)), ((), ())),
            preferred_element_type=jnp.float32,
        )
        for inner in range(GROUP):
            lanes = slice(inner * LANE, (inner + 1) * LANE)
            both = [
                jnp.sum(
                    jnp.where(lows[inner], chosen[case * LANE : (case + 1) * LANE, lanes], 0.0),
                    axis=0,
                    keepdims=True,
                )
                for case in range(2)
            ]
            chosen_rows[block * GROUP + inner] = jnp.concatenate(both, 0)
        return carry

    lax.fori_loop(0, devices // GROUP, step, 0)

    size = (partial.shape[1] - 2 * pieces) // 2

    def share(device, carry):
        sources = [jnp.bitwise_xor(device, table[which]) for which in range(2)]
        for which in range(2):
            at = 2 * pieces + which * size
            out[device, which * size : (which + 1) * size] = partial[sources[which], at : at + size]
        rows = [chosen_rows[device], chosen_rows[sources[0]], chosen_rows[sources[1]]]
        rows.append(jnp.zeros_like(rows[0]))
        out[device, 2 * size :] = jnp.concatenate(rows, 0).astype(jnp.bfloat16)
        return carry

    lax.fori_loop(0, devices, share, 0, unroll=4)


def whole():
    return pl.BlockSpec(memory_space=pltpu.VMEM)


def per_sub(*shape):
    zeros = (0,) * len(shape)
    return pl.BlockSpec((1,) + shape, lambda sub: (sub,) + zeros)


def same(*shape):
    zeros = (0,) * len(shape)
    return pl.BlockSpec(shape, lambda sub: zeros)


def shards(
    residual,
    interface_inverse,
    modes,
    coarse_map,
    coarse_inverse,
    neighbours,
    block_sizes,
    block_offsets,
):
    count, trace_len, cases = residual.shape
    devices = cases // 2
    table = table_of(neighbours, block_sizes, block_offsets)
    field = jax.ShapeDtypeStruct(residual.shape, jnp.bfloat16)

    turned_modes = modes.transpose(0, 2, 1)
    residual = in_hbm(residual)
    offsets = block_offsets.T
    packed_spec = per_sub(2, HALF // 8, 4, 8, LANE)
    packed_shape = jax.ShapeDtypeStruct((count, 2, HALF // 8, 4, 8, LANE), jnp.bfloat16)

    packed = call(
        pack_kernel,
        packed_shape,
        grid=(count,),
        in_specs=[smem(), per_sub(4 * HALF, cases)],
        out_specs=packed_spec,
    )(offsets, residual)
    arrived = exchange(packed, table)
    digits = jnp.stack([coarse_map // LANE, coarse_map % LANE]).astype(jnp.bfloat16)
    digits = jnp.concatenate([jnp.zeros_like(digits), digits], 0)
    shared = turned_modes[:, :, : 4 * HALF].reshape(count, MODES, 2, 2, HALF)
    second = table[4:12].reshape(count, 1, 2, 1) == 1
    shared = jnp.stack(
        [jnp.where(second, shared[:, :, :, 1], shared[:, :, :, 0]), shared[:, :, :, 1]], 3
    ).reshape(devices, 4, HALF)
    base = jnp.concatenate([jnp.broadcast_to(digits[None], (devices,) + digits.shape), shared], 1)
    weighted, payload = call(
        weigh_kernel,
        (pltpu.HBM(residual.shape, jnp.bfloat16), jax.ShapeDtypeStruct(base.shape, jnp.bfloat16)),
        grid=(count,),
        in_specs=[
            smem(),
            per_sub(trace_len, cases),
            per_sub(MODES, trace_len),
            same(*arrived.shape),
            same(*base.shape),
        ],
        out_specs=(per_sub(trace_len, cases), same(*base.shape)),
        scratch_shapes=[
            pltpu.VMEM((count * MODES, cases), jnp.float32),
            pltpu.VMEM((cases + 8, LANE), jnp.float32),
        ],
    )(table, residual, turned_modes, arrived, in_hbm(base))
    received = spread(payload)
    weighted, received = lax.optimization_barrier((weighted, received))

    local_part, packed = call(
        local_kernel,
        (pltpu.HBM(residual.shape, jnp.float32), packed_shape),
        grid=(count,),
        in_specs=[smem(), per_sub(trace_len, trace_len), per_sub(trace_len, cases)],
        out_specs=(per_sub(trace_len, cases), packed_spec),
    )(offsets, in_hbm(interface_inverse), in_hbm(weighted))
    packed = packed.reshape(devices, 32, LANE)

    rows, columns = coarse_inverse.shape
    placed = call(
        scatter_kernel,
        jax.ShapeDtypeStruct((devices, 2 * columns // LANE + 8, LANE), jnp.bfloat16),
        in_specs=[smem(), whole()],
        out_specs=whole(),
        scratch_shapes=[
            pltpu.VMEM((2 * LANE, LANE), jnp.float32),
            pltpu.VMEM((LANE * LANE // columns, 2 * columns // LANE, LANE), jnp.float32),
        ],
    )(table, received)
    placed = spread(placed)
    steps = 4
    joined_shape = (devices, 2 * rows // LANE + 32, LANE)
    modes_shape = (4, count, MODES, HALF)
    joined, their_modes = call(
        product_kernel,
        (
            jax.ShapeDtypeStruct(joined_shape, jnp.bfloat16),
            jax.ShapeDtypeStruct(modes_shape, jnp.bfloat16),
        ),
        grid=(steps,),
        in_specs=[
            same(*placed.shape),
            pl.BlockSpec((rows // steps, columns), lambda step: (step, 0)),
            same(*packed.shape),
        ],
        out_specs=(same(*joined_shape), same(*modes_shape)),
        scratch_shapes=[
            pltpu.VMEM((columns // LANE, cases, LANE), jnp.float32),
            pltpu.VMEM((cases, columns), jnp.bfloat16),
            pltpu.VMEM((steps, cases, rows // steps), jnp.float32),
        ],
    )(placed, in_hbm(coarse_inverse), packed)
    joined = spread(joined)
    last = call(
        functools.partial(gather_kernel, row_blocks=lax.axis_size("row")),
        jax.ShapeDtypeStruct((devices, 40, LANE), jnp.bfloat16),
        in_specs=[smem(), whole(), whole()],
        out_specs=whole(),
        scratch_shapes=[
            pltpu.VMEM((2 * LANE, LANE), jnp.float32),
            pltpu.VMEM((devices, 2, LANE), jnp.float32),
        ],
    )(table, received, joined)
    last = spread(last).reshape(count, 2, HALF // 8, 5, 8, LANE)
    return call(
        finish_kernel,
        field,
        grid=(count,),
        in_specs=[
            smem(),
            per_sub(trace_len, cases),
            per_sub(MODES, trace_len),
            same(*last.shape),
            same(*modes_shape),
        ],
        out_specs=per_sub(trace_len, cases),
        scratch_shapes=[
            pltpu.VMEM((3, cases, LANE), jnp.float32),
            pltpu.VMEM((3, count, MODES, cases), jnp.bfloat16),
        ],
    )(table, in_hbm(local_part), turned_modes, last, their_modes)


def solution(mesh):
    return jax.shard_map(
        shards,
        mesh=mesh,
        in_specs=(
            P(AXES, None, None),
            P(AXES, None, None),
            P(AXES, None, None),
            P(AXES),
            P("row", "col"),
            P(AXES, None),
            P(AXES, None),
            P(AXES, None),
        ),
        out_specs=P(AXES, None, None),
        check_vma=False,
    )
```

```python
import functools

import jax
import jax.numpy as jnp
from jax import lax
from jax.experimental import pallas as pl
from jax.experimental.pallas import tpu as pltpu
from jax.sharding import PartitionSpec as P

AXES = ("row", "col")
MODES = 32
HALF = 128
LANE = 128
GROUP = 64
VMEM_LIMIT = 16 * 1024 * 1024


def spread(value):
    return lax.all_to_all(value, AXES, 0, 0, tiled=True)


def call(kernel, out_shape, **kw):
    return pl.pallas_call(
        kernel,
        out_shape=out_shape,
        compiler_params=pltpu.CompilerParams(vmem_limit_bytes=VMEM_LIMIT),
        **kw,
    )


def in_hbm(value):
    return pltpu.with_memory_space_constraint(value, pltpu.HBM)


def smem():
    return pl.BlockSpec(memory_space=pltpu.SMEM)


def table_of(neighbours, block_sizes, block_offsets):
    count = neighbours.shape[0]
    own = lax.axis_index(AXES).astype(jnp.int32)
    device_mask = jnp.bitwise_xor(neighbours[0] // count, own)
    inner_mask = neighbours[0] % count
    second = (block_offsets // HALF) % 2
    both = block_sizes // HALF - 1
    return jnp.concatenate([device_mask, inner_mask, second.reshape(-1), both.reshape(-1)]).astype(
        jnp.int32
    )


def flags(table, sub, which):
    return table[4 + sub * 2 + which], table[12 + sub * 2 + which]


def store_blocks(offsets, sub, load, packed):
    for which in range(2):
        second = jnp.bitwise_and(jnp.right_shift(offsets[which, sub], 7), 1)
        for half in range(2):
            start = which * 2 * HALF + (second * HALF if half == 0 else HALF)
            rows = load(pl.multiple_of(start, HALF)).astype(jnp.float32)
            for lane in range(2):
                tile = rows[:, lane * LANE : (lane + 1) * LANE].reshape(HALF // 8, 8, LANE)
                packed[0, half, :, which * 2 + lane] = tile.astype(jnp.bfloat16)


def pack_kernel(offsets, tiles, packed, done):
    size = HALF // 8
    copies = []
    for sub in range(tiles.shape[0]):
        for which in range(2):
            second = jnp.bitwise_and(jnp.right_shift(offsets[which, sub], 7), 1)
            for half in range(2):
                start = which * 2 * size + (second * size if half == 0 else size)
                copies.append(
                    pltpu.make_async_copy(
                        tiles.at[sub, pl.ds(start, size)],
                        packed.at[sub, half, :, pl.ds(which * 2, 2)],
                        done.at[sub, which, half],
                    )
                )
                copies[-1].start()
    for copy in copies:
        copy.wait()


def local_kernel(offsets, inverse, weighted, local, packed):
    local[0] = jnp.dot(inverse[0], weighted[0], preferred_element_type=jnp.float32)
    store_blocks(offsets, pl.program_id(0), lambda start: local[0, pl.ds(start, HALF)], packed)


def reroute_kernel(table, chunks, out):
    size = chunks.shape[1] // 2

    def step(device, carry):
        for which in range(2):
            rows = slice(which * size, (which + 1) * size)
            out[device, rows] = chunks[jnp.bitwise_xor(device, table[which]), rows]
        return carry

    lax.fori_loop(0, chunks.shape[0], step, 0, unroll=8)


def exchange(packed, table):
    chunks = spread(packed.reshape(-1, 32, LANE))
    chunks = call(
        reroute_kernel,
        jax.ShapeDtypeStruct(chunks.shape, chunks.dtype),
        in_specs=[smem(), whole()],
        out_specs=whole(),
    )(table, chunks)
    return spread(chunks).reshape(packed.shape)


def arrived_rows(table, sub, which, half, arrived):
    second, both = flags(table, sub, which)
    inside = jnp.maximum(both, (second == half).astype(jnp.int32)).astype(jnp.float32)
    other = jnp.bitwise_xor(sub, table[2 + which])
    tiles = [
        arrived[other, half * both, :, which * 2 + lane].astype(jnp.float32).reshape(HALF, LANE)
        for lane in range(2)
    ]
    return jnp.concatenate(tiles, 1), inside


def weigh_kernel(table, residual, modes, arrived, base, weighted, payload, restricted, turned):
    sub = pl.program_id(0)
    for which in range(2):
        for half in range(2):
            start = (which * 2 + half) * HALF
            rows, inside = arrived_rows(table, sub, which, half, arrived)
            own = residual[0, start : start + HALF].astype(jnp.float32)
            value = (own + rows * inside) * (1.0 - 0.5 * inside)
            weighted[0, start : start + HALF] = value.astype(jnp.bfloat16)
    weighted[0, 4 * HALF :] = residual[0, 4 * HALF :]
    restricted[pl.ds(pl.multiple_of(sub * MODES, MODES), MODES)] = lax.dot_general(
        modes[0], weighted[0], (((1,), (0,)), ((), ())), preferred_element_type=jnp.float32
    )

    @pl.when(sub == pl.num_programs(0) - 1)
    def _():
        devices, rows, _ = payload.shape
        turned[: 2 * devices] = restricted[...].T
        turned[2 * devices :] = jnp.zeros((turned.shape[0] - 2 * devices, LANE), jnp.float32)
        own = lax.broadcasted_iota(jnp.int32, (rows, LANE), 0) < 2

        def step(device, carry):
            piece = turned[pl.ds(2 * device, rows)]
            rest = base[device].astype(jnp.float32)
            payload[device] = jnp.where(own, piece, rest).astype(jnp.bfloat16)
            return carry

        lax.fori_loop(0, devices, step, 0, unroll=8)


def prolong(modes, picked):
    return lax.dot_general(
        modes, picked, (((0,), (0,)), ((), ())), preferred_element_type=jnp.float32
    )


def finish_kernel(table, local, modes, arrived, arrived_modes, out, pairs, picked):
    sub = pl.program_id(0)

    @pl.when(sub == 0)
    def _():
        for first in range(4):
            for half in range(2):

                def step(piece, carry, first=first, half=half):
                    for inner in range(4):
                        tile = arrived[first, half, piece * 4 + inner, 4].astype(jnp.float32)
                        at = (first * 2 + half) * 32 + pl.multiple_of(piece * 8, 8) + inner * 2
                        for kind in range(3):
                            pairs[kind, pl.ds(at, 2)] = tile[kind * 2 : kind * 2 + 2]
                    return carry

                lax.fori_loop(0, 4, step, 0)
        for kind in range(3):
            picked[kind] = pairs[kind].T.reshape(picked.shape[1:]).astype(jnp.bfloat16)

    added = prolong(modes[0], picked[0, sub])
    for which in range(2):
        other = jnp.bitwise_xor(sub, table[2 + which])
        for half in range(2):
            start = (which * 2 + half) * HALF
            rows, inside = arrived_rows(table, sub, which, half, arrived)
            _, both = flags(table, sub, which)
            theirs = prolong(arrived_modes[which * 2 + half * both, other], picked[1 + which, other])
            theirs = (0.5 * (rows + theirs)).astype(jnp.bfloat16).astype(jnp.float32)
            own = local[0, start : start + HALF] + added[start : start + HALF]
            own = (own * (1.0 - 0.5 * inside)).astype(jnp.bfloat16).astype(jnp.float32)
            out[0, start : start + HALF] = (own + theirs * inside).astype(jnp.bfloat16)
    out[0, 4 * HALF :] = (local[0, 4 * HALF :] + added[4 * HALF :]).astype(jnp.bfloat16)


def scatter_kernel(table, received, out, total, staged):
    devices = received.shape[0]
    place = lax.broadcasted_iota(jnp.int32, (LANE, LANE), 0).astype(jnp.float32)
    total[...] = jnp.zeros_like(total)

    def step(block, carry):
        left, right = [], []
        for inner in range(GROUP):
            piece = received[block * GROUP + inner].astype(jnp.float32)
            high = place == piece[2:3]
            low = place == piece[3:4]
            left.append(
                jnp.concatenate(
                    [jnp.where(high, piece[0:1], 0.0), jnp.where(high, piece[1:2], 0.0)], 0
                ).astype(jnp.bfloat16)
            )
            right.append(jnp.where(low, 1.0, 0.0).astype(jnp.bfloat16))
        total[...] += lax.dot_general(
            jnp.concatenate(left, 1),
            jnp.concatenate(right, 1),
            (((1,), (1,)), ((), ())),
            preferred_element_type=jnp.float32,
        )
        return carry

    lax.fori_loop(0, devices // GROUP, step, 0)
    blocks, size, _ = staged.shape
    pieces = size // 2
    for block in range(blocks):
        for case in range(2):
            for piece in range(pieces):
                at = case * LANE + block * pieces + piece
                staged[block, piece * 2 + case : piece * 2 + case + 1] = total[at : at + 1]
    for block in range(blocks):
        value = staged[block].astype(jnp.bfloat16)

        def copies(row, carry, block=block, value=value):
            out[row * blocks + block, :size] = value
            return carry

        lax.fori_loop(0, devices // blocks, copies, 0, unroll=4)
    first = lax.broadcasted_iota(jnp.int32, (8, LANE), 0) < 6

    def forward(device, carry):
        pieces = [
            received[jnp.bitwise_xor(device, table[which])].astype(jnp.float32) for which in range(2)
        ]
        out[device, size:] = jnp.where(first, pieces[0], pieces[1]).astype(jnp.bfloat16)
        return carry

    lax.fori_loop(0, devices, forward, 0, unroll=4)


def product_kernel(placed, inverse, packed, out, their_modes, pairs, left, parts):
    at_step = pl.program_id(0)
    groups = placed.shape[0] // 4
    tiles, steps = pairs.shape[0], parts.shape[0]

    @pl.when(at_step == 0)
    def _():
        def step(group, carry):
            for inner in range(4):
                rows = placed[group * 4 + inner, : 2 * tiles].astype(jnp.float32)
                at = pl.multiple_of(group * 8, 8) + 2 * inner
                for tile in range(tiles):
                    pairs[tile, pl.ds(at, 2)] = rows[2 * tile : 2 * tile + 2]
            return carry

        lax.fori_loop(0, groups, step, 0)
        for tile in range(tiles):
            left[:, tile * LANE : (tile + 1) * LANE] = pairs[tile].astype(jnp.bfloat16)

    @pl.when(at_step == 1)
    def _():
        def step(group, carry):
            for inner in range(8):
                row = pl.multiple_of(group * 8, 8) + inner
                tile = placed[row, 2 * tiles :].astype(jnp.float32)
                for kind in range(4):
                    pairs[kind, pl.ds(row, 1)] = tile[4 + kind : 5 + kind]
            return carry

        lax.fori_loop(0, placed.shape[0] // 8, step, 0)
        for kind in range(4):
            value = pairs[kind, : placed.shape[0]].astype(jnp.bfloat16)
            their_modes[kind] = value.reshape(their_modes.shape[1:])

    parts[at_step] = lax.dot_general(
        left[...], inverse[...], (((1,), (1,)), ((), ())), preferred_element_type=jnp.float32
    )

    @pl.when(at_step == steps - 1)
    def _():
        size = steps * parts.shape[2] // LANE * 2

        def step(group, carry):
            at = pl.multiple_of(group * 8, 8)
            tall = [
                parts[part, pl.ds(at, 8), lane * LANE : (lane + 1) * LANE]
                for part in range(steps)
                for lane in range(parts.shape[2] // LANE)
            ]
            for inner in range(4):
                rows = jnp.concatenate([tile[2 * inner : 2 * inner + 2] for tile in tall], 0)
                out[group * 4 + inner, :size] = rows.astype(jnp.bfloat16)
                out[group * 4 + inner, size:] = packed[group * 4 + inner]
            return carry

        lax.fori_loop(0, groups, step, 0)


def gather_kernel(table, received, partial, out, solved, chosen_rows, *, row_blocks):
    devices = received.shape[0]
    pieces = LANE // row_blocks
    col_blocks = devices // row_blocks
    for block in range(row_blocks):
        value = partial[block * col_blocks, : 2 * pieces].astype(jnp.float32)
        for col in range(1, col_blocks):
            value = value + partial[block * col_blocks + col, : 2 * pieces].astype(jnp.float32)
        for piece in range(pieces):
            for case in range(2):
                at = case * LANE + block * pieces + piece
                solved[at : at + 1] = value[2 * piece + case : 2 * piece + case + 1]
    turned = jnp.concatenate([solved[:LANE].T, solved[LANE:].T], 0).astype(jnp.bfloat16)
    place = lax.broadcasted_iota(jnp.int32, (LANE, LANE), 0).astype(jnp.float32)

    def step(block, carry):
        highs, lows = [], []
        for inner in range(GROUP):
            piece = received[block * GROUP + inner].astype(jnp.float32)
            highs.append(jnp.where(place == piece[2:3], 1.0, 0.0).astype(jnp.bfloat16))
            lows.append(place == piece[3:4])
        chosen = lax.dot_general(
            turned,
            jnp.concatenate(highs, 1),
            (((1,), (0,)), ((), ())),
            preferred_element_type=jnp.float32,
        )
        for inner in range(GROUP):
            lanes = slice(inner * LANE, (inner + 1) * LANE)
            both = [
                jnp.sum(
                    jnp.where(lows[inner], chosen[case * LANE : (case + 1) * LANE, lanes], 0.0),
                    axis=0,
                    keepdims=True,
                )
                for case in range(2)
            ]
            chosen_rows[block * GROUP + inner] = jnp.concatenate(both, 0)
        return carry

    lax.fori_loop(0, devices // GROUP, step, 0)

    size = (partial.shape[1] - 2 * pieces) // 2

    def share(device, carry):
        sources = [jnp.bitwise_xor(device, table[which]) for which in range(2)]
        for which in range(2):
            at = 2 * pieces + which * size
            out[device, which * size : (which + 1) * size] = partial[sources[which], at : at + size]
        rows = [chosen_rows[device], chosen_rows[sources[0]], chosen_rows[sources[1]]]
        rows.append(jnp.zeros_like(rows[0]))
        out[device, 2 * size :] = jnp.concatenate(rows, 0).astype(jnp.bfloat16)
        return carry

    lax.fori_loop(0, devices, share, 0, unroll=4)


def whole():
    return pl.BlockSpec(memory_space=pltpu.VMEM)


def per_sub(*shape):
    zeros = (0,) * len(shape)
    return pl.BlockSpec((1,) + shape, lambda sub: (sub,) + zeros)


def same(*shape):
    zeros = (0,) * len(shape)
    return pl.BlockSpec(shape, lambda sub: zeros)


def shards(
    residual,
    interface_inverse,
    modes,
    coarse_map,
    coarse_inverse,
    neighbours,
    block_sizes,
    block_offsets,
):
    count, trace_len, cases = residual.shape
    devices = cases // 2
    table = table_of(neighbours, block_sizes, block_offsets)
    field = jax.ShapeDtypeStruct(residual.shape, jnp.bfloat16)

    turned_modes = modes.transpose(0, 2, 1)
    offsets = block_offsets.T
    packed_spec = per_sub(2, HALF // 8, 4, 8, LANE)
    packed_shape = jax.ShapeDtypeStruct((count, 2, HALF // 8, 4, 8, LANE), jnp.bfloat16)

    tiles = residual.reshape(count, trace_len // 8, 8, 2, LANE).transpose(0, 1, 3, 2, 4)
    hbm = pl.BlockSpec(memory_space=pltpu.HBM)
    packed = call(
        pack_kernel,
        pltpu.HBM(packed_shape.shape, jnp.bfloat16),
        in_specs=[smem(), hbm],
        out_specs=hbm,
        scratch_shapes=[pltpu.SemaphoreType.DMA((count, 2, 2))],
    )(offsets, in_hbm(tiles))
    arrived = exchange(packed, table)
    digits = jnp.stack([coarse_map // LANE, coarse_map % LANE]).astype(jnp.bfloat16)
    digits = jnp.concatenate([jnp.zeros_like(digits), digits], 0)
    shared = turned_modes[:, :, : 4 * HALF].reshape(count, MODES, 2, 2, HALF)
    second = table[4:12].reshape(count, 1, 2, 1) == 1
    shared = jnp.stack(
        [jnp.where(second, shared[:, :, :, 1], shared[:, :, :, 0]), shared[:, :, :, 1]], 3
    ).reshape(devices, 4, HALF)
    base = jnp.concatenate([jnp.broadcast_to(digits[None], (devices,) + digits.shape), shared], 1)
    weighted, payload = call(
        weigh_kernel,
        (pltpu.HBM(residual.shape, jnp.bfloat16), jax.ShapeDtypeStruct(base.shape, jnp.bfloat16)),
        grid=(count,),
        in_specs=[
            smem(),
            per_sub(trace_len, cases),
            per_sub(MODES, trace_len),
            same(*arrived.shape),
            same(*base.shape),
        ],
        out_specs=(per_sub(trace_len, cases), same(*base.shape)),
        scratch_shapes=[
            pltpu.VMEM((count * MODES, cases), jnp.float32),
            pltpu.VMEM((cases + 8, LANE), jnp.float32),
        ],
    )(table, residual, turned_modes, arrived, in_hbm(base))
    received = spread(payload)
    weighted, received = lax.optimization_barrier((weighted, received))

    local_part, packed = call(
        local_kernel,
        (
            pltpu.HBM(residual.shape, jnp.float32),
            pltpu.HBM(packed_shape.shape, jnp.bfloat16),
        ),
        grid=(count,),
        in_specs=[smem(), per_sub(trace_len, trace_len), per_sub(trace_len, cases)],
        out_specs=(per_sub(trace_len, cases), packed_spec),
    )(offsets, in_hbm(interface_inverse), in_hbm(weighted))
    packed = packed.reshape(devices, 32, LANE)

    rows, columns = coarse_inverse.shape
    placed = call(
        scatter_kernel,
        jax.ShapeDtypeStruct((devices, 2 * columns // LANE + 8, LANE), jnp.bfloat16),
        in_specs=[smem(), whole()],
        out_specs=whole(),
        scratch_shapes=[
            pltpu.VMEM((2 * LANE, LANE), jnp.float32),
            pltpu.VMEM((LANE * LANE // columns, 2 * columns // LANE, LANE), jnp.float32),
        ],
    )(table, received)
    placed = spread(placed)
    steps = 4
    joined_shape = (devices, 2 * rows // LANE + 32, LANE)
    modes_shape = (4, count, MODES, HALF)
    joined, their_modes = call(
        product_kernel,
        (
            jax.ShapeDtypeStruct(joined_shape, jnp.bfloat16),
            jax.ShapeDtypeStruct(modes_shape, jnp.bfloat16),
        ),
        grid=(steps,),
        in_specs=[
            same(*placed.shape),
            pl.BlockSpec((rows // steps, columns), lambda step: (step, 0)),
            same(*packed.shape),
        ],
        out_specs=(same(*joined_shape), same(*modes_shape)),
        scratch_shapes=[
            pltpu.VMEM((columns // LANE, cases, LANE), jnp.float32),
            pltpu.VMEM((cases, columns), jnp.bfloat16),
            pltpu.VMEM((steps, cases, rows // steps), jnp.float32),
        ],
    )(placed, in_hbm(coarse_inverse), in_hbm(packed))
    joined = spread(joined)
    last = call(
        functools.partial(gather_kernel, row_blocks=lax.axis_size("row")),
        jax.ShapeDtypeStruct((devices, 40, LANE), jnp.bfloat16),
        in_specs=[smem(), whole(), whole()],
        out_specs=whole(),
        scratch_shapes=[
            pltpu.VMEM((2 * LANE, LANE), jnp.float32),
            pltpu.VMEM((devices, 2, LANE), jnp.float32),
        ],
    )(table, received, joined)
    last = spread(last).reshape(count, 2, HALF // 8, 5, 8, LANE)
    return call(
        finish_kernel,
        field,
        grid=(count,),
        in_specs=[
            smem(),
            per_sub(trace_len, cases),
            per_sub(MODES, trace_len),
            same(*last.shape),
            same(*modes_shape),
        ],
        out_specs=per_sub(trace_len, cases),
        scratch_shapes=[
            pltpu.VMEM((3, cases, LANE), jnp.float32),
            pltpu.VMEM((3, count, MODES, cases), jnp.bfloat16),
        ],
    )(table, in_hbm(local_part), turned_modes, last, their_modes)


def solution(mesh):
    return jax.shard_map(
        shards,
        mesh=mesh,
        in_specs=(
            P(AXES, None, None),
            P(AXES, None, None),
            P(AXES, None, None),
            P(AXES),
            P("row", "col"),
            P(AXES, None),
            P(AXES, None),
            P(AXES, None),
        ),
        out_specs=P(AXES, None, None),
        check_vma=False,
    )
```

```python
import functools

import jax
import jax.numpy as jnp
from jax import lax
from jax.experimental import pallas as pl
from jax.experimental.pallas import tpu as pltpu
from jax.sharding import PartitionSpec as P

AXES = ("row", "col")
MODES = 32
HALF = 128
LANE = 128
GROUP = 64
VMEM_LIMIT = 16 * 1024 * 1024


def spread(value):
    return lax.all_to_all(value, AXES, 0, 0, tiled=True)


def call(kernel, out_shape, **kw):
    return pl.pallas_call(
        kernel,
        out_shape=out_shape,
        compiler_params=pltpu.CompilerParams(vmem_limit_bytes=VMEM_LIMIT),
        **kw,
    )


def in_hbm(value):
    return pltpu.with_memory_space_constraint(value, pltpu.HBM)


def smem():
    return pl.BlockSpec(memory_space=pltpu.SMEM)


def table_of(neighbours, block_sizes, block_offsets):
    count = neighbours.shape[0]
    own = lax.axis_index(AXES).astype(jnp.int32)
    device_mask = jnp.bitwise_xor(neighbours[0] // count, own)
    inner_mask = neighbours[0] % count
    second = (block_offsets // HALF) % 2
    both = block_sizes // HALF - 1
    return jnp.concatenate([device_mask, inner_mask, second.reshape(-1), both.reshape(-1)]).astype(
        jnp.int32
    )


def flags(table, sub, which):
    return table[4 + sub * 2 + which], table[12 + sub * 2 + which]


def store_blocks(offsets, sub, load, packed):
    before = packed.shape[3] - 4
    for which in range(2):
        second = jnp.bitwise_and(jnp.right_shift(offsets[which, sub], 7), 1)
        for half in range(2):
            start = which * 2 * HALF + (second * HALF if half == 0 else HALF)
            rows = load(pl.multiple_of(start, HALF)).astype(jnp.float32)
            for lane in range(2):
                tile = rows[:, lane * LANE : (lane + 1) * LANE].reshape(HALF // 8, 8, LANE)
                packed[0, half, :, before + which * 2 + lane] = tile.astype(jnp.bfloat16)


def pack_kernel(offsets, tiles, packed, staged, read, written):
    size = HALF // 8
    reads, writes = [], []
    for sub in range(tiles.shape[0]):
        for which in range(2):
            second = jnp.bitwise_and(jnp.right_shift(offsets[which, sub], 7), 1)
            for half in range(2):
                start = which * 2 * size + (second * size if half == 0 else size)
                at = (sub * 2 + which) * 2 + half
                reads.append(
                    pltpu.make_async_copy(
                        tiles.at[sub, pl.ds(start, size)], staged.at[at], read.at[at]
                    )
                )
                reads[-1].start()
                writes.append(
                    pltpu.make_async_copy(
                        staged.at[at],
                        packed.at[sub, half, :, pl.ds(which * 2, 2)],
                        written.at[at],
                    )
                )
    for first, second in zip(reads, writes):
        first.wait()
        second.start()
    for copy in writes:
        copy.wait()


def local_kernel(offsets, inverse, weighted, local, packed):
    local[0] = jnp.dot(inverse[0], weighted[0], preferred_element_type=jnp.float32)
    store_blocks(offsets, pl.program_id(0), lambda start: local[0, pl.ds(start, HALF)], packed)


def reroute_kernel(table, chunks, out):
    size = chunks.shape[1] // 2

    def step(device, carry):
        for which in range(2):
            rows = slice(which * size, (which + 1) * size)
            out[device, rows] = chunks[jnp.bitwise_xor(device, table[which]), rows]
        return carry

    lax.fori_loop(0, chunks.shape[0], step, 0, unroll=8)


def exchange(packed, table):
    chunks = spread(packed.reshape(-1, 32, LANE))
    chunks = call(
        reroute_kernel,
        jax.ShapeDtypeStruct(chunks.shape, chunks.dtype),
        in_specs=[smem(), whole()],
        out_specs=whole(),
    )(table, chunks)
    return spread(chunks).reshape(packed.shape)


def arrived_rows(table, sub, which, half, arrived):
    second, both = flags(table, sub, which)
    inside = jnp.maximum(both, (second == half).astype(jnp.int32)).astype(jnp.float32)
    other = jnp.bitwise_xor(sub, table[2 + which])
    tiles = [
        arrived[other, half * both, :, which * 2 + lane].astype(jnp.float32).reshape(HALF, LANE)
        for lane in range(2)
    ]
    return jnp.concatenate(tiles, 1), inside


def weigh_kernel(table, residual, modes, arrived, base, weighted, payload, restricted, turned):
    sub = pl.program_id(0)
    for which in range(2):
        for half in range(2):
            start = (which * 2 + half) * HALF
            rows, inside = arrived_rows(table, sub, which, half, arrived)
            own = residual[0, start : start + HALF].astype(jnp.float32)
            value = (own + rows * inside) * (1.0 - 0.5 * inside)
            weighted[0, start : start + HALF] = value.astype(jnp.bfloat16)
    weighted[0, 4 * HALF :] = residual[0, 4 * HALF :]
    restricted[pl.ds(pl.multiple_of(sub * MODES, MODES), MODES)] = lax.dot_general(
        modes[0], weighted[0], (((1,), (0,)), ((), ())), preferred_element_type=jnp.float32
    )

    @pl.when(sub == pl.num_programs(0) - 1)
    def _():
        devices, rows, _ = payload.shape
        turned[: 2 * devices] = restricted[...].T
        turned[2 * devices :] = jnp.zeros((turned.shape[0] - 2 * devices, LANE), jnp.float32)
        own = lax.broadcasted_iota(jnp.int32, (rows, LANE), 0) < 2

        def step(device, carry):
            piece = turned[pl.ds(2 * device, rows)]
            rest = base[device].astype(jnp.float32)
            payload[device] = jnp.where(own, piece, rest).astype(jnp.bfloat16)
            return carry

        lax.fori_loop(0, devices, step, 0, unroll=8)


def prolong(modes, picked):
    return lax.dot_general(
        modes, picked, (((0,), (0,)), ((), ())), preferred_element_type=jnp.float32
    )


def finish_kernel(table, local, modes, arrived, arrived_modes, out, pairs, picked):
    sub = pl.program_id(0)

    @pl.when(sub == 0)
    def _():
        for first in range(4):
            for half in range(2):

                def step(piece, carry, first=first, half=half):
                    for inner in range(4):
                        tile = arrived[first, half, piece * 4 + inner, 4].astype(jnp.float32)
                        at = (first * 2 + half) * 32 + pl.multiple_of(piece * 8, 8) + inner * 2
                        for kind in range(3):
                            pairs[kind, pl.ds(at, 2)] = tile[kind * 2 : kind * 2 + 2]
                    return carry

                lax.fori_loop(0, 4, step, 0)
        for kind in range(3):
            picked[kind] = pairs[kind].T.reshape(picked.shape[1:]).astype(jnp.bfloat16)

    added = prolong(modes[0], picked[0, sub])
    for which in range(2):
        other = jnp.bitwise_xor(sub, table[2 + which])
        for half in range(2):
            start = (which * 2 + half) * HALF
            rows, inside = arrived_rows(table, sub, which, half, arrived)
            _, both = flags(table, sub, which)
            theirs = prolong(arrived_modes[which * 2 + half * both, other], picked[1 + which, other])
            theirs = (0.5 * (rows + theirs)).astype(jnp.bfloat16).astype(jnp.float32)
            own = local[0, start : start + HALF] + added[start : start + HALF]
            own = (own * (1.0 - 0.5 * inside)).astype(jnp.bfloat16).astype(jnp.float32)
            out[0, start : start + HALF] = (own + theirs * inside).astype(jnp.bfloat16)
    out[0, 4 * HALF :] = (local[0, 4 * HALF :] + added[4 * HALF :]).astype(jnp.bfloat16)


def scatter_kernel(table, received, out, total, staged):
    devices = received.shape[0]
    place = lax.broadcasted_iota(jnp.int32, (LANE, LANE), 0).astype(jnp.float32)
    total[...] = jnp.zeros_like(total)

    def step(block, carry):
        left, right = [], []
        for inner in range(GROUP):
            piece = received[block * GROUP + inner].astype(jnp.float32)
            high = place == piece[2:3]
            low = place == piece[3:4]
            left.append(
                jnp.concatenate(
                    [jnp.where(high, piece[0:1], 0.0), jnp.where(high, piece[1:2], 0.0)], 0
                ).astype(jnp.bfloat16)
            )
            right.append(jnp.where(low, 1.0, 0.0).astype(jnp.bfloat16))
        total[...] += lax.dot_general(
            jnp.concatenate(left, 1),
            jnp.concatenate(right, 1),
            (((1,), (1,)), ((), ())),
            preferred_element_type=jnp.float32,
        )
        return carry

    lax.fori_loop(0, devices // GROUP, step, 0)
    blocks, size, _ = staged.shape
    pieces = size // 2
    for block in range(blocks):
        for case in range(2):
            for piece in range(pieces):
                at = case * LANE + block * pieces + piece
                staged[block, piece * 2 + case : piece * 2 + case + 1] = total[at : at + 1]
    for block in range(blocks):
        value = staged[block].astype(jnp.bfloat16)

        def copies(row, carry, block=block, value=value):
            out[row * blocks + block, :size] = value
            return carry

        lax.fori_loop(0, devices // blocks, copies, 0, unroll=4)
    first = lax.broadcasted_iota(jnp.int32, (8, LANE), 0) < 6

    def forward(device, carry):
        pieces = [
            received[jnp.bitwise_xor(device, table[which])].astype(jnp.float32) for which in range(2)
        ]
        out[device, size:] = jnp.where(first, pieces[0], pieces[1]).astype(jnp.bfloat16)
        return carry

    lax.fori_loop(0, devices, forward, 0, unroll=4)


def product_kernel(
    placed, inverse, packed, out, their_modes, pairs, left, parts, own, written
):
    at_step = pl.program_id(0)
    groups = placed.shape[0] // 4
    tiles, steps = pairs.shape[0], parts.shape[0]

    @pl.when(at_step == 0)
    def _():
        def step(group, carry):
            for inner in range(4):
                rows = placed[group * 4 + inner, : 2 * tiles].astype(jnp.float32)
                at = pl.multiple_of(group * 8, 8) + 2 * inner
                for tile in range(tiles):
                    pairs[tile, pl.ds(at, 2)] = rows[2 * tile : 2 * tile + 2]
            return carry

        lax.fori_loop(0, groups, step, 0)
        for tile in range(tiles):
            left[:, tile * LANE : (tile + 1) * LANE] = pairs[tile].astype(jnp.bfloat16)

    @pl.when(at_step == 1)
    def _():
        def step(group, carry):
            for inner in range(8):
                row = pl.multiple_of(group * 8, 8) + inner
                tile = placed[row, 2 * tiles :].astype(jnp.float32)
                for kind in range(4):
                    pairs[kind, pl.ds(row, 1)] = tile[4 + kind : 5 + kind]
            return carry

        lax.fori_loop(0, placed.shape[0] // 8, step, 0)
        for kind in range(4):
            value = pairs[kind, : placed.shape[0]].astype(jnp.bfloat16)
            their_modes[kind] = value.reshape(their_modes.shape[1:])

    parts[at_step] = lax.dot_general(
        left[...], inverse[...], (((1,), (1,)), ((), ())), preferred_element_type=jnp.float32
    )

    @pl.when(at_step == steps - 1)
    def _():
        size = own.shape[1]

        def step(group, carry):
            at = pl.multiple_of(group * 8, 8)
            tall = [
                parts[part, pl.ds(at, 8), lane * LANE : (lane + 1) * LANE]
                for part in range(steps)
                for lane in range(parts.shape[2] // LANE)
            ]
            for inner in range(4):
                rows = jnp.concatenate([tile[2 * inner : 2 * inner + 2] for tile in tall], 0)
                own[group * 4 + inner] = rows.astype(jnp.bfloat16)
            return carry

        lax.fori_loop(0, groups, step, 0)
        copy = pltpu.make_async_copy(own, out.at[:, :size], written)
        copy.start()
        copy.wait()


def gather_kernel(table, received, partial, out, solved, chosen_rows, *, row_blocks):
    devices = received.shape[0]
    pieces = LANE // row_blocks
    col_blocks = devices // row_blocks
    for block in range(row_blocks):
        value = partial[block * col_blocks, : 2 * pieces].astype(jnp.float32)
        for col in range(1, col_blocks):
            value = value + partial[block * col_blocks + col, : 2 * pieces].astype(jnp.float32)
        for piece in range(pieces):
            for case in range(2):
                at = case * LANE + block * pieces + piece
                solved[at : at + 1] = value[2 * piece + case : 2 * piece + case + 1]
    turned = jnp.concatenate([solved[:LANE].T, solved[LANE:].T], 0).astype(jnp.bfloat16)
    place = lax.broadcasted_iota(jnp.int32, (LANE, LANE), 0).astype(jnp.float32)

    def step(block, carry):
        highs, lows = [], []
        for inner in range(GROUP):
            piece = received[block * GROUP + inner].astype(jnp.float32)
            highs.append(jnp.where(place == piece[2:3], 1.0, 0.0).astype(jnp.bfloat16))
            lows.append(place == piece[3:4])
        chosen = lax.dot_general(
            turned,
            jnp.concatenate(highs, 1),
            (((1,), (0,)), ((), ())),
            preferred_element_type=jnp.float32,
        )
        for inner in range(GROUP):
            lanes = slice(inner * LANE, (inner + 1) * LANE)
            both = [
                jnp.sum(
                    jnp.where(lows[inner], chosen[case * LANE : (case + 1) * LANE, lanes], 0.0),
                    axis=0,
                    keepdims=True,
                )
                for case in range(2)
            ]
            chosen_rows[block * GROUP + inner] = jnp.concatenate(both, 0)
        return carry

    lax.fori_loop(0, devices // GROUP, step, 0)

    size = (partial.shape[1] - 2 * pieces) // 2

    def share(device, carry):
        sources = [jnp.bitwise_xor(device, table[which]) for which in range(2)]
        for which in range(2):
            at = 2 * pieces + which * size
            out[device, which * size : (which + 1) * size] = partial[sources[which], at : at + size]
        rows = [chosen_rows[device], chosen_rows[sources[0]], chosen_rows[sources[1]]]
        rows.append(jnp.zeros_like(rows[0]))
        out[device, 2 * size :] = jnp.concatenate(rows, 0).astype(jnp.bfloat16)
        return carry

    lax.fori_loop(0, devices, share, 0, unroll=4)


def whole():
    return pl.BlockSpec(memory_space=pltpu.VMEM)


def per_sub(*shape):
    zeros = (0,) * len(shape)
    return pl.BlockSpec((1,) + shape, lambda sub: (sub,) + zeros)


def same(*shape):
    zeros = (0,) * len(shape)
    return pl.BlockSpec(shape, lambda sub: zeros)


def shards(
    residual,
    interface_inverse,
    modes,
    coarse_map,
    coarse_inverse,
    neighbours,
    block_sizes,
    block_offsets,
):
    count, trace_len, cases = residual.shape
    devices = cases // 2
    table = table_of(neighbours, block_sizes, block_offsets)
    field = jax.ShapeDtypeStruct(residual.shape, jnp.bfloat16)

    turned_modes = modes.transpose(0, 2, 1)
    offsets = block_offsets.T
    packed_shape = jax.ShapeDtypeStruct((count, 2, HALF // 8, 4, 8, LANE), jnp.bfloat16)

    tiles = residual.reshape(count, trace_len // 8, 8, 2, LANE).transpose(0, 1, 3, 2, 4)
    hbm = pl.BlockSpec(memory_space=pltpu.HBM)
    packed = call(
        pack_kernel,
        pltpu.HBM(packed_shape.shape, jnp.bfloat16),
        in_specs=[smem(), hbm],
        out_specs=hbm,
        scratch_shapes=[
            pltpu.VMEM((count * 4, HALF // 8, 2, 8, LANE), jnp.bfloat16),
            pltpu.SemaphoreType.DMA((count * 4,)),
            pltpu.SemaphoreType.DMA((count * 4,)),
        ],
    )(offsets, in_hbm(tiles))
    arrived = exchange(packed, table)
    digits = jnp.stack([coarse_map // LANE, coarse_map % LANE]).astype(jnp.bfloat16)
    digits = jnp.concatenate([jnp.zeros_like(digits), digits], 0)
    shared = turned_modes[:, :, : 4 * HALF].reshape(count, MODES, 2, 2, HALF)
    second = table[4:12].reshape(count, 1, 2, 1) == 1
    shared = jnp.stack(
        [jnp.where(second, shared[:, :, :, 1], shared[:, :, :, 0]), shared[:, :, :, 1]], 3
    ).reshape(devices, 4, HALF)
    base = jnp.concatenate([jnp.broadcast_to(digits[None], (devices,) + digits.shape), shared], 1)
    weighted, payload = call(
        weigh_kernel,
        (pltpu.HBM(residual.shape, jnp.bfloat16), jax.ShapeDtypeStruct(base.shape, jnp.bfloat16)),
        grid=(count,),
        in_specs=[
            smem(),
            per_sub(trace_len, cases),
            per_sub(MODES, trace_len),
            same(*arrived.shape),
            same(*base.shape),
        ],
        out_specs=(per_sub(trace_len, cases), same(*base.shape)),
        scratch_shapes=[
            pltpu.VMEM((count * MODES, cases), jnp.float32),
            pltpu.VMEM((cases + 8, LANE), jnp.float32),
        ],
    )(table, residual, turned_modes, arrived, in_hbm(base))
    received = spread(payload)
    weighted, received = lax.optimization_barrier((weighted, received))

    rows, columns = coarse_inverse.shape
    own_tiles = 2 * rows // LANE // 8
    local_part, packed = call(
        local_kernel,
        (
            pltpu.HBM(residual.shape, jnp.float32),
            pltpu.HBM((count, 2, HALF // 8, own_tiles + 4, 8, LANE), jnp.bfloat16),
        ),
        grid=(count,),
        in_specs=[smem(), per_sub(trace_len, trace_len), per_sub(trace_len, cases)],
        out_specs=(
            per_sub(trace_len, cases),
            per_sub(2, HALF // 8, own_tiles + 4, 8, LANE),
        ),
    )(offsets, in_hbm(interface_inverse), in_hbm(weighted))
    joined_shape = (devices, 8 * own_tiles + 32, LANE)
    packed = packed.reshape(joined_shape)

    placed = call(
        scatter_kernel,
        jax.ShapeDtypeStruct((devices, 2 * columns // LANE + 8, LANE), jnp.bfloat16),
        in_specs=[smem(), whole()],
        out_specs=whole(),
        scratch_shapes=[
            pltpu.VMEM((2 * LANE, LANE), jnp.float32),
            pltpu.VMEM((LANE * LANE // columns, 2 * columns // LANE, LANE), jnp.float32),
        ],
    )(table, received)
    placed = spread(placed)
    steps = 4
    modes_shape = (4, count, MODES, HALF)
    joined, their_modes = call(
        product_kernel,
        (
            pltpu.HBM(joined_shape, jnp.bfloat16),
            jax.ShapeDtypeStruct(modes_shape, jnp.bfloat16),
        ),
        grid=(steps,),
        in_specs=[
            same(*placed.shape),
            pl.BlockSpec((rows // steps, columns), lambda step: (step, 0)),
            hbm,
        ],
        out_specs=(hbm, same(*modes_shape)),
        input_output_aliases={2: 0},
        scratch_shapes=[
            pltpu.VMEM((columns // LANE, cases, LANE), jnp.float32),
            pltpu.VMEM((cases, columns), jnp.bfloat16),
            pltpu.VMEM((steps, cases, rows // steps), jnp.float32),
            pltpu.VMEM((devices, 8 * own_tiles, LANE), jnp.bfloat16),
            pltpu.SemaphoreType.DMA(()),
        ],
    )(placed, in_hbm(coarse_inverse), in_hbm(packed))
    joined = spread(joined)
    last = call(
        functools.partial(gather_kernel, row_blocks=lax.axis_size("row")),
        jax.ShapeDtypeStruct((devices, 40, LANE), jnp.bfloat16),
        in_specs=[smem(), whole(), whole()],
        out_specs=whole(),
        scratch_shapes=[
            pltpu.VMEM((2 * LANE, LANE), jnp.float32),
            pltpu.VMEM((devices, 2, LANE), jnp.float32),
        ],
    )(table, received, joined)
    last = spread(last).reshape(count, 2, HALF // 8, 5, 8, LANE)
    return call(
        finish_kernel,
        field,
        grid=(count,),
        in_specs=[
            smem(),
            per_sub(trace_len, cases),
            per_sub(MODES, trace_len),
            same(*last.shape),
            same(*modes_shape),
        ],
        out_specs=per_sub(trace_len, cases),
        scratch_shapes=[
            pltpu.VMEM((3, cases, LANE), jnp.float32),
            pltpu.VMEM((3, count, MODES, cases), jnp.bfloat16),
        ],
    )(table, in_hbm(local_part), turned_modes, last, their_modes)


def solution(mesh):
    return jax.shard_map(
        shards,
        mesh=mesh,
        in_specs=(
            P(AXES, None, None),
            P(AXES, None, None),
            P(AXES, None, None),
            P(AXES),
            P("row", "col"),
            P(AXES, None),
            P(AXES, None),
            P(AXES, None),
        ),
        out_specs=P(AXES, None, None),
        check_vma=False,
    )
```

```python
import functools

import jax
import jax.numpy as jnp
from jax import lax
from jax.experimental import pallas as pl
from jax.experimental.pallas import tpu as pltpu
from jax.sharding import PartitionSpec as P

AXES = ("row", "col")
MODES = 32
HALF = 128
LANE = 128
GROUP = 128
SUBS = 2
VMEM_LIMIT = 16 * 1024 * 1024


def spread(value):
    return lax.all_to_all(value, AXES, 0, 0, tiled=True)


def call(kernel, out_shape, **kw):
    return pl.pallas_call(
        kernel,
        out_shape=out_shape,
        compiler_params=pltpu.CompilerParams(vmem_limit_bytes=VMEM_LIMIT),
        **kw,
    )


def in_hbm(value):
    return pltpu.with_memory_space_constraint(value, pltpu.HBM)


def smem():
    return pl.BlockSpec(memory_space=pltpu.SMEM)


def table_of(neighbours, block_sizes, block_offsets):
    count = neighbours.shape[0]
    own = lax.axis_index(AXES).astype(jnp.int32)
    device_mask = jnp.bitwise_xor(neighbours[0] // count, own)
    inner_mask = neighbours[0] % count
    second = (block_offsets // HALF) % 2
    both = block_sizes // HALF - 1
    return jnp.concatenate([device_mask, inner_mask, second.reshape(-1), both.reshape(-1)]).astype(
        jnp.int32
    )


def flags(table, sub, which):
    return table[4 + sub * 2 + which], table[12 + sub * 2 + which]


def store_blocks(offsets, sub, load, packed):
    for which in range(2):
        second = jnp.bitwise_and(jnp.right_shift(offsets[which, sub], 7), 1)
        for half in range(2):
            start = which * 2 * HALF + (second * HALF if half == 0 else HALF)
            rows = load(pl.multiple_of(start, HALF)).astype(jnp.float32)
            for lane in range(2):
                tile = rows[:, lane * LANE : (lane + 1) * LANE].reshape(HALF // 8, 8, LANE)
                packed[0, half, :, which * 2 + lane] = tile.astype(jnp.bfloat16)


def pack_kernel(offsets, tiles, packed, staged, read, written):
    size = HALF // 8
    reads, writes = [], []
    for sub in range(tiles.shape[0]):
        for which in range(2):
            second = jnp.bitwise_and(jnp.right_shift(offsets[which, sub], 7), 1)
            for half in range(2):
                start = which * 2 * size + (second * size if half == 0 else size)
                at = (sub * 2 + which) * 2 + half
                reads.append(
                    pltpu.make_async_copy(
                        tiles.at[sub, pl.ds(start, size)], staged.at[at], read.at[at]
                    )
                )
                reads[-1].start()
                writes.append(
                    pltpu.make_async_copy(
                        staged.at[at],
                        packed.at[sub, half, :, pl.ds(which * 2, 2)],
                        written.at[at],
                    )
                )
    for first, second in zip(reads, writes):
        first.wait()
        second.start()
    for copy in writes:
        copy.wait()


def local_kernel(offsets, inverse, weighted, local, packed):
    local[0] = jnp.dot(inverse[0], weighted[0], preferred_element_type=jnp.float32)
    store_blocks(offsets, pl.program_id(0), lambda start: local[0, pl.ds(start, HALF)], packed)


def reroute_kernel(table, chunks, out):
    size = chunks.shape[1] // 2

    def step(device, carry):
        for which in range(2):
            rows = slice(which * size, (which + 1) * size)
            out[device, rows] = chunks[jnp.bitwise_xor(device, table[which]), rows]
        return carry

    lax.fori_loop(0, chunks.shape[0], step, 0, unroll=8)


def exchange(packed, table, early):
    chunks = spread(packed.reshape(-1, 32, LANE))
    chunks, early = lax.optimization_barrier((chunks, early))
    chunks = call(
        reroute_kernel,
        jax.ShapeDtypeStruct(chunks.shape, chunks.dtype),
        in_specs=[smem(), whole()],
        out_specs=whole(),
    )(table, chunks)
    return spread(chunks).reshape(packed.shape), early


def arrived_rows(table, sub, which, half, arrived):
    second, both = flags(table, sub, which)
    inside = jnp.maximum(both, (second == half).astype(jnp.int32)).astype(jnp.float32)
    other = jnp.bitwise_xor(sub, table[2 + which])
    tiles = [
        arrived[other, half * both, :, which * 2 + lane].astype(jnp.float32).reshape(HALF, LANE)
        for lane in range(2)
    ]
    return jnp.concatenate(tiles, 1), inside


def weigh_kernel(table, residual, modes, arrived, base, weighted, payload, restricted, turned):
    step_at = pl.program_id(0)
    subs = residual.shape[0]
    for at in range(subs):
        sub = step_at * subs + at
        for which in range(2):
            for half in range(2):
                start = (which * 2 + half) * HALF
                rows, inside = arrived_rows(table, sub, which, half, arrived)
                own = residual[at, start : start + HALF].astype(jnp.float32)
                value = (own + rows * inside) * (1.0 - 0.5 * inside)
                weighted[at, start : start + HALF] = value.astype(jnp.bfloat16)
        weighted[at, 4 * HALF :] = residual[at, 4 * HALF :]
        restricted[pl.ds(pl.multiple_of(sub * MODES, MODES), MODES)] = lax.dot_general(
            modes[at], weighted[at], (((1,), (0,)), ((), ())), preferred_element_type=jnp.float32
        )

    @pl.when(step_at == pl.num_programs(0) - 1)
    def _():
        devices, rows, _ = payload.shape
        turned[: 2 * devices] = restricted[...].T
        turned[2 * devices :] = jnp.zeros((turned.shape[0] - 2 * devices, LANE), jnp.float32)
        own = lax.broadcasted_iota(jnp.int32, (rows, LANE), 0) < 2

        def step(device, carry):
            piece = turned[pl.ds(2 * device, rows)]
            rest = base[device].astype(jnp.float32)
            payload[device] = jnp.where(own, piece, rest).astype(jnp.bfloat16)
            return carry

        lax.fori_loop(0, devices, step, 0, unroll=8)


def prolong(modes, picked):
    return lax.dot_general(
        modes, picked, (((0,), (0,)), ((), ())), preferred_element_type=jnp.float32
    )


def finish_kernel(table, local, modes, arrived, their_modes, out, pairs, picked):
    step_at = pl.program_id(0)
    subs = local.shape[0]

    @pl.when(step_at == 0)
    def _():
        for first in range(4):
            for half in range(2):

                def step(piece, carry, first=first, half=half):
                    for inner in range(4):
                        tile = arrived[first, half, piece * 4 + inner, 4].astype(jnp.float32)
                        at = (first * 2 + half) * 32 + pl.multiple_of(piece * 8, 8) + inner * 2
                        for kind in range(3):
                            pairs[kind, pl.ds(at, 2)] = tile[kind * 2 : kind * 2 + 2]
                    return carry

                lax.fori_loop(0, 4, step, 0)
        for kind in range(3):
            picked[kind] = pairs[kind].T.reshape(picked.shape[1:]).astype(jnp.bfloat16)

    for at in range(subs):
        sub = step_at * subs + at
        added = prolong(modes[at], picked[0, sub])
        for which in range(2):
            other = jnp.bitwise_xor(sub, table[2 + which])
            for half in range(2):
                start = (which * 2 + half) * HALF
                rows, inside = arrived_rows(table, sub, which, half, arrived)
                _, both = flags(table, sub, which)
                theirs = prolong(their_modes[which * 2 + half * both, other], picked[1 + which, other])
                theirs = (0.5 * (rows + theirs)).astype(jnp.bfloat16).astype(jnp.float32)
                own = local[at, start : start + HALF] + added[start : start + HALF]
                own = (own * (1.0 - 0.5 * inside)).astype(jnp.bfloat16).astype(jnp.float32)
                out[at, start : start + HALF] = (own + theirs * inside).astype(jnp.bfloat16)
        out[at, 4 * HALF :] = (local[at, 4 * HALF :] + added[4 * HALF :]).astype(jnp.bfloat16)


def scatter_kernel(table, received, out, total, staged):
    devices = received.shape[0]
    place = lax.broadcasted_iota(jnp.int32, (LANE, LANE), 0).astype(jnp.float32)
    total[...] = jnp.zeros_like(total)

    def step(block, carry):
        left, right = [], []
        for inner in range(GROUP):
            piece = received[block * GROUP + inner].astype(jnp.float32)
            high = place == piece[2:3]
            low = place == piece[3:4]
            left.append(
                jnp.concatenate(
                    [jnp.where(high, piece[0:1], 0.0), jnp.where(high, piece[1:2], 0.0)], 0
                ).astype(jnp.bfloat16)
            )
            right.append(jnp.where(low, 1.0, 0.0).astype(jnp.bfloat16))
        total[...] += lax.dot_general(
            jnp.concatenate(left, 1),
            jnp.concatenate(right, 1),
            (((1,), (1,)), ((), ())),
            preferred_element_type=jnp.float32,
        )
        return carry

    lax.fori_loop(0, devices // GROUP, step, 0)
    blocks, size, _ = staged.shape
    pieces = size // 2
    for block in range(blocks):
        for case in range(2):
            for piece in range(pieces):
                at = case * LANE + block * pieces + piece
                staged[block, piece * 2 + case : piece * 2 + case + 1] = total[at : at + 1]
    for block in range(blocks):
        value = staged[block].astype(jnp.bfloat16)

        def copies(row, carry, block=block, value=value):
            out[row * blocks + block, :size] = value
            return carry

        lax.fori_loop(0, devices // blocks, copies, 0, unroll=4)
    first = lax.broadcasted_iota(jnp.int32, (8, LANE), 0) < 6

    def forward(device, carry):
        pieces = [
            received[jnp.bitwise_xor(device, table[which])].astype(jnp.float32) for which in range(2)
        ]
        out[device, size:] = jnp.where(first, pieces[0], pieces[1]).astype(jnp.bfloat16)
        return carry

    lax.fori_loop(0, devices, forward, 0, unroll=4)


def product_kernel(placed, inverse, packed, out, their_modes, pairs, left, parts):
    at_step = pl.program_id(0)
    groups = placed.shape[0] // 4
    tiles, steps = pairs.shape[0], parts.shape[0]

    @pl.when(at_step == 0)
    def _():
        def step(group, carry):
            rows = [placed[group * 4 + inner, : 2 * tiles].astype(jnp.float32) for inner in range(4)]
            at = pl.multiple_of(group * 8, 8)
            for tile in range(tiles):
                taken = [piece[2 * tile : 2 * tile + 2] for piece in rows]
                pairs[tile, pl.ds(at, 8)] = jnp.concatenate(taken, 0)
            return carry

        lax.fori_loop(0, groups, step, 0)
        for tile in range(tiles):
            left[:, tile * LANE : (tile + 1) * LANE] = pairs[tile].astype(jnp.bfloat16)

    @pl.when(at_step == 1)
    def _():
        def step(group, carry):
            for inner in range(8):
                row = pl.multiple_of(group * 8, 8) + inner
                tile = placed[row, 2 * tiles :].astype(jnp.float32)
                for kind in range(4):
                    pairs[kind, pl.ds(row, 1)] = tile[4 + kind : 5 + kind]
            return carry

        lax.fori_loop(0, placed.shape[0] // 8, step, 0)
        for kind in range(4):
            value = pairs[kind, : placed.shape[0]].astype(jnp.bfloat16)
            their_modes[kind] = value.reshape(their_modes.shape[1:])

    parts[at_step] = lax.dot_general(
        left[...], inverse[...], (((1,), (1,)), ((), ())), preferred_element_type=jnp.float32
    )

    @pl.when(at_step == steps - 1)
    def _():
        size = steps * parts.shape[2] // LANE * 2

        def step(group, carry):
            at = pl.multiple_of(group * 8, 8)
            tall = [
                parts[part, pl.ds(at, 8), lane * LANE : (lane + 1) * LANE]
                for part in range(steps)
                for lane in range(parts.shape[2] // LANE)
            ]
            for inner in range(4):
                rows = jnp.concatenate([tile[2 * inner : 2 * inner + 2] for tile in tall], 0)
                out[group * 4 + inner, :size] = rows.astype(jnp.bfloat16)
                out[group * 4 + inner, size:] = packed[group * 4 + inner]
            return carry

        lax.fori_loop(0, groups, step, 0)


def gather_kernel(table, received, partial, out, solved, chosen_rows, *, row_blocks):
    devices = received.shape[0]
    pieces = LANE // row_blocks
    col_blocks = devices // row_blocks
    for block in range(row_blocks):
        value = partial[block * col_blocks, : 2 * pieces].astype(jnp.float32)
        for col in range(1, col_blocks):
            value = value + partial[block * col_blocks + col, : 2 * pieces].astype(jnp.float32)
        for piece in range(pieces):
            for case in range(2):
                at = case * LANE + block * pieces + piece
                solved[at : at + 1] = value[2 * piece + case : 2 * piece + case + 1]
    turned = jnp.concatenate([solved[:LANE].T, solved[LANE:].T], 0).astype(jnp.bfloat16)
    place = lax.broadcasted_iota(jnp.int32, (LANE, LANE), 0).astype(jnp.float32)

    def step(block, carry):
        highs, lows = [], []
        for inner in range(GROUP):
            piece = received[block * GROUP + inner].astype(jnp.float32)
            highs.append(jnp.where(place == piece[2:3], 1.0, 0.0).astype(jnp.bfloat16))
            lows.append(place == piece[3:4])
        chosen = lax.dot_general(
            turned,
            jnp.concatenate(highs, 1),
            (((1,), (0,)), ((), ())),
            preferred_element_type=jnp.float32,
        )
        for inner in range(GROUP):
            lanes = slice(inner * LANE, (inner + 1) * LANE)
            both = [
                jnp.sum(
                    jnp.where(lows[inner], chosen[case * LANE : (case + 1) * LANE, lanes], 0.0),
                    axis=0,
                    keepdims=True,
                )
                for case in range(2)
            ]
            chosen_rows[block * GROUP + inner] = jnp.concatenate(both, 0)
        return carry

    lax.fori_loop(0, devices // GROUP, step, 0)

    size = (partial.shape[1] - 2 * pieces) // 2

    def share(device, carry):
        sources = [jnp.bitwise_xor(device, table[which]) for which in range(2)]
        for which in range(2):
            at = 2 * pieces + which * size
            out[device, which * size : (which + 1) * size] = partial[sources[which], at : at + size]
        rows = [chosen_rows[device], chosen_rows[sources[0]], chosen_rows[sources[1]]]
        rows.append(jnp.zeros_like(rows[0]))
        out[device, 2 * size :] = jnp.concatenate(rows, 0).astype(jnp.bfloat16)
        return carry

    lax.fori_loop(0, devices, share, 0, unroll=4)


def whole():
    return pl.BlockSpec(memory_space=pltpu.VMEM)


def per_sub(*shape, subs=1):
    zeros = (0,) * len(shape)
    return pl.BlockSpec((subs,) + shape, lambda step: (step,) + zeros)


def same(*shape):
    zeros = (0,) * len(shape)
    return pl.BlockSpec(shape, lambda sub: zeros)


def shards(
    residual,
    interface_inverse,
    modes,
    coarse_map,
    coarse_inverse,
    neighbours,
    block_sizes,
    block_offsets,
):
    count, trace_len, cases = residual.shape
    devices = cases // 2
    table = table_of(neighbours, block_sizes, block_offsets)
    field = jax.ShapeDtypeStruct(residual.shape, jnp.bfloat16)

    turned_modes = modes.transpose(0, 2, 1)
    offsets = block_offsets.T
    packed_shape = jax.ShapeDtypeStruct((count, 2, HALF // 8, 4, 8, LANE), jnp.bfloat16)

    tiles = residual.reshape(count, trace_len // 8, 8, 2, LANE).transpose(0, 1, 3, 2, 4)
    hbm = pl.BlockSpec(memory_space=pltpu.HBM)
    packed = call(
        pack_kernel,
        pltpu.HBM(packed_shape.shape, jnp.bfloat16),
        in_specs=[smem(), hbm],
        out_specs=hbm,
        scratch_shapes=[
            pltpu.VMEM((count * 4, HALF // 8, 2, 8, LANE), jnp.bfloat16),
            pltpu.SemaphoreType.DMA((count * 4,)),
            pltpu.SemaphoreType.DMA((count * 4,)),
        ],
    )(offsets, in_hbm(tiles))
    digits = jnp.stack([coarse_map // LANE, coarse_map % LANE]).astype(jnp.bfloat16)
    digits = jnp.concatenate([jnp.zeros_like(digits), digits], 0)
    shared = turned_modes[:, :, : 4 * HALF].reshape(count, MODES, 2, 2, HALF)
    second = table[4:12].reshape(count, 1, 2, 1) == 1
    shared = jnp.stack(
        [jnp.where(second, shared[:, :, :, 1], shared[:, :, :, 0]), shared[:, :, :, 1]], 3
    ).reshape(devices, 4, HALF)
    base = jnp.concatenate([jnp.broadcast_to(digits[None], (devices,) + digits.shape), shared], 1)
    arrived, base = exchange(packed, table, base)
    weighted, payload = call(
        weigh_kernel,
        (pltpu.HBM(residual.shape, jnp.bfloat16), jax.ShapeDtypeStruct(base.shape, jnp.bfloat16)),
        grid=(count // SUBS,),
        in_specs=[
            smem(),
            per_sub(trace_len, cases, subs=SUBS),
            per_sub(MODES, trace_len, subs=SUBS),
            same(*arrived.shape),
            same(*base.shape),
        ],
        out_specs=(per_sub(trace_len, cases, subs=SUBS), same(*base.shape)),
        scratch_shapes=[
            pltpu.VMEM((count * MODES, cases), jnp.float32),
            pltpu.VMEM((cases + 8, LANE), jnp.float32),
        ],
    )(table, residual, turned_modes, arrived, base)
    received = spread(payload)
    weighted, received = lax.optimization_barrier((weighted, received))

    local_part, packed = call(
        local_kernel,
        (
            pltpu.HBM(residual.shape, jnp.float32),
            pltpu.HBM(packed_shape.shape, jnp.bfloat16),
        ),
        grid=(count,),
        in_specs=[smem(), per_sub(trace_len, trace_len), per_sub(trace_len, cases)],
        out_specs=(per_sub(trace_len, cases), per_sub(*packed_shape.shape[1:])),
    )(offsets, in_hbm(interface_inverse), in_hbm(weighted))
    packed = packed.reshape(devices, 32, LANE)

    rows, columns = coarse_inverse.shape
    placed = call(
        scatter_kernel,
        jax.ShapeDtypeStruct((devices, 2 * columns // LANE + 8, LANE), jnp.bfloat16),
        in_specs=[smem(), whole()],
        out_specs=whole(),
        scratch_shapes=[
            pltpu.VMEM((2 * LANE, LANE), jnp.float32),
            pltpu.VMEM((LANE * LANE // columns, 2 * columns // LANE, LANE), jnp.float32),
        ],
    )(table, received)
    placed = spread(placed)
    steps = 2
    joined_shape = (devices, 2 * rows // LANE + 32, LANE)
    modes_shape = (4, count, MODES, HALF)
    joined, their_modes = call(
        product_kernel,
        (
            jax.ShapeDtypeStruct(joined_shape, jnp.bfloat16),
            jax.ShapeDtypeStruct(modes_shape, jnp.bfloat16),
        ),
        grid=(steps,),
        in_specs=[
            same(*placed.shape),
            pl.BlockSpec((rows // steps, columns), lambda step: (step, 0)),
            same(*packed.shape),
        ],
        out_specs=(same(*joined_shape), same(*modes_shape)),
        scratch_shapes=[
            pltpu.VMEM((columns // LANE, cases, LANE), jnp.float32),
            pltpu.VMEM((cases, columns), jnp.bfloat16),
            pltpu.VMEM((steps, cases, rows // steps), jnp.float32),
        ],
    )(placed, in_hbm(coarse_inverse), in_hbm(packed))
    joined = spread(joined)
    last = call(
        functools.partial(gather_kernel, row_blocks=lax.axis_size("row")),
        jax.ShapeDtypeStruct((devices, 40, LANE), jnp.bfloat16),
        in_specs=[smem(), whole(), whole()],
        out_specs=whole(),
        scratch_shapes=[
            pltpu.VMEM((2 * LANE, LANE), jnp.float32),
            pltpu.VMEM((devices, 2, LANE), jnp.float32),
        ],
    )(table, received, joined)
    last = spread(last).reshape(count, 2, HALF // 8, 5, 8, LANE)
    return call(
        finish_kernel,
        field,
        grid=(count // SUBS,),
        in_specs=[
            smem(),
            per_sub(trace_len, cases, subs=SUBS),
            per_sub(MODES, trace_len, subs=SUBS),
            same(*last.shape),
            same(*modes_shape),
        ],
        out_specs=per_sub(trace_len, cases, subs=SUBS),
        scratch_shapes=[
            pltpu.VMEM((3, cases, LANE), jnp.float32),
            pltpu.VMEM((3, count, MODES, cases), jnp.bfloat16),
        ],
    )(table, in_hbm(local_part), turned_modes, last, their_modes)


def solution(mesh):
    return jax.shard_map(
        shards,
        mesh=mesh,
        in_specs=(
            P(AXES, None, None),
            P(AXES, None, None),
            P(AXES, None, None),
            P(AXES),
            P("row", "col"),
            P(AXES, None),
            P(AXES, None),
            P(AXES, None),
        ),
        out_specs=P(AXES, None, None),
        check_vma=False,
    )
```

```python
import functools

import jax
import jax.numpy as jnp
from jax import lax
from jax.experimental import pallas as pl
from jax.experimental.pallas import tpu as pltpu
from jax.sharding import PartitionSpec as P

AXES = ("row", "col")
MODES = 32
HALF = 128
LANE = 128
GROUP = 128
SUBS = 2
VMEM_LIMIT = 16 * 1024 * 1024


def spread(value):
    return lax.all_to_all(value, AXES, 0, 0, tiled=True)


def call(kernel, out_shape, **kw):
    return pl.pallas_call(
        kernel,
        out_shape=out_shape,
        compiler_params=pltpu.CompilerParams(vmem_limit_bytes=VMEM_LIMIT),
        **kw,
    )


def in_hbm(value):
    return pltpu.with_memory_space_constraint(value, pltpu.HBM)


def smem():
    return pl.BlockSpec(memory_space=pltpu.SMEM)


def table_of(neighbours, block_sizes, block_offsets):
    count = neighbours.shape[0]
    own = lax.axis_index(AXES).astype(jnp.int32)
    device_mask = jnp.bitwise_xor(neighbours[0] // count, own)
    inner_mask = neighbours[0] % count
    second = (block_offsets // HALF) % 2
    both = block_sizes // HALF - 1
    return jnp.concatenate([device_mask, inner_mask, second.reshape(-1), both.reshape(-1)]).astype(
        jnp.int32
    )


def flags(table, sub, which):
    return table[4 + sub * 2 + which], table[12 + sub * 2 + which]


def store_blocks(offsets, sub, load, packed):
    for which in range(2):
        second = jnp.bitwise_and(jnp.right_shift(offsets[which, sub], 7), 1)
        for half in range(2):
            start = which * 2 * HALF + (second * HALF if half == 0 else HALF)
            rows = load(pl.multiple_of(start, HALF)).astype(jnp.float32)
            for lane in range(2):
                tile = rows[:, lane * LANE : (lane + 1) * LANE].reshape(HALF // 8, 8, LANE)
                packed[0, half, :, which * 2 + lane] = tile.astype(jnp.bfloat16)


def pack_kernel(offsets, tiles, packed, staged, read, written):
    size = HALF // 8
    reads, writes = [], []
    for sub in range(tiles.shape[0]):
        for which in range(2):
            second = jnp.bitwise_and(jnp.right_shift(offsets[which, sub], 7), 1)
            for half in range(2):
                start = which * 2 * size + (second * size if half == 0 else size)
                at = (sub * 2 + which) * 2 + half
                reads.append(
                    pltpu.make_async_copy(
                        tiles.at[sub, pl.ds(start, size)], staged.at[at], read.at[at]
                    )
                )
                reads[-1].start()
                writes.append(
                    pltpu.make_async_copy(
                        staged.at[at],
                        packed.at[sub, half, :, pl.ds(which * 2, 2)],
                        written.at[at],
                    )
                )
    for first, second in zip(reads, writes):
        first.wait()
        second.start()
    for copy in writes:
        copy.wait()


def local_kernel(offsets, inverse, weighted, local, packed):
    local[0] = jnp.dot(inverse[0], weighted[0], preferred_element_type=jnp.float32)
    store_blocks(offsets, pl.program_id(0), lambda start: local[0, pl.ds(start, HALF)], packed)


def reroute_kernel(table, chunks, out):
    size = chunks.shape[1] // 2

    def step(device, carry):
        for which in range(2):
            rows = slice(which * size, (which + 1) * size)
            out[device, rows] = chunks[jnp.bitwise_xor(device, table[which]), rows]
        return carry

    lax.fori_loop(0, chunks.shape[0], step, 0, unroll=8)


def exchange(packed, table, early):
    chunks = spread(packed.reshape(-1, 32, LANE))
    chunks, early = lax.optimization_barrier((chunks, early))
    chunks = call(
        reroute_kernel,
        jax.ShapeDtypeStruct(chunks.shape, chunks.dtype),
        in_specs=[smem(), whole()],
        out_specs=whole(),
    )(table, chunks)
    return spread(chunks).reshape(packed.shape), early


def arrived_rows(table, sub, which, half, arrived):
    second, both = flags(table, sub, which)
    inside = jnp.maximum(both, (second == half).astype(jnp.int32)).astype(jnp.float32)
    other = jnp.bitwise_xor(sub, table[2 + which])
    tiles = [
        arrived[other, half * both, :, which * 2 + lane].astype(jnp.float32).reshape(HALF, LANE)
        for lane in range(2)
    ]
    return jnp.concatenate(tiles, 1), inside


def weigh_kernel(table, residual, modes, arrived, base, weighted, payload, restricted, turned):
    step_at = pl.program_id(0)
    subs = residual.shape[0]
    for at in range(subs):
        sub = step_at * subs + at
        for which in range(2):
            for half in range(2):
                start = (which * 2 + half) * HALF
                rows, inside = arrived_rows(table, sub, which, half, arrived)
                own = residual[at, start : start + HALF].astype(jnp.float32)
                value = (own + rows * inside) * (1.0 - 0.5 * inside)
                weighted[at, start : start + HALF] = value.astype(jnp.bfloat16)
        weighted[at, 4 * HALF :] = residual[at, 4 * HALF :]
        restricted[pl.ds(pl.multiple_of(sub * MODES, MODES), MODES)] = lax.dot_general(
            modes[at], weighted[at], (((1,), (0,)), ((), ())), preferred_element_type=jnp.float32
        )

    @pl.when(step_at == pl.num_programs(0) - 1)
    def _():
        devices, rows, _ = payload.shape
        turned[: 2 * devices] = restricted[...].T
        turned[2 * devices :] = jnp.zeros((turned.shape[0] - 2 * devices, LANE), jnp.float32)
        own = lax.broadcasted_iota(jnp.int32, (rows, LANE), 0) < 2

        def step(device, carry):
            piece = turned[pl.ds(2 * device, rows)]
            rest = base[device].astype(jnp.float32)
            payload[device] = jnp.where(own, piece, rest).astype(jnp.bfloat16)
            return carry

        lax.fori_loop(0, devices, step, 0, unroll=8)


def prolong(modes, picked):
    return lax.dot_general(
        modes, picked, (((0,), (0,)), ((), ())), preferred_element_type=jnp.float32
    )


def finish_kernel(
    table, local, modes, arrived, their_modes, out, pairs, picked, taken, given, read, sent
):
    subs = local.shape[0]
    loads, leaves = (
        [pltpu.make_async_copy(source.at[sub], target.at[sub], done.at[sub]) for sub in range(subs)]
        for source, target, done in ((local, taken, read), (given, out, sent))
    )
    for load in loads:
        load.start()

    for first in range(4):
        for half in range(2):

            def step(piece, carry, first=first, half=half):
                for inner in range(4):
                    tile = arrived[first, half, piece * 4 + inner, 4].astype(jnp.float32)
                    at = (first * 2 + half) * 32 + pl.multiple_of(piece * 8, 8) + inner * 2
                    for kind in range(3):
                        pairs[kind, pl.ds(at, 2)] = tile[kind * 2 : kind * 2 + 2]
                return carry

            lax.fori_loop(0, 4, step, 0)
    for kind in range(3):
        picked[kind] = pairs[kind].T.reshape(picked.shape[1:]).astype(jnp.bfloat16)

    for sub in range(subs):
        loads[sub].wait()
        added = prolong(modes[sub], picked[0, sub])
        for which in range(2):
            other = jnp.bitwise_xor(sub, table[2 + which])
            for half in range(2):
                start = (which * 2 + half) * HALF
                rows, inside = arrived_rows(table, sub, which, half, arrived)
                _, both = flags(table, sub, which)
                theirs = prolong(their_modes[which * 2 + half * both, other], picked[1 + which, other])
                theirs = (0.5 * (rows + theirs)).astype(jnp.bfloat16).astype(jnp.float32)
                own = taken[sub, start : start + HALF] + added[start : start + HALF]
                own = (own * (1.0 - 0.5 * inside)).astype(jnp.bfloat16).astype(jnp.float32)
                given[sub, start : start + HALF] = (own + theirs * inside).astype(jnp.bfloat16)
        given[sub, 4 * HALF :] = (taken[sub, 4 * HALF :] + added[4 * HALF :]).astype(jnp.bfloat16)
        leaves[sub].start()
    for leave in leaves:
        leave.wait()


def scatter_kernel(table, received, out, total, staged, ready, shared, sent, shared_sent):
    devices = received.shape[0]
    place = lax.broadcasted_iota(jnp.int32, (LANE, LANE), 0).astype(jnp.float32)
    first = lax.broadcasted_iota(jnp.int32, (8, LANE), 0) < 6

    def forward(device, carry):
        pieces = [
            received[jnp.bitwise_xor(device, table[which])].astype(jnp.float32) for which in range(2)
        ]
        shared[device] = jnp.where(first, pieces[0], pieces[1]).astype(jnp.bfloat16)
        return carry

    lax.fori_loop(0, devices, forward, 0, unroll=4)
    shares = pltpu.make_async_copy(shared, out.at[:, pl.ds(staged.shape[1], 8)], shared_sent)
    shares.start()
    total[...] = jnp.zeros_like(total)

    def step(block, carry):
        left, right = [], []
        for inner in range(GROUP):
            piece = received[block * GROUP + inner].astype(jnp.float32)
            high = place == piece[2:3]
            low = place == piece[3:4]
            left.append(
                jnp.concatenate(
                    [jnp.where(high, piece[0:1], 0.0), jnp.where(high, piece[1:2], 0.0)], 0
                ).astype(jnp.bfloat16)
            )
            right.append(jnp.where(low, 1.0, 0.0).astype(jnp.bfloat16))
        total[...] += lax.dot_general(
            jnp.concatenate(left, 1),
            jnp.concatenate(right, 1),
            (((1,), (1,)), ((), ())),
            preferred_element_type=jnp.float32,
        )
        return carry

    lax.fori_loop(0, devices // GROUP, step, 0)
    blocks, size, _ = staged.shape
    pieces = size // 2
    for block in range(blocks):
        for case in range(2):
            for piece in range(pieces):
                at = case * LANE + block * pieces + piece
                staged[block, piece * 2 + case : piece * 2 + case + 1] = total[at : at + 1]
    ready[...] = staged[...].astype(jnp.bfloat16)
    copies = [
        pltpu.make_async_copy(
            ready, out.at[pl.ds(row * blocks, blocks), pl.ds(0, size)], sent.at[row]
        )
        for row in range(devices // blocks)
    ]
    for copy in copies:
        copy.start()
    for copy in copies:
        copy.wait()
    shares.wait()


def product_kernel(
    placed, inverse, packed, out, their_modes, pairs, left, parts, blocks, read, sent
):
    groups = placed.shape[0] // 4
    tiles, steps = pairs.shape[0], parts.shape[0]
    size = out.shape[1] - packed.shape[1]
    taken = inverse.shape[0] // steps
    loads = [
        pltpu.make_async_copy(inverse.at[pl.ds(step * taken, taken)], blocks.at[step], read.at[step])
        for step in range(steps)
    ]
    for load in loads:
        load.start()
    chunks = pltpu.make_async_copy(packed, out.at[:, pl.ds(size, packed.shape[1])], sent)
    chunks.start()

    def order(group, carry):
        rows = [placed[group * 4 + inner, : 2 * tiles].astype(jnp.float32) for inner in range(4)]
        at = pl.multiple_of(group * 8, 8)
        for tile in range(tiles):
            piece = [row[2 * tile : 2 * tile + 2] for row in rows]
            pairs[tile, pl.ds(at, 8)] = jnp.concatenate(piece, 0)
        return carry

    lax.fori_loop(0, groups, order, 0)
    for tile in range(tiles):
        left[:, tile * LANE : (tile + 1) * LANE] = pairs[tile].astype(jnp.bfloat16)

    def order_modes(group, carry):
        for inner in range(8):
            row = pl.multiple_of(group * 8, 8) + inner
            tile = placed[row, 2 * tiles :].astype(jnp.float32)
            for kind in range(4):
                pairs[kind, pl.ds(row, 1)] = tile[4 + kind : 5 + kind]
        return carry

    lax.fori_loop(0, placed.shape[0] // 8, order_modes, 0)
    for kind in range(4):
        value = pairs[kind, : placed.shape[0]].astype(jnp.bfloat16)
        their_modes[kind] = value.reshape(their_modes.shape[1:])
    for step in range(steps):
        loads[step].wait()
        parts[step] = lax.dot_general(
            left[...], blocks[step], (((1,), (1,)), ((), ())), preferred_element_type=jnp.float32
        )
    chunks.wait()

    def leave(group, carry):
        at = pl.multiple_of(group * 8, 8)
        tall = [
            parts[part, pl.ds(at, 8), lane * LANE : (lane + 1) * LANE]
            for part in range(steps)
            for lane in range(parts.shape[2] // LANE)
        ]
        for inner in range(4):
            rows = jnp.concatenate([tile[2 * inner : 2 * inner + 2] for tile in tall], 0)
            out[group * 4 + inner, :size] = rows.astype(jnp.bfloat16)
        return carry

    lax.fori_loop(0, groups, leave, 0)


def gather_kernel(table, received, partial, out, solved, chosen_rows, *, row_blocks):
    devices = received.shape[0]
    pieces = LANE // row_blocks
    col_blocks = devices // row_blocks
    for block in range(row_blocks):
        value = partial[block * col_blocks, : 2 * pieces].astype(jnp.float32)
        for col in range(1, col_blocks):
            value = value + partial[block * col_blocks + col, : 2 * pieces].astype(jnp.float32)
        for piece in range(pieces):
            for case in range(2):
                at = case * LANE + block * pieces + piece
                solved[at : at + 1] = value[2 * piece + case : 2 * piece + case + 1]
    turned = jnp.concatenate([solved[:LANE].T, solved[LANE:].T], 0).astype(jnp.bfloat16)
    place = lax.broadcasted_iota(jnp.int32, (LANE, LANE), 0).astype(jnp.float32)

    def step(block, carry):
        highs, lows = [], []
        for inner in range(GROUP):
            piece = received[block * GROUP + inner].astype(jnp.float32)
            highs.append(jnp.where(place == piece[2:3], 1.0, 0.0).astype(jnp.bfloat16))
            lows.append(place == piece[3:4])
        chosen = lax.dot_general(
            turned,
            jnp.concatenate(highs, 1),
            (((1,), (0,)), ((), ())),
            preferred_element_type=jnp.float32,
        )
        for inner in range(GROUP):
            lanes = slice(inner * LANE, (inner + 1) * LANE)
            both = [
                jnp.sum(
                    jnp.where(lows[inner], chosen[case * LANE : (case + 1) * LANE, lanes], 0.0),
                    axis=0,
                    keepdims=True,
                )
                for case in range(2)
            ]
            chosen_rows[block * GROUP + inner] = jnp.concatenate(both, 0)
        return carry

    lax.fori_loop(0, devices // GROUP, step, 0)

    size = (partial.shape[1] - 2 * pieces) // 2

    def share(device, carry):
        sources = [jnp.bitwise_xor(device, table[which]) for which in range(2)]
        for which in range(2):
            at = 2 * pieces + which * size
            out[device, which * size : (which + 1) * size] = partial[sources[which], at : at + size]
        rows = [chosen_rows[device], chosen_rows[sources[0]], chosen_rows[sources[1]]]
        rows.append(jnp.zeros_like(rows[0]))
        out[device, 2 * size :] = jnp.concatenate(rows, 0).astype(jnp.bfloat16)
        return carry

    lax.fori_loop(0, devices, share, 0, unroll=4)


def whole():
    return pl.BlockSpec(memory_space=pltpu.VMEM)


def per_sub(*shape, subs=1):
    zeros = (0,) * len(shape)
    return pl.BlockSpec((subs,) + shape, lambda step: (step,) + zeros)


def same(*shape):
    zeros = (0,) * len(shape)
    return pl.BlockSpec(shape, lambda sub: zeros)


def shards(
    residual,
    interface_inverse,
    modes,
    coarse_map,
    coarse_inverse,
    neighbours,
    block_sizes,
    block_offsets,
):
    count, trace_len, cases = residual.shape
    devices = cases // 2
    table = table_of(neighbours, block_sizes, block_offsets)
    field = jax.ShapeDtypeStruct(residual.shape, jnp.bfloat16)

    turned_modes = modes.transpose(0, 2, 1)
    offsets = block_offsets.T
    packed_shape = jax.ShapeDtypeStruct((count, 2, HALF // 8, 4, 8, LANE), jnp.bfloat16)

    tiles = residual.reshape(count, trace_len // 8, 8, 2, LANE).transpose(0, 1, 3, 2, 4)
    hbm = pl.BlockSpec(memory_space=pltpu.HBM)
    packed = call(
        pack_kernel,
        pltpu.HBM(packed_shape.shape, jnp.bfloat16),
        in_specs=[smem(), hbm],
        out_specs=hbm,
        scratch_shapes=[
            pltpu.VMEM((count * 4, HALF // 8, 2, 8, LANE), jnp.bfloat16),
            pltpu.SemaphoreType.DMA((count * 4,)),
            pltpu.SemaphoreType.DMA((count * 4,)),
        ],
    )(offsets, in_hbm(tiles))
    digits = jnp.stack([coarse_map // LANE, coarse_map % LANE]).astype(jnp.bfloat16)
    digits = jnp.concatenate([jnp.zeros_like(digits), digits], 0)
    shared = turned_modes[:, :, : 4 * HALF].reshape(count, MODES, 2, 2, HALF)
    second = table[4:12].reshape(count, 1, 2, 1) == 1
    shared = jnp.stack(
        [jnp.where(second, shared[:, :, :, 1], shared[:, :, :, 0]), shared[:, :, :, 1]], 3
    ).reshape(devices, 4, HALF)
    base = jnp.concatenate([jnp.broadcast_to(digits[None], (devices,) + digits.shape), shared], 1)
    arrived, base = exchange(packed, table, base)
    weighted, payload = call(
        weigh_kernel,
        (pltpu.HBM(residual.shape, jnp.bfloat16), jax.ShapeDtypeStruct(base.shape, jnp.bfloat16)),
        grid=(count // SUBS,),
        in_specs=[
            smem(),
            per_sub(trace_len, cases, subs=SUBS),
            per_sub(MODES, trace_len, subs=SUBS),
            same(*arrived.shape),
            same(*base.shape),
        ],
        out_specs=(per_sub(trace_len, cases, subs=SUBS), same(*base.shape)),
        scratch_shapes=[
            pltpu.VMEM((count * MODES, cases), jnp.float32),
            pltpu.VMEM((cases + 8, LANE), jnp.float32),
        ],
    )(table, residual, turned_modes, arrived, base)
    received = spread(payload)
    weighted, received = lax.optimization_barrier((weighted, received))

    local_part, packed = call(
        local_kernel,
        (
            pltpu.HBM(residual.shape, jnp.float32),
            pltpu.HBM(packed_shape.shape, jnp.bfloat16),
        ),
        grid=(count,),
        in_specs=[smem(), per_sub(trace_len, trace_len), per_sub(trace_len, cases)],
        out_specs=(per_sub(trace_len, cases), per_sub(*packed_shape.shape[1:])),
    )(offsets, in_hbm(interface_inverse), in_hbm(weighted))
    packed = packed.reshape(devices, 32, LANE)

    rows, columns = coarse_inverse.shape
    blocks = LANE * LANE // columns
    placed = call(
        scatter_kernel,
        pltpu.HBM((devices, 2 * columns // LANE + 8, LANE), jnp.bfloat16),
        in_specs=[smem(), whole()],
        out_specs=hbm,
        scratch_shapes=[
            pltpu.VMEM((2 * LANE, LANE), jnp.float32),
            pltpu.VMEM((blocks, 2 * columns // LANE, LANE), jnp.float32),
            pltpu.VMEM((blocks, 2 * columns // LANE, LANE), jnp.bfloat16),
            pltpu.VMEM((devices, 8, LANE), jnp.bfloat16),
            pltpu.SemaphoreType.DMA((devices // blocks,)),
            pltpu.SemaphoreType.DMA(()),
        ],
    )(table, received)
    placed = spread(placed)
    steps = 2
    joined_shape = (devices, 2 * rows // LANE + 32, LANE)
    modes_shape = (4, count, MODES, HALF)
    joined, their_modes = call(
        product_kernel,
        (
            jax.ShapeDtypeStruct(joined_shape, jnp.bfloat16),
            jax.ShapeDtypeStruct(modes_shape, jnp.bfloat16),
        ),
        in_specs=[whole(), hbm, hbm],
        out_specs=(whole(), whole()),
        scratch_shapes=[
            pltpu.VMEM((columns // LANE, cases, LANE), jnp.float32),
            pltpu.VMEM((cases, columns), jnp.bfloat16),
            pltpu.VMEM((steps, cases, rows // steps), jnp.float32),
            pltpu.VMEM((steps, rows // steps, columns), jnp.bfloat16),
            pltpu.SemaphoreType.DMA((steps,)),
            pltpu.SemaphoreType.DMA(()),
        ],
    )(placed, in_hbm(coarse_inverse), in_hbm(packed))
    joined = spread(joined)
    last = call(
        functools.partial(gather_kernel, row_blocks=lax.axis_size("row")),
        jax.ShapeDtypeStruct((devices, 40, LANE), jnp.bfloat16),
        in_specs=[smem(), whole(), whole()],
        out_specs=whole(),
        scratch_shapes=[
            pltpu.VMEM((2 * LANE, LANE), jnp.float32),
            pltpu.VMEM((devices, 2, LANE), jnp.float32),
        ],
    )(table, received, joined)
    last = spread(last).reshape(count, 2, HALF // 8, 5, 8, LANE)
    return call(
        finish_kernel,
        field,
        in_specs=[smem(), hbm, whole(), whole(), whole()],
        out_specs=hbm,
        scratch_shapes=[
            pltpu.VMEM((3, cases, LANE), jnp.float32),
            pltpu.VMEM((3, count, MODES, cases), jnp.bfloat16),
            pltpu.VMEM(residual.shape, jnp.float32),
            pltpu.VMEM(residual.shape, jnp.bfloat16),
            pltpu.SemaphoreType.DMA((count,)),
            pltpu.SemaphoreType.DMA((count,)),
        ],
    )(table, in_hbm(local_part), turned_modes, last, their_modes)


def solution(mesh):
    return jax.shard_map(
        shards,
        mesh=mesh,
        in_specs=(
            P(AXES, None, None),
            P(AXES, None, None),
            P(AXES, None, None),
            P(AXES),
            P("row", "col"),
            P(AXES, None),
            P(AXES, None),
            P(AXES, None),
        ),
        out_specs=P(AXES, None, None),
        check_vma=False,
    )
```

```python
import functools

import jax
import jax.numpy as jnp
from jax import lax
from jax.experimental import pallas as pl
from jax.experimental.pallas import tpu as pltpu
from jax.sharding import PartitionSpec as P

AXES = ("row", "col")
MODES = 32
HALF = 128
LANE = 128
GROUP = 128
SUBS = 2
VMEM_LIMIT = 16 * 1024 * 1024


def spread(value):
    return lax.all_to_all(value, AXES, 0, 0, tiled=True)


def call(kernel, out_shape, **kw):
    return pl.pallas_call(
        kernel,
        out_shape=out_shape,
        compiler_params=pltpu.CompilerParams(vmem_limit_bytes=VMEM_LIMIT),
        **kw,
    )


def in_hbm(value):
    return pltpu.with_memory_space_constraint(value, pltpu.HBM)


def smem():
    return pl.BlockSpec(memory_space=pltpu.SMEM)


def table_of(neighbours, block_sizes, block_offsets):
    count = neighbours.shape[0]
    own = lax.axis_index(AXES).astype(jnp.int32)
    device_mask = jnp.bitwise_xor(neighbours[0] // count, own)
    inner_mask = neighbours[0] % count
    second = (block_offsets // HALF) % 2
    both = block_sizes // HALF - 1
    return jnp.concatenate([device_mask, inner_mask, second.reshape(-1), both.reshape(-1)]).astype(
        jnp.int32
    )


def flags(table, sub, which):
    return table[4 + sub * 2 + which], table[12 + sub * 2 + which]


def store_blocks(offsets, sub, load, packed):
    for which in range(2):
        second = jnp.bitwise_and(jnp.right_shift(offsets[which, sub], 7), 1)
        for half in range(2):
            start = which * 2 * HALF + (second * HALF if half == 0 else HALF)
            rows = load(pl.multiple_of(start, HALF)).astype(jnp.float32)
            for lane in range(2):
                tile = rows[:, lane * LANE : (lane + 1) * LANE].reshape(HALF // 8, 8, LANE)
                packed[0, half, :, which * 2 + lane] = tile.astype(jnp.bfloat16)


def pack_kernel(offsets, tiles, packed, staged, read, written):
    size = HALF // 8
    reads, writes = [], []
    for sub in range(tiles.shape[0]):
        for which in range(2):
            second = jnp.bitwise_and(jnp.right_shift(offsets[which, sub], 7), 1)
            for half in range(2):
                start = which * 2 * size + (second * size if half == 0 else size)
                at = (sub * 2 + which) * 2 + half
                reads.append(
                    pltpu.make_async_copy(
                        tiles.at[sub, pl.ds(start, size)], staged.at[at], read.at[at]
                    )
                )
                reads[-1].start()
                writes.append(
                    pltpu.make_async_copy(
                        staged.at[at],
                        packed.at[sub, half, :, pl.ds(which * 2, 2)],
                        written.at[at],
                    )
                )
    for first, second in zip(reads, writes):
        first.wait()
        second.start()
    for copy in writes:
        copy.wait()


def local_kernel(offsets, inverse, weighted, local, packed):
    local[0] = jnp.dot(inverse[0], weighted[0], preferred_element_type=jnp.float32)
    store_blocks(offsets, pl.program_id(0), lambda start: local[0, pl.ds(start, HALF)], packed)


def reroute_kernel(table, chunks, out):
    size = chunks.shape[1] // 2

    def step(device, carry):
        for which in range(2):
            rows = slice(which * size, (which + 1) * size)
            out[device, rows] = chunks[jnp.bitwise_xor(device, table[which]), rows]
        return carry

    lax.fori_loop(0, chunks.shape[0], step, 0, unroll=8)


def exchange(packed, table, early):
    chunks = spread(packed.reshape(-1, 32, LANE))
    chunks, early = lax.optimization_barrier((chunks, early))
    chunks = call(
        reroute_kernel,
        jax.ShapeDtypeStruct(chunks.shape, chunks.dtype),
        in_specs=[smem(), whole()],
        out_specs=whole(),
    )(table, chunks)
    return spread(chunks).reshape(packed.shape), early


def arrived_rows(table, sub, which, half, arrived):
    second, both = flags(table, sub, which)
    inside = jnp.maximum(both, (second == half).astype(jnp.int32)).astype(jnp.float32)
    other = jnp.bitwise_xor(sub, table[2 + which])
    tiles = [
        arrived[other, half * both, :, which * 2 + lane].astype(jnp.float32).reshape(HALF, LANE)
        for lane in range(2)
    ]
    return jnp.concatenate(tiles, 1), inside


def weigh_kernel(table, residual, modes, arrived, base, weighted, payload, restricted, turned):
    step_at = pl.program_id(0)
    subs = residual.shape[0]
    for at in range(subs):
        sub = step_at * subs + at
        for which in range(2):
            for half in range(2):
                start = (which * 2 + half) * HALF
                rows, inside = arrived_rows(table, sub, which, half, arrived)
                own = residual[at, start : start + HALF].astype(jnp.float32)
                value = (own + rows * inside) * (1.0 - 0.5 * inside)
                weighted[at, start : start + HALF] = value.astype(jnp.bfloat16)
        weighted[at, 4 * HALF :] = residual[at, 4 * HALF :]
        restricted[pl.ds(pl.multiple_of(sub * MODES, MODES), MODES)] = lax.dot_general(
            modes[at], weighted[at], (((1,), (0,)), ((), ())), preferred_element_type=jnp.float32
        )

    @pl.when(step_at == pl.num_programs(0) - 1)
    def _():
        devices, rows, _ = payload.shape
        turned[: 2 * devices] = restricted[...].T
        turned[2 * devices :] = jnp.zeros((turned.shape[0] - 2 * devices, LANE), jnp.float32)
        own = lax.broadcasted_iota(jnp.int32, (rows, LANE), 0) < 2

        def step(device, carry):
            piece = turned[pl.ds(2 * device, rows)]
            rest = base[device].astype(jnp.float32)
            payload[device] = jnp.where(own, piece, rest).astype(jnp.bfloat16)
            return carry

        lax.fori_loop(0, devices, step, 0, unroll=8)


def prolong(modes, picked):
    return lax.dot_general(
        modes, picked, (((0,), (0,)), ((), ())), preferred_element_type=jnp.float32
    )


def finish_kernel(
    table, local, modes, arrived, their_modes, out, pairs, picked, taken, given, read, sent
):
    subs = local.shape[0]
    loads, leaves = (
        [pltpu.make_async_copy(source.at[sub], target.at[sub], done.at[sub]) for sub in range(subs)]
        for source, target, done in ((local, taken, read), (given, out, sent))
    )
    for load in loads:
        load.start()

    for first in range(4):
        for half in range(2):

            def step(piece, carry, first=first, half=half):
                for inner in range(4):
                    tile = arrived[first, half, piece * 4 + inner, 4].astype(jnp.float32)
                    at = (first * 2 + half) * 32 + pl.multiple_of(piece * 8, 8) + inner * 2
                    for kind in range(3):
                        pairs[kind, pl.ds(at, 2)] = tile[kind * 2 : kind * 2 + 2]
                return carry

            lax.fori_loop(0, 4, step, 0)
    for kind in range(3):
        picked[kind] = pairs[kind].T.reshape(picked.shape[1:]).astype(jnp.bfloat16)

    for sub in range(subs):
        loads[sub].wait()
        added = prolong(modes[sub], picked[0, sub])
        for which in range(2):
            other = jnp.bitwise_xor(sub, table[2 + which])
            for half in range(2):
                start = (which * 2 + half) * HALF
                rows, inside = arrived_rows(table, sub, which, half, arrived)
                _, both = flags(table, sub, which)
                theirs = prolong(their_modes[which * 2 + half * both, other], picked[1 + which, other])
                theirs = (0.5 * (rows + theirs)).astype(jnp.bfloat16).astype(jnp.float32)
                own = taken[sub, start : start + HALF] + added[start : start + HALF]
                own = (own * (1.0 - 0.5 * inside)).astype(jnp.bfloat16).astype(jnp.float32)
                given[sub, start : start + HALF] = (own + theirs * inside).astype(jnp.bfloat16)
        given[sub, 4 * HALF :] = (taken[sub, 4 * HALF :] + added[4 * HALF :]).astype(jnp.bfloat16)
        leaves[sub].start()
    for leave in leaves:
        leave.wait()


def scatter_kernel(table, received, out, total, staged, ready, shared, sent, shared_sent):
    devices = received.shape[0]
    place = lax.broadcasted_iota(jnp.int32, (LANE, LANE), 0).astype(jnp.float32)
    first = lax.broadcasted_iota(jnp.int32, (8, LANE), 0) < 6

    def forward(device, carry):
        pieces = [
            received[jnp.bitwise_xor(device, table[which])].astype(jnp.float32) for which in range(2)
        ]
        shared[device, 0] = jnp.where(first, pieces[0], pieces[1])[4:].astype(jnp.bfloat16)
        return carry

    lax.fori_loop(0, devices, forward, 0, unroll=4)
    shares = pltpu.make_async_copy(shared, out.at[:, pl.ds(staged.shape[1], 1)], shared_sent)
    shares.start()
    total[...] = jnp.zeros_like(total)

    def step(block, carry):
        left, right = [], []
        for inner in range(GROUP):
            piece = received[block * GROUP + inner].astype(jnp.float32)
            high = place == piece[2:3]
            low = place == piece[3:4]
            left.append(
                jnp.concatenate(
                    [jnp.where(high, piece[0:1], 0.0), jnp.where(high, piece[1:2], 0.0)], 0
                ).astype(jnp.bfloat16)
            )
            right.append(jnp.where(low, 1.0, 0.0).astype(jnp.bfloat16))
        total[...] += lax.dot_general(
            jnp.concatenate(left, 1),
            jnp.concatenate(right, 1),
            (((1,), (1,)), ((), ())),
            preferred_element_type=jnp.float32,
        )
        return carry

    lax.fori_loop(0, devices // GROUP, step, 0)
    blocks, size, rows, _ = staged.shape
    pieces = size * rows // 2
    for block in range(blocks):
        for case in range(2):
            for piece in range(pieces):
                at = case * LANE + block * pieces + piece
                tile, row = divmod(piece * 2 + case, rows)
                staged[block, tile, row : row + 1] = total[at : at + 1]
    ready[...] = staged[...].astype(jnp.bfloat16)
    copies = [
        pltpu.make_async_copy(
            ready, out.at[pl.ds(row * blocks, blocks), pl.ds(0, size)], sent.at[row]
        )
        for row in range(devices // blocks)
    ]
    for copy in copies:
        copy.start()
    for copy in copies:
        copy.wait()
    shares.wait()


def product_kernel(
    placed, inverse, packed, out, their_modes, pairs, left, parts, blocks, read, sent
):
    groups = placed.shape[0] // 4
    tiles, steps = pairs.shape[0], parts.shape[0]
    size = out.shape[1] - packed.shape[1]
    taken = inverse.shape[0] // steps
    loads = [
        pltpu.make_async_copy(inverse.at[pl.ds(step * taken, taken)], blocks.at[step], read.at[step])
        for step in range(steps)
    ]
    for load in loads:
        load.start()
    chunks = pltpu.make_async_copy(packed, out.at[:, pl.ds(size, packed.shape[1])], sent)
    chunks.start()

    def order(group, carry):
        rows = [placed[group * 4 + inner, : tiles // 2].astype(jnp.float32) for inner in range(4)]
        at = pl.multiple_of(group * 8, 8)
        for tile in range(tiles):
            first = tile % 2 * 2
            piece = [row[tile // 2, first : first + 2] for row in rows]
            pairs[tile, pl.ds(at, 8)] = jnp.concatenate(piece, 0)
        return carry

    lax.fori_loop(0, groups, order, 0)
    for tile in range(tiles):
        left[:, tile * LANE : (tile + 1) * LANE] = pairs[tile].astype(jnp.bfloat16)

    def order_modes(group, carry):
        for inner in range(8):
            row = pl.multiple_of(group * 8, 8) + inner
            tile = placed[row, tiles // 2].astype(jnp.float32)
            for kind in range(4):
                pairs[kind, pl.ds(row, 1)] = tile[kind : kind + 1]
        return carry

    lax.fori_loop(0, placed.shape[0] // 8, order_modes, 0)
    for kind in range(4):
        value = pairs[kind, : placed.shape[0]].astype(jnp.bfloat16)
        their_modes[kind] = value.reshape(their_modes.shape[1:])
    for step in range(steps):
        loads[step].wait()
        parts[step] = lax.dot_general(
            left[...], blocks[step], (((1,), (1,)), ((), ())), preferred_element_type=jnp.float32
        )
    chunks.wait()

    def leave(group, carry):
        at = pl.multiple_of(group * 8, 8)
        tall = [
            parts[part, pl.ds(at, 8), lane * LANE : (lane + 1) * LANE]
            for part in range(steps)
            for lane in range(parts.shape[2] // LANE)
        ]
        for inner in range(4):
            rows = jnp.concatenate([tile[2 * inner : 2 * inner + 2] for tile in tall], 0)
            out[group * 4 + inner, :size] = rows.astype(jnp.bfloat16)
        return carry

    lax.fori_loop(0, groups, leave, 0)


def gather_kernel(table, received, partial, out, solved, chosen_rows, *, row_blocks):
    devices = received.shape[0]
    pieces = LANE // row_blocks
    col_blocks = devices // row_blocks
    for block in range(row_blocks):
        value = partial[block * col_blocks, : 2 * pieces].astype(jnp.float32)
        for col in range(1, col_blocks):
            value = value + partial[block * col_blocks + col, : 2 * pieces].astype(jnp.float32)
        for piece in range(pieces):
            for case in range(2):
                at = case * LANE + block * pieces + piece
                solved[at : at + 1] = value[2 * piece + case : 2 * piece + case + 1]
    turned = jnp.concatenate([solved[:LANE].T, solved[LANE:].T], 0).astype(jnp.bfloat16)
    place = lax.broadcasted_iota(jnp.int32, (LANE, LANE), 0).astype(jnp.float32)

    def step(block, carry):
        highs, lows = [], []
        for inner in range(GROUP):
            piece = received[block * GROUP + inner].astype(jnp.float32)
            highs.append(jnp.where(place == piece[2:3], 1.0, 0.0).astype(jnp.bfloat16))
            lows.append(place == piece[3:4])
        chosen = lax.dot_general(
            turned,
            jnp.concatenate(highs, 1),
            (((1,), (0,)), ((), ())),
            preferred_element_type=jnp.float32,
        )
        for inner in range(GROUP):
            lanes = slice(inner * LANE, (inner + 1) * LANE)
            both = [
                jnp.sum(
                    jnp.where(lows[inner], chosen[case * LANE : (case + 1) * LANE, lanes], 0.0),
                    axis=0,
                    keepdims=True,
                )
                for case in range(2)
            ]
            chosen_rows[block * GROUP + inner] = jnp.concatenate(both, 0)
        return carry

    lax.fori_loop(0, devices // GROUP, step, 0)

    size = (partial.shape[1] - 2 * pieces) // 2

    def share(device, carry):
        sources = [jnp.bitwise_xor(device, table[which]) for which in range(2)]
        for which in range(2):
            at = 2 * pieces + which * size
            out[device, which * size : (which + 1) * size] = partial[sources[which], at : at + size]
        rows = [chosen_rows[device], chosen_rows[sources[0]], chosen_rows[sources[1]]]
        rows.append(jnp.zeros_like(rows[0]))
        out[device, 2 * size :] = jnp.concatenate(rows, 0).astype(jnp.bfloat16)
        return carry

    lax.fori_loop(0, devices, share, 0, unroll=4)


def whole():
    return pl.BlockSpec(memory_space=pltpu.VMEM)


def per_sub(*shape, subs=1):
    zeros = (0,) * len(shape)
    return pl.BlockSpec((subs,) + shape, lambda step: (step,) + zeros)


def same(*shape):
    zeros = (0,) * len(shape)
    return pl.BlockSpec(shape, lambda sub: zeros)


def shards(
    residual,
    interface_inverse,
    modes,
    coarse_map,
    coarse_inverse,
    neighbours,
    block_sizes,
    block_offsets,
):
    count, trace_len, cases = residual.shape
    devices = cases // 2
    table = table_of(neighbours, block_sizes, block_offsets)
    field = jax.ShapeDtypeStruct(residual.shape, jnp.bfloat16)

    turned_modes = modes.transpose(0, 2, 1)
    offsets = block_offsets.T
    packed_shape = jax.ShapeDtypeStruct((count, 2, HALF // 8, 4, 8, LANE), jnp.bfloat16)

    tiles = residual.reshape(count, trace_len // 8, 8, 2, LANE).transpose(0, 1, 3, 2, 4)
    hbm = pl.BlockSpec(memory_space=pltpu.HBM)
    packed = call(
        pack_kernel,
        pltpu.HBM(packed_shape.shape, jnp.bfloat16),
        in_specs=[smem(), hbm],
        out_specs=hbm,
        scratch_shapes=[
            pltpu.VMEM((count * 4, HALF // 8, 2, 8, LANE), jnp.bfloat16),
            pltpu.SemaphoreType.DMA((count * 4,)),
            pltpu.SemaphoreType.DMA((count * 4,)),
        ],
    )(offsets, in_hbm(tiles))
    digits = jnp.stack([coarse_map // LANE, coarse_map % LANE]).astype(jnp.bfloat16)
    digits = jnp.concatenate([jnp.zeros_like(digits), digits], 0)
    shared = turned_modes[:, :, : 4 * HALF].reshape(count, MODES, 2, 2, HALF)
    second = table[4:12].reshape(count, 1, 2, 1) == 1
    shared = jnp.stack(
        [jnp.where(second, shared[:, :, :, 1], shared[:, :, :, 0]), shared[:, :, :, 1]], 3
    ).reshape(devices, 4, HALF)
    base = jnp.concatenate([jnp.broadcast_to(digits[None], (devices,) + digits.shape), shared], 1)
    arrived, base = exchange(packed, table, base)
    weighted, payload = call(
        weigh_kernel,
        (pltpu.HBM(residual.shape, jnp.bfloat16), jax.ShapeDtypeStruct(base.shape, jnp.bfloat16)),
        grid=(count // SUBS,),
        in_specs=[
            smem(),
            per_sub(trace_len, cases, subs=SUBS),
            per_sub(MODES, trace_len, subs=SUBS),
            same(*arrived.shape),
            same(*base.shape),
        ],
        out_specs=(per_sub(trace_len, cases, subs=SUBS), same(*base.shape)),
        scratch_shapes=[
            pltpu.VMEM((count * MODES, cases), jnp.float32),
            pltpu.VMEM((cases + 8, LANE), jnp.float32),
        ],
    )(table, residual, turned_modes, arrived, base)
    received = spread(payload)
    weighted, received = lax.optimization_barrier((weighted, received))

    local_part, packed = call(
        local_kernel,
        (
            pltpu.HBM(residual.shape, jnp.float32),
            pltpu.HBM(packed_shape.shape, jnp.bfloat16),
        ),
        grid=(count,),
        in_specs=[smem(), per_sub(trace_len, trace_len), per_sub(trace_len, cases)],
        out_specs=(per_sub(trace_len, cases), per_sub(*packed_shape.shape[1:])),
    )(offsets, in_hbm(interface_inverse), in_hbm(weighted))
    packed = packed.reshape(devices, 32, LANE)

    rows, columns = coarse_inverse.shape
    blocks = LANE * LANE // columns
    tiles = columns // LANE // 2
    placed = call(
        scatter_kernel,
        pltpu.HBM((devices, tiles + 1, 4, LANE), jnp.bfloat16),
        in_specs=[smem(), whole()],
        out_specs=hbm,
        scratch_shapes=[
            pltpu.VMEM((2 * LANE, LANE), jnp.float32),
            pltpu.VMEM((blocks, tiles, 4, LANE), jnp.float32),
            pltpu.VMEM((blocks, tiles, 4, LANE), jnp.bfloat16),
            pltpu.VMEM((devices, 1, 4, LANE), jnp.bfloat16),
            pltpu.SemaphoreType.DMA((devices // blocks,)),
            pltpu.SemaphoreType.DMA(()),
        ],
    )(table, received)
    placed = spread(placed)
    steps = 2
    joined_shape = (devices, 2 * rows // LANE + 32, LANE)
    modes_shape = (4, count, MODES, HALF)
    joined, their_modes = call(
        product_kernel,
        (
            jax.ShapeDtypeStruct(joined_shape, jnp.bfloat16),
            jax.ShapeDtypeStruct(modes_shape, jnp.bfloat16),
        ),
        in_specs=[whole(), hbm, hbm],
        out_specs=(whole(), whole()),
        scratch_shapes=[
            pltpu.VMEM((columns // LANE, cases, LANE), jnp.float32),
            pltpu.VMEM((cases, columns), jnp.bfloat16),
            pltpu.VMEM((steps, cases, rows // steps), jnp.float32),
            pltpu.VMEM((steps, rows // steps, columns), jnp.bfloat16),
            pltpu.SemaphoreType.DMA((steps,)),
            pltpu.SemaphoreType.DMA(()),
        ],
    )(placed, in_hbm(coarse_inverse), in_hbm(packed))
    joined = spread(joined)
    last = call(
        functools.partial(gather_kernel, row_blocks=lax.axis_size("row")),
        jax.ShapeDtypeStruct((devices, 40, LANE), jnp.bfloat16),
        in_specs=[smem(), whole(), whole()],
        out_specs=whole(),
        scratch_shapes=[
            pltpu.VMEM((2 * LANE, LANE), jnp.float32),
            pltpu.VMEM((devices, 2, LANE), jnp.float32),
        ],
    )(table, received, joined)
    last = spread(last).reshape(count, 2, HALF // 8, 5, 8, LANE)
    return call(
        finish_kernel,
        field,
        in_specs=[smem(), hbm, whole(), whole(), whole()],
        out_specs=hbm,
        scratch_shapes=[
            pltpu.VMEM((3, cases, LANE), jnp.float32),
            pltpu.VMEM((3, count, MODES, cases), jnp.bfloat16),
            pltpu.VMEM(residual.shape, jnp.float32),
            pltpu.VMEM(residual.shape, jnp.bfloat16),
            pltpu.SemaphoreType.DMA((count,)),
            pltpu.SemaphoreType.DMA((count,)),
        ],
    )(table, in_hbm(local_part), turned_modes, last, their_modes)


def solution(mesh):
    return jax.shard_map(
        shards,
        mesh=mesh,
        in_specs=(
            P(AXES, None, None),
            P(AXES, None, None),
            P(AXES, None, None),
            P(AXES),
            P("row", "col"),
            P(AXES, None),
            P(AXES, None),
            P(AXES, None),
        ),
        out_specs=P(AXES, None, None),
        check_vma=False,
    )
```

```python
import functools

import jax
import jax.numpy as jnp
from jax import lax
from jax.experimental import pallas as pl
from jax.experimental.pallas import tpu as pltpu
from jax.sharding import PartitionSpec as P

AXES = ("row", "col")
MODES = 32
HALF = 128
LANE = 128
GROUP = 128
SUBS = 2
VMEM_LIMIT = 16 * 1024 * 1024


def spread(value):
    return lax.all_to_all(value, AXES, 0, 0, tiled=True)


def call(kernel, out_shape, **kw):
    return pl.pallas_call(
        kernel,
        out_shape=out_shape,
        compiler_params=pltpu.CompilerParams(vmem_limit_bytes=VMEM_LIMIT),
        **kw,
    )


def in_hbm(value):
    return pltpu.with_memory_space_constraint(value, pltpu.HBM)


def smem():
    return pl.BlockSpec(memory_space=pltpu.SMEM)


def table_of(neighbours, block_sizes, block_offsets):
    count = neighbours.shape[0]
    own = lax.axis_index(AXES).astype(jnp.int32)
    device_mask = jnp.bitwise_xor(neighbours[0] // count, own)
    inner_mask = neighbours[0] % count
    second = (block_offsets // HALF) % 2
    both = block_sizes // HALF - 1
    return jnp.concatenate([device_mask, inner_mask, second.reshape(-1), both.reshape(-1)]).astype(
        jnp.int32
    )


def flags(table, sub, which):
    return table[4 + sub * 2 + which], table[12 + sub * 2 + which]


def store_blocks(offsets, sub, load, packed):
    for which in range(2):
        second = jnp.bitwise_and(jnp.right_shift(offsets[which, sub], 7), 1)
        for half in range(2):
            start = which * 2 * HALF + (second * HALF if half == 0 else HALF)
            rows = load(pl.multiple_of(start, HALF)).astype(jnp.float32)
            for lane in range(2):
                tile = rows[:, lane * LANE : (lane + 1) * LANE].reshape(HALF // 8, 8, LANE)
                packed[0, half, :, which * 2 + lane] = tile.astype(jnp.bfloat16)


def pack_kernel(offsets, tiles, packed, staged, read, written):
    size = HALF // 8
    reads, writes = [], []
    for sub in range(tiles.shape[0]):
        for which in range(2):
            second = jnp.bitwise_and(jnp.right_shift(offsets[which, sub], 7), 1)
            for half in range(2):
                start = which * 2 * size + (second * size if half == 0 else size)
                at = (sub * 2 + which) * 2 + half
                reads.append(
                    pltpu.make_async_copy(
                        tiles.at[sub, pl.ds(start, size)], staged.at[at], read.at[at]
                    )
                )
                reads[-1].start()
                writes.append(
                    pltpu.make_async_copy(
                        staged.at[at],
                        packed.at[sub, half, :, pl.ds(which * 2, 2)],
                        written.at[at],
                    )
                )
    for first, second in zip(reads, writes):
        first.wait()
        second.start()
    for copy in writes:
        copy.wait()


def local_kernel(offsets, inverse, weighted, local, packed):
    local[0] = jnp.dot(inverse[0], weighted[0], preferred_element_type=jnp.float32)
    store_blocks(offsets, pl.program_id(0), lambda start: local[0, pl.ds(start, HALF)], packed)


def reroute_kernel(table, chunks, out):
    size = chunks.shape[1] // 2

    def step(device, carry):
        for which in range(2):
            rows = slice(which * size, (which + 1) * size)
            out[device, rows] = chunks[jnp.bitwise_xor(device, table[which]), rows]
        return carry

    lax.fori_loop(0, chunks.shape[0], step, 0, unroll=8)


def exchange(packed, table, early):
    chunks = spread(packed.reshape(-1, 32, LANE))
    chunks, early = lax.optimization_barrier((chunks, early))
    chunks = call(
        reroute_kernel,
        jax.ShapeDtypeStruct(chunks.shape, chunks.dtype),
        in_specs=[smem(), whole()],
        out_specs=whole(),
    )(table, chunks)
    return spread(chunks).reshape(packed.shape), early


def arrived_rows(table, sub, which, half, arrived):
    second, both = flags(table, sub, which)
    inside = jnp.maximum(both, (second == half).astype(jnp.int32)).astype(jnp.float32)
    other = jnp.bitwise_xor(sub, table[2 + which])
    tiles = [
        arrived[other, half * both, :, which * 2 + lane].astype(jnp.float32).reshape(HALF, LANE)
        for lane in range(2)
    ]
    return jnp.concatenate(tiles, 1), inside


def weigh_kernel(table, residual, modes, arrived, base, weighted, payload, restricted, turned):
    step_at = pl.program_id(0)
    subs = residual.shape[0]
    for at in range(subs):
        sub = step_at * subs + at
        for which in range(2):
            for half in range(2):
                start = (which * 2 + half) * HALF
                rows, inside = arrived_rows(table, sub, which, half, arrived)
                own = residual[at, start : start + HALF].astype(jnp.float32)
                value = (own + rows * inside) * (1.0 - 0.5 * inside)
                weighted[at, start : start + HALF] = value.astype(jnp.bfloat16)
        weighted[at, 4 * HALF :] = residual[at, 4 * HALF :]
        restricted[pl.ds(pl.multiple_of(sub * MODES, MODES), MODES)] = lax.dot_general(
            modes[at], weighted[at], (((1,), (0,)), ((), ())), preferred_element_type=jnp.float32
        )

    @pl.when(step_at == pl.num_programs(0) - 1)
    def _():
        devices, rows, _ = payload.shape
        turned[: 2 * devices] = restricted[...].T
        turned[2 * devices :] = jnp.zeros((turned.shape[0] - 2 * devices, LANE), jnp.float32)
        own = lax.broadcasted_iota(jnp.int32, (rows, LANE), 0) < 2

        def step(device, carry):
            piece = turned[pl.ds(2 * device, rows)]
            rest = base[device].astype(jnp.float32)
            payload[device] = jnp.where(own, piece, rest).astype(jnp.bfloat16)
            return carry

        lax.fori_loop(0, devices, step, 0, unroll=8)


def prolong(modes, picked):
    return lax.dot_general(
        modes, picked, (((0,), (0,)), ((), ())), preferred_element_type=jnp.float32
    )


def finish_kernel(
    table, local, modes, arrived, their_modes, out, pairs, picked, taken, given, read, sent
):
    subs = local.shape[0]
    loads, leaves = (
        [pltpu.make_async_copy(source.at[sub], target.at[sub], done.at[sub]) for sub in range(subs)]
        for source, target, done in ((local, taken, read), (given, out, sent))
    )
    for load in loads:
        load.start()

    for first in range(4):
        for half in range(2):

            def step(piece, carry, first=first, half=half):
                tall = [
                    arrived[first, half, piece * 4 + inner, 4].astype(jnp.float32)
                    for inner in range(4)
                ]
                at = pl.multiple_of((first * 2 + half) * 32 + piece * 8, 8)
                for kind in range(3):
                    taken_rows = [tile[kind * 2 : kind * 2 + 2] for tile in tall]
                    pairs[kind, pl.ds(at, 8)] = jnp.concatenate(taken_rows, 0)
                return carry

            lax.fori_loop(0, 4, step, 0)
    for kind in range(3):
        picked[kind] = pairs[kind].T.reshape(picked.shape[1:]).astype(jnp.bfloat16)

    for sub in range(subs):
        loads[sub].wait()
        added = prolong(modes[sub], picked[0, sub])
        for which in range(2):
            other = jnp.bitwise_xor(sub, table[2 + which])
            for half in range(2):
                start = (which * 2 + half) * HALF
                rows, inside = arrived_rows(table, sub, which, half, arrived)
                _, both = flags(table, sub, which)
                theirs = prolong(their_modes[which * 2 + half * both, other], picked[1 + which, other])
                theirs = (0.5 * (rows + theirs)).astype(jnp.bfloat16).astype(jnp.float32)
                own = taken[sub, start : start + HALF] + added[start : start + HALF]
                own = (own * (1.0 - 0.5 * inside)).astype(jnp.bfloat16).astype(jnp.float32)
                given[sub, start : start + HALF] = (own + theirs * inside).astype(jnp.bfloat16)
        given[sub, 4 * HALF :] = (taken[sub, 4 * HALF :] + added[4 * HALF :]).astype(jnp.bfloat16)
        leaves[sub].start()
    for leave in leaves:
        leave.wait()


def scatter_kernel(table, received, out, total, staged, ready, shared, sent, shared_sent):
    devices = received.shape[0]
    place = lax.broadcasted_iota(jnp.int32, (LANE, LANE), 0).astype(jnp.float32)
    first = lax.broadcasted_iota(jnp.int32, (8, LANE), 0) < 6

    def forward(device, carry):
        pieces = [
            received[jnp.bitwise_xor(device, table[which])].astype(jnp.float32) for which in range(2)
        ]
        shared[device, 0] = jnp.where(first, pieces[0], pieces[1])[4:].astype(jnp.bfloat16)
        return carry

    lax.fori_loop(0, devices, forward, 0, unroll=4)
    shares = pltpu.make_async_copy(shared, out.at[:, pl.ds(staged.shape[1], 1)], shared_sent)
    shares.start()
    total[...] = jnp.zeros_like(total)

    def step(block, carry):
        left, right = [], []
        for inner in range(GROUP):
            piece = received[block * GROUP + inner].astype(jnp.float32)
            high = place == piece[2:3]
            low = place == piece[3:4]
            left.append(
                jnp.concatenate(
                    [jnp.where(high, piece[0:1], 0.0), jnp.where(high, piece[1:2], 0.0)], 0
                ).astype(jnp.bfloat16)
            )
            right.append(jnp.where(low, 1.0, 0.0).astype(jnp.bfloat16))
        total[...] += lax.dot_general(
            jnp.concatenate(left, 1),
            jnp.concatenate(right, 1),
            (((1,), (1,)), ((), ())),
            preferred_element_type=jnp.float32,
        )
        return carry

    lax.fori_loop(0, devices // GROUP, step, 0)
    blocks, size, rows, _ = staged.shape
    pieces = size * rows // 2
    for block in range(blocks):
        for case in range(2):
            for piece in range(pieces):
                at = case * LANE + block * pieces + piece
                tile, row = divmod(piece * 2 + case, rows)
                staged[block, tile, row : row + 1] = total[at : at + 1]
    ready[...] = staged[...].astype(jnp.bfloat16)
    copies = [
        pltpu.make_async_copy(
            ready, out.at[pl.ds(row * blocks, blocks), pl.ds(0, size)], sent.at[row]
        )
        for row in range(devices // blocks)
    ]
    for copy in copies:
        copy.start()
    for copy in copies:
        copy.wait()
    shares.wait()


def product_kernel(
    placed, inverse, packed, out, their_modes, pairs, left, parts, blocks, read, sent
):
    groups = placed.shape[0] // 4
    tiles, steps = pairs.shape[0], parts.shape[0]
    size = out.shape[1] - packed.shape[1]
    taken = inverse.shape[0] // steps
    loads = [
        pltpu.make_async_copy(inverse.at[pl.ds(step * taken, taken)], blocks.at[step], read.at[step])
        for step in range(steps)
    ]
    for load in loads:
        load.start()
    chunks = pltpu.make_async_copy(packed, out.at[:, pl.ds(size, packed.shape[1])], sent)
    chunks.start()

    def order(group, carry):
        rows = [placed[group * 4 + inner, : tiles // 2].astype(jnp.float32) for inner in range(4)]
        at = pl.multiple_of(group * 8, 8)
        for tile in range(tiles):
            first = tile % 2 * 2
            piece = [row[tile // 2, first : first + 2] for row in rows]
            pairs[tile, pl.ds(at, 8)] = jnp.concatenate(piece, 0)
        return carry

    lax.fori_loop(0, groups, order, 0)
    for tile in range(tiles):
        left[:, tile * LANE : (tile + 1) * LANE] = pairs[tile].astype(jnp.bfloat16)

    def order_modes(group, carry):
        for inner in range(8):
            row = pl.multiple_of(group * 8, 8) + inner
            tile = placed[row, tiles // 2].astype(jnp.float32)
            for kind in range(4):
                pairs[kind, pl.ds(row, 1)] = tile[kind : kind + 1]
        return carry

    lax.fori_loop(0, placed.shape[0] // 8, order_modes, 0)
    for kind in range(4):
        value = pairs[kind, : placed.shape[0]].astype(jnp.bfloat16)
        their_modes[kind] = value.reshape(their_modes.shape[1:])
    for step in range(steps):
        loads[step].wait()
        parts[step] = lax.dot_general(
            left[...], blocks[step], (((1,), (1,)), ((), ())), preferred_element_type=jnp.float32
        )
    chunks.wait()

    def leave(group, carry):
        at = pl.multiple_of(group * 8, 8)
        tall = [
            parts[part, pl.ds(at, 8), lane * LANE : (lane + 1) * LANE]
            for part in range(steps)
            for lane in range(parts.shape[2] // LANE)
        ]
        for inner in range(4):
            rows = jnp.concatenate([tile[2 * inner : 2 * inner + 2] for tile in tall], 0)
            out[group * 4 + inner, :size] = rows.astype(jnp.bfloat16)
        return carry

    lax.fori_loop(0, groups, leave, 0)


def gather_kernel(table, received, partial, out, solved, chosen_rows, *, row_blocks):
    devices = received.shape[0]
    pieces = LANE // row_blocks
    col_blocks = devices // row_blocks
    for block in range(row_blocks):
        value = partial[block * col_blocks, : 2 * pieces].astype(jnp.float32)
        for col in range(1, col_blocks):
            value = value + partial[block * col_blocks + col, : 2 * pieces].astype(jnp.float32)
        for piece in range(pieces):
            for case in range(2):
                at = case * LANE + block * pieces + piece
                solved[at : at + 1] = value[2 * piece + case : 2 * piece + case + 1]
    turned = jnp.concatenate([solved[:LANE].T, solved[LANE:].T], 0).astype(jnp.bfloat16)
    place = lax.broadcasted_iota(jnp.int32, (LANE, LANE), 0).astype(jnp.float32)

    def step(block, carry):
        highs, lows = [], []
        for inner in range(GROUP):
            piece = received[block * GROUP + inner].astype(jnp.float32)
            highs.append(jnp.where(place == piece[2:3], 1.0, 0.0).astype(jnp.bfloat16))
            lows.append(place == piece[3:4])
        chosen = lax.dot_general(
            turned,
            jnp.concatenate(highs, 1),
            (((1,), (0,)), ((), ())),
            preferred_element_type=jnp.float32,
        )
        for inner in range(GROUP):
            lanes = slice(inner * LANE, (inner + 1) * LANE)
            both = [
                jnp.sum(
                    jnp.where(lows[inner], chosen[case * LANE : (case + 1) * LANE, lanes], 0.0),
                    axis=0,
                    keepdims=True,
                )
                for case in range(2)
            ]
            chosen_rows[block * GROUP + inner] = jnp.concatenate(both, 0)
        return carry

    lax.fori_loop(0, devices // GROUP, step, 0)

    size = (partial.shape[1] - 2 * pieces) // 2

    def share(device, carry):
        sources = [jnp.bitwise_xor(device, table[which]) for which in range(2)]
        for which in range(2):
            at = 2 * pieces + which * size
            out[device, which * size : (which + 1) * size] = partial[sources[which], at : at + size]
        rows = [chosen_rows[device], chosen_rows[sources[0]], chosen_rows[sources[1]]]
        rows.append(jnp.zeros_like(rows[0]))
        out[device, 2 * size :] = jnp.concatenate(rows, 0).astype(jnp.bfloat16)
        return carry

    lax.fori_loop(0, devices, share, 0, unroll=4)


def whole():
    return pl.BlockSpec(memory_space=pltpu.VMEM)


def per_sub(*shape, subs=1):
    zeros = (0,) * len(shape)
    return pl.BlockSpec((subs,) + shape, lambda step: (step,) + zeros)


def same(*shape):
    zeros = (0,) * len(shape)
    return pl.BlockSpec(shape, lambda sub: zeros)


def shards(
    residual,
    interface_inverse,
    modes,
    coarse_map,
    coarse_inverse,
    neighbours,
    block_sizes,
    block_offsets,
):
    count, trace_len, cases = residual.shape
    devices = cases // 2
    table = table_of(neighbours, block_sizes, block_offsets)
    field = jax.ShapeDtypeStruct(residual.shape, jnp.bfloat16)

    turned_modes = modes.transpose(0, 2, 1)
    offsets = block_offsets.T
    packed_shape = jax.ShapeDtypeStruct((count, 2, HALF // 8, 4, 8, LANE), jnp.bfloat16)

    tiles = residual.reshape(count, trace_len // 8, 8, 2, LANE).transpose(0, 1, 3, 2, 4)
    hbm = pl.BlockSpec(memory_space=pltpu.HBM)
    packed = call(
        pack_kernel,
        pltpu.HBM(packed_shape.shape, jnp.bfloat16),
        in_specs=[smem(), hbm],
        out_specs=hbm,
        scratch_shapes=[
            pltpu.VMEM((count * 4, HALF // 8, 2, 8, LANE), jnp.bfloat16),
            pltpu.SemaphoreType.DMA((count * 4,)),
            pltpu.SemaphoreType.DMA((count * 4,)),
        ],
    )(in_hbm(offsets), in_hbm(tiles))
    digits = jnp.stack([coarse_map // LANE, coarse_map % LANE]).astype(jnp.bfloat16)
    digits = jnp.concatenate([jnp.zeros_like(digits), digits], 0)
    shared = turned_modes[:, :, : 4 * HALF].reshape(count, MODES, 2, 2, HALF)
    second = table[4:12].reshape(count, 1, 2, 1) == 1
    shared = jnp.stack(
        [jnp.where(second, shared[:, :, :, 1], shared[:, :, :, 0]), shared[:, :, :, 1]], 3
    ).reshape(devices, 4, HALF)
    base = jnp.concatenate([jnp.broadcast_to(digits[None], (devices,) + digits.shape), shared], 1)
    arrived, base = exchange(packed, table, base)
    weighted, payload = call(
        weigh_kernel,
        (pltpu.HBM(residual.shape, jnp.bfloat16), jax.ShapeDtypeStruct(base.shape, jnp.bfloat16)),
        grid=(count // SUBS,),
        in_specs=[
            smem(),
            per_sub(trace_len, cases, subs=SUBS),
            per_sub(MODES, trace_len, subs=SUBS),
            same(*arrived.shape),
            same(*base.shape),
        ],
        out_specs=(per_sub(trace_len, cases, subs=SUBS), same(*base.shape)),
        scratch_shapes=[
            pltpu.VMEM((count * MODES, cases), jnp.float32),
            pltpu.VMEM((cases + 8, LANE), jnp.float32),
        ],
    )(table, residual, turned_modes, arrived, base)
    received = spread(payload)
    weighted, received = lax.optimization_barrier((weighted, received))

    local_part, packed = call(
        local_kernel,
        (
            pltpu.HBM(residual.shape, jnp.float32),
            pltpu.HBM(packed_shape.shape, jnp.bfloat16),
        ),
        grid=(count,),
        in_specs=[smem(), per_sub(trace_len, trace_len), per_sub(trace_len, cases)],
        out_specs=(per_sub(trace_len, cases), per_sub(*packed_shape.shape[1:])),
    )(offsets, in_hbm(interface_inverse), in_hbm(weighted))
    packed = packed.reshape(devices, 32, LANE)

    rows, columns = coarse_inverse.shape
    blocks = LANE * LANE // columns
    tiles = columns // LANE // 2
    placed = call(
        scatter_kernel,
        pltpu.HBM((devices, tiles + 1, 4, LANE), jnp.bfloat16),
        in_specs=[smem(), whole()],
        out_specs=hbm,
        scratch_shapes=[
            pltpu.VMEM((2 * LANE, LANE), jnp.float32),
            pltpu.VMEM((blocks, tiles, 4, LANE), jnp.float32),
            pltpu.VMEM((blocks, tiles, 4, LANE), jnp.bfloat16),
            pltpu.VMEM((devices, 1, 4, LANE), jnp.bfloat16),
            pltpu.SemaphoreType.DMA((devices // blocks,)),
            pltpu.SemaphoreType.DMA(()),
        ],
    )(table, received)
    placed = spread(placed)
    steps = 2
    joined_shape = (devices, 2 * rows // LANE + 32, LANE)
    modes_shape = (4, count, MODES, HALF)
    joined, their_modes = call(
        product_kernel,
        (
            jax.ShapeDtypeStruct(joined_shape, jnp.bfloat16),
            jax.ShapeDtypeStruct(modes_shape, jnp.bfloat16),
        ),
        in_specs=[whole(), hbm, hbm],
        out_specs=(whole(), whole()),
        scratch_shapes=[
            pltpu.VMEM((columns // LANE, cases, LANE), jnp.float32),
            pltpu.VMEM((cases, columns), jnp.bfloat16),
            pltpu.VMEM((steps, cases, rows // steps), jnp.float32),
            pltpu.VMEM((steps, rows // steps, columns), jnp.bfloat16),
            pltpu.SemaphoreType.DMA((steps,)),
            pltpu.SemaphoreType.DMA(()),
        ],
    )(placed, in_hbm(coarse_inverse), in_hbm(packed))
    joined = spread(joined)
    last = call(
        functools.partial(gather_kernel, row_blocks=lax.axis_size("row")),
        jax.ShapeDtypeStruct((devices, 40, LANE), jnp.bfloat16),
        in_specs=[smem(), whole(), whole()],
        out_specs=whole(),
        scratch_shapes=[
            pltpu.VMEM((2 * LANE, LANE), jnp.float32),
            pltpu.VMEM((devices, 2, LANE), jnp.float32),
        ],
    )(table, received, joined)
    last = spread(last).reshape(count, 2, HALF // 8, 5, 8, LANE)
    return call(
        finish_kernel,
        field,
        in_specs=[smem(), hbm, whole(), whole(), whole()],
        out_specs=hbm,
        scratch_shapes=[
            pltpu.VMEM((3, cases, LANE), jnp.float32),
            pltpu.VMEM((3, count, MODES, cases), jnp.bfloat16),
            pltpu.VMEM(residual.shape, jnp.float32),
            pltpu.VMEM(residual.shape, jnp.bfloat16),
            pltpu.SemaphoreType.DMA((count,)),
            pltpu.SemaphoreType.DMA((count,)),
        ],
    )(table, in_hbm(local_part), turned_modes, last, their_modes)


def solution(mesh):
    return jax.shard_map(
        shards,
        mesh=mesh,
        in_specs=(
            P(AXES, None, None),
            P(AXES, None, None),
            P(AXES, None, None),
            P(AXES),
            P("row", "col"),
            P(AXES, None),
            P(AXES, None),
            P(AXES, None),
        ),
        out_specs=P(AXES, None, None),
        check_vma=False,
    )
```
